32 devices in a mesh: group: 4 (over z), dev: 8 (over y, x, core).
Axes of the slice: x: 2, y: 2, z: 4, core: 2. Of those that a mesh axis runs over, the one named last changes fastest.
Arguments:
- populations: float32 [128, 19, 4096], P(('group', 'dev')), may hold values from -3 to 3
- fluid_flags: int32 [128, 4096], P(('group', 'dev')), may hold values from 0 to 1, as said below
- neighbours: int32 [128, 18], P(('group', 'dev')), may hold values from -1 to 11, as said below
- relax_rate: float32 [128], P(('group', 'dev')), may hold values from 1 to 1.9
Outputs:
- advanced: float32 [128, 19, 4096], P(('group', 'dev'))
The draws below stay inside these ranges and needn't reach their ends.
Inputs may be any that keep to these rules, and one draw needn't show every extreme that they name: `fluid_flags`: on every device the slots that hold a block come first and the later slots have no fluid cell. In every group some device holds a block in all 4 slots. `neighbours`: an entry is -1 or (dz + 1) * 4 + t, where dz is the third component of the direction; it names slot t of the device dz places further along dev in the same group, a slot that holds a block, and that block's entry in the opposite direction names back. Slots that hold no block have -1 in every direction.
All inputs are finite; a program needn't handle non-finite values.
Results may differ from the reference program's by a relative error of at most 0.0003.
Values sent between devices are 32-bit elements; how exact they have to be, the bound alone decides.
No kernel may reach another device: no remote copies, remote signals or barrier semaphores. Data moves between devices by JAX's collectives and lax.ppermute only.
A program may use at most 128 MiB of HBM per device.

```python
import jax
import jax.numpy as jnp
import numpy as np
from jax import lax

BLOCK = 16
PX = 4
PY = 1
STEPS = 2
SLOTS = 4
CELLS = 4096
NBLOCKS = 128
N_GROUP = 4
N_DEV = 8


def directions():
    listed = []
    for axis_num in range(3):
        for side_sign in (1, -1):
            vector = [0, 0, 0]
            vector[axis_num] = side_sign
            listed.append(vector)
    for axis_one, axis_two in ((0, 1), (0, 2), (1, 2)):
        for sign_one in (1, -1):
            for sign_two in (1, -1):
                vector = [0, 0, 0]
                vector[axis_one] = sign_one
                vector[axis_two] = sign_two
                listed.append(vector)
    return np.array(listed, dtype=np.int32)


def geometry(key):
    device_count = N_GROUP * N_DEV
    slot_count = PX * PY
    subkeys = jax.random.split(jax.random.fold_in(key, 11), 5)
    light_load = jax.random.randint(subkeys[0], (device_count,), slot_count // 4, slot_count // 2 + 1)
    heavy_pick = jax.random.randint(subkeys[1], (N_GROUP,), 0, N_DEV)
    extra_heavy = jax.random.randint(subkeys[2], (device_count,), 0, 8) == 0
    device_ids = jnp.arange(device_count)
    heavy_dev = (device_ids % N_DEV == heavy_pick[device_ids // N_DEV]) | extra_heavy
    live_slots = jnp.where(heavy_dev, slot_count, light_load)
    orders = jax.vmap(lambda subkey: jax.random.permutation(subkey, slot_count))(jax.random.split(subkeys[3], device_count))
    holder = jnp.argsort(orders, axis=1)
    return (live_slots, orders, holder, subkeys[4])


def draw_fluid_flags(key, part):
    device_count = N_GROUP * N_DEV
    slot_count = PX * PY
    live_slots, orders, holder, cell_key = geometry(key)
    wet_draw = jax.random.randint(cell_key, (device_count, slot_count, BLOCK ** 3), 0, 20) < 17
    holds = jnp.arange(slot_count)[None, :] < live_slots[:, None]
    return (wet_draw & holds[:, :, None]).astype(jnp.int32).reshape(device_count * slot_count, BLOCK ** 3)


def draw_neighbours(key, part):
    device_count = N_GROUP * N_DEV
    slot_count = PX * PY
    live_slots, orders, holder, cell_key = geometry(key)
    offsets = jnp.asarray(directions())
    pos_x = orders // PY
    pos_y = orders % PY
    to_x = pos_x[:, :, None] + offsets[None, None, :, 0]
    to_y = pos_y[:, :, None] + offsets[None, None, :, 1]
    device_ids = jnp.arange(device_count)
    along_dev = (device_ids % N_DEV)[:, None, None] + offsets[None, None, :, 2]
    inside = (to_x >= 0) & (to_x < PX) & (to_y >= 0) & (to_y < PY) & (along_dev >= 0) & (along_dev < N_DEV)
    to_dev = jnp.clip(device_ids[:, None, None] + offsets[None, None, :, 2], 0, device_count - 1)
    to_pos = jnp.clip(to_x, 0, PX - 1) * PY + jnp.clip(to_y, 0, PY - 1)
    to_slot = holder[to_dev, to_pos]
    own_live = jnp.arange(slot_count)[None, :, None] < live_slots[:, None, None]
    present = inside & (to_slot < live_slots[to_dev]) & own_live
    entries = jnp.where(present, (offsets[None, None, :, 2] + 1) * slot_count + to_slot, -1)
    return entries.reshape(device_count * slot_count, 18).astype(jnp.int32)


def levels(stream_key, shape, cuts, least, top_value):
    loudness = 1.0
    for position, parts in cuts:
        draws = jax.random.uniform(jax.random.fold_in(jax.random.fold_in(stream_key, 6), position), (parts,), jnp.float32, least / len(cuts), top_value / len(cuts))
        loudness = loudness * jnp.repeat(jnp.exp(draws), shape[position] // parts).reshape((-1,) + (1,) * (len(shape) - 1 - position))
    return loudness


def gaussian(key, shape, deviation, bound, cuts=(), kind=jnp.bfloat16):
    values = deviation * jax.random.normal(key, shape, jnp.float32)
    if cuts:
        values = values * levels(key, shape, cuts, -0.22, 0.18)
    return jnp.clip(values, -bound, bound).astype(kind)


def setup_inputs(seed: int = 0) -> dict:
    arg_keys = jax.random.split(jax.random.key(seed), 5)
    populations = gaussian(arg_keys[0], (NBLOCKS, 19, CELLS), 0.5, 3.0, ((0, 32),), jnp.float32)
    fluid_flags = draw_fluid_flags(jax.random.fold_in(arg_keys[4], 71), 0)
    neighbours = draw_neighbours(jax.random.fold_in(arg_keys[4], 71), 0)
    relax_rate = jnp.clip(1.0 + 0.9 * jax.random.uniform(arg_keys[3], (NBLOCKS,), jnp.float32) ** levels(arg_keys[3], (NBLOCKS,), ((0, 32),), -0.2, 0.2), 1.0, 1.9)
    return {"populations": populations, "fluid_flags": fluid_flags, "neighbours": neighbours, "relax_rate": relax_rate}


def invert_matrix(rows_in):
    size_n = len(rows_in)
    work = [list(rows_in[row_num]) + [1.0 if col_num == row_num else 0.0 for col_num in range(size_n)] for row_num in range(size_n)]
    for col_num in range(size_n):
        pivot_row = max(range(col_num, size_n), key=lambda row_num: abs(work[row_num][col_num]))
        work[col_num], work[pivot_row] = work[pivot_row], work[col_num]
        pivot_val = work[col_num][col_num]
        work[col_num] = [entry / pivot_val for entry in work[col_num]]
        for row_num in range(size_n):
            if row_num != col_num:
                factor = work[row_num][col_num]
                if factor != 0.0:
                    work[row_num] = [entry - factor * pivot_entry for entry, pivot_entry in zip(work[row_num], work[col_num])]
    return [row_list[size_n:] for row_list in work]


def lattice():
    velocity = [[0, 0, 0]]
    for axis_num in range(3):
        for side_sign in (1, -1):
            vector = [0, 0, 0]
            vector[axis_num] = side_sign
            velocity.append(vector)
    for axis_one, axis_two in ((0, 1), (0, 2), (1, 2)):
        for sign_one in (1, -1):
            for sign_two in (1, -1):
                vector = [0, 0, 0]
                vector[axis_one] = sign_one
                vector[axis_two] = sign_two
                velocity.append(vector)
    weights = [1.0 / 3.0] + [1.0 / 18.0] * 6 + [1.0 / 36.0] * 12
    opposite = [velocity.index([-entry for entry in velocity[lane_num]]) for lane_num in range(19)]
    comp_x = [float(vector[0]) for vector in velocity]
    comp_y = [float(vector[1]) for vector in velocity]
    comp_z = [float(vector[2]) for vector in velocity]
    makers = [
        lambda a, b, c: 1.0, lambda a, b, c: a, lambda a, b, c: b, lambda a, b, c: c,
        lambda a, b, c: a * b, lambda a, b, c: a * c, lambda a, b, c: b * c,
        lambda a, b, c: a * a - b * b, lambda a, b, c: a * a - c * c, lambda a, b, c: a * a + b * b + c * c,
        lambda a, b, c: a * b * b, lambda a, b, c: a * c * c, lambda a, b, c: b * a * a, lambda a, b, c: b * c * c,
        lambda a, b, c: c * a * a, lambda a, b, c: c * b * b, lambda a, b, c: a * a * b * b,
        lambda a, b, c: a * a * c * c, lambda a, b, c: b * b * c * c]
    moment_rows = [[maker(comp_x[col_num], comp_y[col_num], comp_z[col_num]) for col_num in range(19)] for maker in makers]
    inverse = invert_matrix(moment_rows)
    table_other = []
    table_shear = []
    for row_num in range(19):
        other_row = []
        shear_row = []
        for col_num in range(19):
            other_sum = sum(inverse[row_num][mom_num] * moment_rows[mom_num][col_num] for mom_num in range(9, 19))
            shear_sum = sum(inverse[row_num][mom_num] * moment_rows[mom_num][col_num] for mom_num in range(4, 9))
            ratio = weights[col_num] / weights[row_num]
            other_row.append(other_sum * ratio)
            shear_row.append(shear_sum * ratio)
        table_other.append(other_row)
        table_shear.append(shear_row)
    return np.array(velocity), np.array(weights), opposite, np.array(table_other), np.array(table_shear)


def collide(current, rates):
    velocity, weights, opposite, table_other, table_shear = lattice()
    moment_in = np.concatenate([weights[None, :], (weights[:, None] * velocity).T], 0)
    density_momentum = jnp.einsum("ki,nic->nkc", jnp.asarray(moment_in, jnp.float32), current, precision=lax.Precision.HIGHEST)
    density = density_momentum[:, 0]
    momentum = density_momentum[:, 1:]
    projected = jnp.einsum("ik,nkc->nic", jnp.asarray(velocity, jnp.float32), momentum, precision=lax.Precision.HIGHEST)
    speed_sq = jnp.sum(momentum * momentum, axis=1)
    equilibrium = density[:, None] + 3.0 * projected + 4.5 * projected * projected - 1.5 * speed_sq[:, None]
    departure = current - equilibrium
    matrices = jnp.asarray(table_other, jnp.float32)[None] + rates[:, None, None] * jnp.asarray(table_shear, jnp.float32)[None]
    return current - jnp.einsum("nij,njc->nic", matrices, departure, precision=lax.Precision.HIGHEST)


def make_slabs(collided, fluid_flags):
    velocity = lattice()[0]
    block_count = collided.shape[0]
    blocked = collided.reshape(block_count, 19, BLOCK, BLOCK, BLOCK)
    wet_cells = fluid_flags.reshape(block_count, BLOCK, BLOCK, BLOCK).astype(jnp.float32)
    face_list = []
    for lane_num in range(1, 7):
        axis_num = int(np.argmax(np.abs(velocity[lane_num])))
        side_sign = int(velocity[lane_num][axis_num])
        layer_index = BLOCK - 1 if side_sign > 0 else 0
        members = [lane_two for lane_two in range(19) if int(velocity[lane_two][axis_num]) == side_sign]
        layer_values = lax.index_in_dim(blocked, layer_index, axis_num + 2, keepdims=False)[:, members]
        layer_flags = lax.index_in_dim(wet_cells, layer_index, axis_num + 1, keepdims=False)
        face_list.append(jnp.concatenate([layer_values, layer_flags[:, None]], 1).reshape(block_count, 6, BLOCK * BLOCK))
    edge_list = []
    for lane_num in range(7, 19):
        nonzero = [axis_num for axis_num in range(3) if int(velocity[lane_num][axis_num]) != 0]
        axis_one, axis_two = nonzero
        end_one = BLOCK - 1 if velocity[lane_num][axis_one] > 0 else 0
        end_two = BLOCK - 1 if velocity[lane_num][axis_two] > 0 else 0
        line_values = lax.index_in_dim(lax.index_in_dim(blocked[:, lane_num], end_one, axis_one + 1, keepdims=False), end_two, axis_two, keepdims=False)
        line_flags = lax.index_in_dim(lax.index_in_dim(wet_cells, end_one, axis_one + 1, keepdims=False), end_two, axis_two, keepdims=False)
        edge_list.append(jnp.stack([line_values, line_flags], 1))
    return jnp.stack(face_list, 1), jnp.stack(edge_list, 1)


def propagate(current, collided, fluid_flags, rim_faces, rim_edges):
    velocity, weights, opposite, table_other, table_shear = lattice()
    block_count = current.shape[0]
    blocked = collided.reshape(block_count, 19, BLOCK, BLOCK, BLOCK)
    wet_cells = fluid_flags.reshape(block_count, BLOCK, BLOCK, BLOCK).astype(jnp.float32)
    padded = jnp.zeros((block_count, 19, BLOCK + 2, BLOCK + 2, BLOCK + 2), collided.dtype)
    padded = padded.at[:, :, 1:-1, 1:-1, 1:-1].set(blocked)
    open_mask = jnp.zeros((block_count, BLOCK + 2, BLOCK + 2, BLOCK + 2), wet_cells.dtype)
    open_mask = open_mask.at[:, 1:-1, 1:-1, 1:-1].set(wet_cells)
    inner = slice(1, BLOCK + 1)
    for face_num in range(6):
        lane_num = face_num + 1
        axis_num = int(np.argmax(np.abs(velocity[lane_num])))
        side_sign = int(velocity[lane_num][axis_num])
        rim_at = BLOCK + 1 if side_sign > 0 else 0
        spatial = tuple(rim_at if axis_two == axis_num else inner for axis_two in range(3))
        members = [lane_two for lane_two in range(19) if int(velocity[lane_two][axis_num]) == -side_sign]
        face_values = rim_faces[:, face_num].reshape(block_count, 6, BLOCK, BLOCK)
        for member_num, lane_two in enumerate(members):
            padded = padded.at[(slice(None), lane_two) + spatial].set(face_values[:, member_num])
        open_mask = open_mask.at[(slice(None),) + spatial].set(face_values[:, 5])
    for edge_num in range(12):
        lane_num = edge_num + 7
        spatial = tuple((BLOCK + 1 if velocity[lane_num][axis_two] > 0 else 0) if int(velocity[lane_num][axis_two]) != 0 else inner for axis_two in range(3))
        padded = padded.at[(slice(None), opposite[lane_num]) + spatial].set(rim_edges[:, edge_num, 0])
        open_mask = open_mask.at[(slice(None),) + spatial].set(rim_edges[:, edge_num, 1])
    arrived_list = []
    for lane_num in range(19):
        window = tuple(slice(1 - int(component), 1 - int(component) + BLOCK) for component in velocity[lane_num])
        pulled = padded[(slice(None), lane_num) + window]
        open_here = open_mask[(slice(None),) + window]
        arrived_list.append(jnp.where(open_here > 0, pulled, blocked[:, opposite[lane_num]]))
    arrived = jnp.stack(arrived_list, 1).reshape(block_count, 19, BLOCK * BLOCK * BLOCK)
    return jnp.where(fluid_flags[:, None, :] > 0, arrived, current)


def reference(populations, fluid_flags, neighbours, relax_rate):
    device_count = N_GROUP * N_DEV
    current = populations
    flags_split = fluid_flags.reshape(device_count, SLOTS, CELLS)
    table_split = neighbours.reshape(device_count, SLOTS, 18)
    rates_split = relax_rate.reshape(device_count, SLOTS)
    for step_num in range(STEPS):
        def slab_share(packed):
            share_pops, share_flags, share_rates = packed
            return make_slabs(collide(share_pops, share_rates), share_flags)

        face_slabs, edge_slabs = lax.map(slab_share, (current.reshape(device_count, SLOTS, 19, CELLS), flags_split, rates_split))
        face_slabs = face_slabs.reshape((NBLOCKS,) + face_slabs.shape[2:])
        edge_slabs = edge_slabs.reshape((NBLOCKS,) + edge_slabs.shape[2:])

        def advance(packed):
            share_pops, share_flags, share_table, share_rates, device_num = packed
            collided = collide(share_pops, share_rates)
            present = share_table >= 0
            global_id = jnp.where(present, (device_num + share_table // SLOTS - 1) * SLOTS + share_table % SLOTS, 0)
            rim_faces = jnp.stack([jnp.where(present[:, face_num, None, None], face_slabs[global_id[:, face_num], face_num ^ 1], 0.0) for face_num in range(6)], 1)
            rim_edges = jnp.stack([jnp.where(present[:, 6 + edge_num, None, None], edge_slabs[global_id[:, 6 + edge_num], 4 * (edge_num // 4) + 3 - edge_num % 4], 0.0) for edge_num in range(12)], 1)
            return propagate(share_pops, collided, share_flags, rim_faces, rim_edges)

        current = lax.map(advance, (current.reshape(device_count, SLOTS, 19, CELLS), flags_split, table_split, rates_split, jnp.arange(device_count, dtype=jnp.int32)))
        current = current.reshape(NBLOCKS, 19, CELLS)
    return current
```

```python
import functools

import jax
import jax.numpy as jnp
import numpy as np
from jax import lax
from jax.experimental import pallas as pl
from jax.experimental.pallas import tpu as pltpu
from jax.sharding import PartitionSpec as P

LANES = 128
ROWS = 32
PAD = 8
HEIGHT = ROWS + 2 * PAD
CLOSED = 1.0e30
LIMIT = 1.0e29


def directions():
    listed = [(0, 0, 0)]
    for axis in range(3):
        for sign in (1, -1):
            vector = [0, 0, 0]
            vector[axis] = sign
            listed.append(tuple(vector))
    for one, two in ((0, 1), (0, 2), (1, 2)):
        for sign_one in (1, -1):
            for sign_two in (1, -1):
                vector = [0, 0, 0]
                vector[one] = sign_one
                vector[two] = sign_two
                listed.append(tuple(vector))
    return listed


C = directions()
INDEX = {vector: num for num, vector in enumerate(C)}
OPP = [INDEX[tuple(-part for part in vector)] for vector in C]
FLAT = ((0, 0), (1, 0), (-1, 0), (0, 1), (0, -1))
UPWARD = [INDEX[(a, b, 1)] for a, b in FLAT]
DOWNWARD = [INDEX[(a, b, -1)] for a, b in FLAT]
N_MOM = 9
N_MSG = N_MOM + 5 + 1


def column(vector):
    return INDEX[vector] - 1


def moments(g):
    sx, dx = g[1] + g[2], g[1] - g[2]
    sy, dy = g[3] + g[4], g[3] - g[4]
    sz, dz = g[5] + g[6], g[5] - g[6]
    pairs = []
    for base in (7, 11, 15):
        pairs.append((g[base] + g[base + 3], g[base] - g[base + 3], g[base + 1] + g[base + 2], g[base + 1] - g[base + 2]))
    (xys, xyd, xyt, xye), (xzs, xzd, xzt, xze), (yzs, yzd, yzt, yze) = pairs
    exy, exz, eyz = xys + xyt, xzs + xzt, yzs + yzt
    rho = g[0] * (1.0 / 3.0) + (sx + sy + sz) * (1.0 / 18.0) + (exy + exz + eyz) * (1.0 / 36.0)
    ux = dx * (1.0 / 6.0) + (xyd + xye + xzd + xze) * (1.0 / 12.0)
    uy = dy * (1.0 / 6.0) + (xyd - xye + yzd + yze) * (1.0 / 12.0)
    uz = dz * (1.0 / 6.0) + (xzd - xze + yzd - yze) * (1.0 / 12.0)
    qxy = (xys - xyt) * 0.25
    qxz = (xzs - xzt) * 0.25
    qyz = (yzs - yzt) * 0.25
    gxz = (sx - sz) * 0.5 + (exy - eyz) * 0.25
    gyz = (sy - sz) * 0.5 + (exy - exz) * 0.25
    return [rho, ux, uy, uz, qxy, qxz, qyz, gxz, gyz]


def add_crossing(mom, e, sign):
    ez, xp, xm, yp, ym = e
    rho, ux, uy, uz, qxy, qxz, qyz, gxz, gyz = mom
    xs, xd, ys, yd = xp + xm, xp - xm, yp + ym, yp - ym
    four = xs + ys
    half = ez * 0.5
    return [
        rho + ez * (1.0 / 18.0) + four * (1.0 / 36.0),
        ux + xd * (1.0 / 12.0),
        uy + yd * (1.0 / 12.0),
        uz + sign * (ez * (1.0 / 6.0) + four * (1.0 / 12.0)),
        qxy,
        qxz + (sign * 0.25) * xd,
        qyz + (sign * 0.25) * yd,
        gxz - ys * 0.25 - half,
        gyz - xs * 0.25 - half,
    ]


def collided_from(mom, tau, wanted=None):
    rho, ux, uy, uz, qxy, qxz, qyz, gxz, gyz = mom
    xx, yy, zz = ux * ux, uy * uy, uz * uz
    base = rho - (xx + yy + zz) * (1.0 / 6.0)
    hx = gxz - (xx - zz)
    hy = gyz - (yy - zz)
    third = tau * (1.0 / 3.0)
    shear = {
        (0,): third * (hx + hx - hy),
        (1,): third * (hy + hy - hx),
        (2,): -third * (hx + hy),
        (0, 1): tau * (qxy - ux * uy),
        (0, 2): tau * (qxz - ux * uz),
        (1, 2): tau * (qyz - uy * uz),
    }
    u = (ux, uy, uz)
    out = {0: base}
    wanted = range(19) if wanted is None else wanted
    for num in wanted:
        if num in out:
            continue
        vector = C[num]
        axes = tuple(axis for axis in range(3) if vector[axis])
        if len(axes) == 1:
            speed = u[axes[0]]
            lead = vector[axes[0]]
            even = base + speed * speed * 0.5 + shear[axes]
        else:
            first, second = vector[axes[0]], vector[axes[1]]
            speed = u[axes[0]] + u[axes[1]] if first == second else u[axes[0]] - u[axes[1]]
            lead = first
            even = base + speed * speed * 0.5
            even = even + shear[axes] if first == second else even - shear[axes]
        plus = num if lead > 0 else OPP[num]
        out[plus] = even + speed
        out[OPP[plus]] = even - speed
    return out


def turned(value, shift):
    shift = shift % LANES
    return value if shift == 0 else pltpu.roll(value, shift, 1)


def iotas():
    lane = lax.broadcasted_iota(jnp.int32, (8, LANES), 1)
    row = lax.broadcasted_iota(jnp.int32, (8, LANES), 0)
    return row, lane


def fill_closed(pops, slots):
    blank = jnp.full((8, LANES), CLOSED, jnp.float32)
    for num in range(1, 19):
        if C[num][0] or C[num][1]:
            for group in range(4):
                pops[num, slots, PAD + 8 * group : PAD + 8 * group + 8, :] = blank


def plane_slot(nbr, block, vector, slots):
    entry = nbr[block, column(vector)]
    return jnp.where(entry >= 0, entry - slots, slots)


def fill_x_rims(pops, nbr, slots):
    for block in range(slots):
        before = plane_slot(nbr, block, (-1, 0, 0), slots)
        after = plane_slot(nbr, block, (1, 0, 0), slots)
        for num in range(1, 19):
            if C[num][0] > 0:
                pops[num, block, PAD - 2 : PAD, :] = pops[num, before, PAD + ROWS - 2 : PAD + ROWS, :]
            elif C[num][0] < 0:
                pops[num, block, PAD + ROWS : PAD + ROWS + 2, :] = pops[num, after, PAD : PAD + 2, :]


def pulled(pops, nbr, block, group, num, slots, row, lane):
    cx, cy, cz = C[num]
    start = PAD + 8 * group - 2 * cx
    value = pops[num, block, start : start + 8, :]
    if cy:
        own = pops[num, block, start - cy : start - cy + 8, :]
        beside = plane_slot(nbr, block, (0, -cy, 0), slots)
        other = pops[num, beside, start + cy : start + cy + 8, :]
        if cx and group == (0 if cx > 0 else 3):
            corner = plane_slot(nbr, block, (-cx, -cy, 0), slots)
            at = start + cy + (ROWS if cx > 0 else -ROWS)
            edge = pops[num, corner, at : at + 8, :]
            other = jnp.where((row < 2) if cx > 0 else (row >= 6), edge, other)
        high = (row & 1) == 1
        crossing = jnp.where(high, own, other) if cy > 0 else jnp.where(high, other, own)
        value = jnp.where((lane >= 112) if cy > 0 else (lane < 16), crossing, value)
    return turned(value, 16 * cy + cz)


def slot_vector(entries, base, lane, slots):
    own = (lane >> 2) & 3
    found = jnp.full((8, LANES), -1, jnp.int32)
    for slot in range(slots):
        entry = entries[slot]
        found = jnp.where((own == slot) & (entry >= 0), entry - base, found)
    return found


def naming_vector(entries, base, lane, slots):
    own = (lane >> 2) & 3
    found = jnp.full((8, LANES), -1, jnp.int32)
    for block in range(slots):
        found = jnp.where(own == entries[block] - base, block, found)
    return found


def face_sources(flat, straight, corner, row, lane):
    cx, cy = flat
    up = (lane >> 4) & 7
    part = lane & 3
    if cx:
        edge_row = (row < 2) if cx > 0 else (row >= 6)
        leaves = edge_row & (part == (0 if cx > 0 else 3))
        part = jnp.where(edge_row, (part - cx) & 3, part)
        slot = jnp.where(leaves, corner, straight)
    elif cy:
        at = up == (0 if cy > 0 else 7)
        leaves = at & ((row & 1) == (0 if cy > 0 else 1))
        up = (up - cy) & 7
        slot = jnp.where(leaves, corner, straight)
    else:
        slot = straight
    return jnp.where(slot >= 0, up * 16 + slot * 4 + part, -1)


def face_pull(plane, flat, source, row, lane):
    cx, cy = flat
    if cx:
        plane = pltpu.roll(plane, (2 * cx) % 8, 0)
    elif cy:
        swapped = jnp.where((row & 1) == 1, pltpu.roll(plane, 1, 0), pltpu.roll(plane, 7, 0))
        plane = jnp.where((lane >= 112) if cy > 0 else (lane < 16), swapped, plane)
    moved = jnp.take_along_axis(plane, jnp.maximum(source, 0), axis=1)
    return jnp.where(source >= 0, moved, CLOSED)


def stage_flags(flags, flag_tiles, slots):
    for tile in range(ROWS):
        flag_tiles[8 * tile : 8 * tile + slots, :] = flags[:, LANES * tile : LANES * tile + LANES]


def wet(flag_tiles, block, group):
    return flag_tiles[pl.ds(64 * group + block, 8, stride=8), :] > 0


def tile_row(block, num, tile):
    return ((block * 3 + num // 8) * ROWS + tile) * 8


def first_kernel(pop_hbm, flags, nbr, rate, mom_out, msg_even, msg_odd, raw, tiles, flag_tiles, pops, sides, sems):
    slots = flags.shape[0]
    copies = [pltpu.make_async_copy(pop_hbm.at[b], raw.at[b], sems.at[b]) for b in range(slots)]
    for copy in copies:
        copy.start()
    row, lane = iotas()
    stage_flags(flags, flag_tiles, slots)
    fill_closed(pops, slots)
    depth = lane & 15
    for block in range(slots):
        copies[block].wait()
        for first in (0, 8, 16):
            high = min(first + 8, 19)
            for tile in range(ROWS):
                at = tile_row(block, first, tile)
                tiles[at : at + high - first, :] = raw[block, first:high, LANES * tile : LANES * tile + LANES]
        tau = 1.0 - rate[block]
        for group in range(4):
            g = [tiles[pl.ds(tile_row(block, num, 8 * group) + num % 8, 8, stride=8), :] for num in range(19)]
            h = collided_from(moments(g), tau)
            fluid = wet(flag_tiles, block, group)
            spot = depth == 4 * block + group
            for num in range(19):
                value = jnp.where(fluid, h[num], CLOSED)
                pops[num, block, PAD + 8 * group : PAD + 8 * group + 8, :] = value
                if num in UPWARD:
                    pltpu.store(sides.at[0, N_MOM + UPWARD.index(num)], turned(value, 4 * block + group - 15), mask=spot)
                if num in DOWNWARD:
                    pltpu.store(sides.at[1, N_MOM + DOWNWARD.index(num)], turned(value, 4 * block + group), mask=spot)
    fill_x_rims(pops, nbr, slots)
    for block in range(slots):
        for group in range(4):
            g = []
            for num in range(19):
                if num == 0:
                    g.append(pops[0, block, PAD + 8 * group : PAD + 8 * group + 8, :])
                    continue
                value = pulled(pops, nbr, block, group, num, slots, row, lane)
                back = pops[OPP[num], block, PAD + 8 * group : PAD + 8 * group + 8, :]
                value = jnp.where(value < LIMIT, value, back)
                if C[num][2]:
                    value = jnp.where(depth == (0 if C[num][2] > 0 else 15), 0.0, value)
                g.append(value)
            mom = moments(g)
            spot = depth == 4 * block + group
            for at in range(N_MOM):
                mom_out[at, block, 8 * group : 8 * group + 8, :] = mom[at]
                pltpu.store(sides.at[0, at], turned(mom[at], 4 * block + group - 15), mask=spot)
                pltpu.store(sides.at[1, at], turned(mom[at], 4 * block + group), mask=spot)
    own = (lane >> 2) & 3
    tau = jnp.zeros((8, LANES), jnp.float32)
    for block in range(slots):
        tau = jnp.where(own == block, 1.0 - rate[block], tau)
    odd = lax.axis_index("dev") % 2 == 1
    for at in range(N_MSG):
        upper = tau if at == N_MSG - 1 else sides[0, at]
        lower = tau if at == N_MSG - 1 else sides[1, at]
        msg_even[at] = jnp.where(odd, lower, upper)
        msg_odd[at] = jnp.where(odd, upper, lower)


def second_kernel(
    pop_hbm, flags, nbr, rate, mom_in, msg_even, msg_odd, got_even, got_odd, out_hbm,
    raw, tiles, flag_tiles, pops, faces, sems, out_sems,
):
    slots = flags.shape[0]
    copies = [pltpu.make_async_copy(pop_hbm.at[b], raw.at[b], sems.at[b]) for b in range(slots)]
    for copy in copies:
        copy.start()
    row, lane = iotas()
    depth = lane & 15
    stage_flags(flags, flag_tiles, slots)
    fill_closed(pops, slots)
    odd = lax.axis_index("dev") % 2 == 1

    def upper_own(at):
        return jnp.where(odd, msg_odd[at], msg_even[at])

    def lower_own(at):
        return jnp.where(odd, msg_even[at], msg_odd[at])

    def upper_got(at):
        return jnp.where(odd, got_odd[at], got_even[at])

    def lower_got(at):
        return jnp.where(odd, got_even[at], got_odd[at])

    for side, sign in ((0, 1), (1, -1)):
        own_msg, got_msg = (upper_own, upper_got) if sign > 0 else (lower_own, lower_got)
        base = (sign + 1) * slots
        inward = DOWNWARD if sign > 0 else UPWARD
        outward = UPWARD if sign > 0 else DOWNWARD
        straight = slot_vector([nbr[b, column((0, 0, sign))] for b in range(slots)], base, lane, slots)
        naming = naming_vector([nbr[b, column((0, 0, sign))] for b in range(slots)], base, lane, slots)
        own_out = [own_msg(N_MOM + at) for at in range(5)]
        got_in = [got_msg(N_MOM + at) for at in range(5)]
        entering, leaving, sources = [], [], []
        for at, (cx, cy) in enumerate(FLAT):
            if cx or cy:
                toward = [nbr[b, column((-cx, -cy, sign))] for b in range(slots)]
                corner = slot_vector(toward, base, lane, slots)
                away = [nbr[b, column((cx, cy, sign))] for b in range(slots)]
                far_corner = naming_vector(away, base, lane, slots)
            else:
                corner, far_corner = straight, naming
            source = face_sources((cx, cy), straight, corner, row, lane)
            sources.append(source)
            value = face_pull(got_in[at], (cx, cy), source, row, lane)
            mirror = FLAT.index((-cx, -cy))
            entering.append(jnp.where(value < LIMIT, value, own_out[mirror]))
            far = face_sources((cx, cy), naming, far_corner, row, lane)
            value = face_pull(own_out[at], (cx, cy), far, row, lane)
            leaving.append(jnp.where(value < LIMIT, value, got_in[mirror]))
        for at in range(5):
            faces[side, at] = entering[at]
        mom = add_crossing([got_msg(at) for at in range(N_MOM)], leaving, float(sign))
        h = collided_from(mom, got_msg(N_MSG - 1), inward)
        for at, flat in enumerate(FLAT):
            value = jnp.where(got_in[0] < LIMIT, h[inward[at]], CLOSED)
            faces[side, 5 + at] = face_pull(value, flat, sources[at], row, lane)

    top, bottom = depth == 15, depth == 0
    sign = jnp.where(bottom, 1.0, -1.0)
    for block in range(slots):
        tau = 1.0 - rate[block]
        for group in range(4):
            shift = 4 * block + group
            crossing = []
            for at in range(5):
                value = jnp.where(top, turned(faces[0, at], 15 - shift), 0.0)
                crossing.append(jnp.where(bottom, turned(faces[1, at], -shift), value))
            mom = [mom_in[at, block, 8 * group : 8 * group + 8, :] for at in range(N_MOM)]
            h = collided_from(add_crossing(mom, crossing, sign), tau)
            fluid = wet(flag_tiles, block, group)
            for num in range(19):
                pops[num, block, PAD + 8 * group : PAD + 8 * group + 8, :] = jnp.where(fluid, h[num], CLOSED)
    fill_x_rims(pops, nbr, slots)
    outs = [pltpu.make_async_copy(raw.at[b], out_hbm.at[b], out_sems.at[b]) for b in range(slots)]
    for block in range(slots):
        for group in range(4):
            shift = 4 * block + group
            for num in range(19):
                back = pops[OPP[num], block, PAD + 8 * group : PAD + 8 * group + 8, :]
                if num:
                    cx, cy, cz = C[num]
                    value = pulled(pops, nbr, block, group, num, slots, row, lane)
                    if cz > 0:
                        value = jnp.where(bottom, turned(faces[1, 5 + UPWARD.index(num)], -shift), value)
                    elif cz < 0:
                        value = jnp.where(top, turned(faces[0, 5 + DOWNWARD.index(num)], 15 - shift), value)
                    value = jnp.where(value < LIMIT, value, back)
                else:
                    value = back
                tiles[pl.ds(tile_row(block, num, 8 * group) + num % 8, 8, stride=8), :] = value
        copies[block].wait()
        for tile in range(ROWS):
            fluid = flags[block : block + 1, LANES * tile : LANES * tile + LANES] > 0
            for first in (0, 8, 16):
                high = min(first + 8, 19)
                at = tile_row(block, first, tile)
                where = (block, slice(first, high), slice(LANES * tile, LANES * tile + LANES))
                raw[where] = jnp.where(fluid, tiles[at : at + high - first, :], raw[where])
        outs[block].start()
    for block in range(slots):
        outs[block].wait()


def body(populations, fluid_flags, neighbours, relax_rate):
    slots, _, cells = populations.shape
    assert cells == ROWS * LANES and slots <= 4
    peers = lax.axis_size("dev")
    assert peers % 2 == 0
    vmem = pl.BlockSpec(memory_space=pltpu.VMEM)
    smem = pl.BlockSpec(memory_space=pltpu.SMEM)
    anywhere = pl.BlockSpec(memory_space=pl.ANY)
    face = (8, LANES)
    raw = pltpu.VMEM((slots, 19, cells), jnp.float32)
    tiles = pltpu.VMEM((slots * 3 * ROWS * 8, LANES), jnp.float32)
    flag_tiles = pltpu.VMEM((8 * ROWS, LANES), jnp.int32)
    pops = pltpu.VMEM((19, slots + 1, HEIGHT, LANES), jnp.float32)
    message = jax.ShapeDtypeStruct((N_MSG,) + face, jnp.float32)
    mom, msg_even, msg_odd = pl.pallas_call(
        first_kernel,
        out_shape=(jax.ShapeDtypeStruct((N_MOM, slots, ROWS, LANES), jnp.float32), message, message),
        in_specs=[anywhere, vmem, smem, smem],
        out_specs=(vmem, vmem, vmem),
        scratch_shapes=[
            raw, tiles, flag_tiles, pops,
            pltpu.VMEM((2, N_MOM + 5) + face, jnp.float32),
            pltpu.SemaphoreType.DMA((slots,)),
        ],
        name="collide_and_stream",
    )(populations, fluid_flags, neighbours, relax_rate)
    even_pairs = [(i, i ^ 1) for i in range(peers)]
    odd_pairs = [(i, (i + 1) % peers if i % 2 else (i - 1) % peers) for i in range(peers)]
    got_odd = lax.ppermute(msg_odd, "dev", odd_pairs)
    got_even = lax.ppermute(msg_even, "dev", even_pairs)
    return pl.pallas_call(
        second_kernel,
        out_shape=jax.ShapeDtypeStruct(populations.shape, jnp.float32),
        in_specs=[anywhere, vmem, smem, smem, vmem, vmem, vmem, vmem, vmem],
        out_specs=anywhere,
        scratch_shapes=[
            raw, tiles, flag_tiles, pops,
            pltpu.VMEM((2, 10) + face, jnp.float32),
            pltpu.SemaphoreType.DMA((slots,)),
            pltpu.SemaphoreType.DMA((slots,)),
        ],
        name="finish",
    )(populations, fluid_flags, neighbours, relax_rate, mom, msg_even, msg_odd, got_even, got_odd)


def solution(mesh):
    placed = (
        P(("group", "dev"), None, None),
        P(("group", "dev"), None),
        P(("group", "dev"), None),
        P(("group", "dev")),
    )
    return jax.shard_map(
        body, mesh=mesh, in_specs=placed, out_specs=P(("group", "dev"), None, None), check_vma=False
    )
```

```python
import jax
import jax.numpy as jnp
from jax import lax
from jax.experimental import pallas as pl
from jax.experimental.pallas import tpu as pltpu
from jax.sharding import PartitionSpec as P

EDGE = 16
LANES = 128
SUB = 8
CLOSED = 1.0e30
LIMIT = 1.0e29
GROUP = 4


def directions():
    listed = [(0, 0, 0)]
    for axis in range(3):
        for sign in (1, -1):
            vector = [0, 0, 0]
            vector[axis] = sign
            listed.append(tuple(vector))
    for one, two in ((0, 1), (0, 2), (1, 2)):
        for sign_one in (1, -1):
            for sign_two in (1, -1):
                vector = [0, 0, 0]
                vector[one] = sign_one
                vector[two] = sign_two
                listed.append(tuple(vector))
    return listed


C = directions()
INDEX = {vector: num for num, vector in enumerate(C)}
OPP = [INDEX[tuple(-part for part in vector)] for vector in C]
FLAT = ((0, 0), (1, 0), (-1, 0), (0, 1), (0, -1))
UPWARD = [INDEX[(a, b, 1)] for a, b in FLAT]
DOWNWARD = [INDEX[(a, b, -1)] for a, b in FLAT]
N_MOM = 9
N_MSG = N_MOM + 5 + 1


def column(vector):
    return INDEX[vector] - 1


def moments(g):
    sx, dx = g[1] + g[2], g[1] - g[2]
    sy, dy = g[3] + g[4], g[3] - g[4]
    sz, dz = g[5] + g[6], g[5] - g[6]
    pairs = []
    for base in (7, 11, 15):
        pairs.append((g[base] + g[base + 3], g[base] - g[base + 3], g[base + 1] + g[base + 2], g[base + 1] - g[base + 2]))
    (xys, xyd, xyt, xye), (xzs, xzd, xzt, xze), (yzs, yzd, yzt, yze) = pairs
    exy, exz, eyz = xys + xyt, xzs + xzt, yzs + yzt
    rho = g[0] * (1.0 / 3.0) + (sx + sy + sz) * (1.0 / 18.0) + (exy + exz + eyz) * (1.0 / 36.0)
    ux = dx * (1.0 / 6.0) + (xyd + xye + xzd + xze) * (1.0 / 12.0)
    uy = dy * (1.0 / 6.0) + (xyd - xye + yzd + yze) * (1.0 / 12.0)
    uz = dz * (1.0 / 6.0) + (xzd - xze + yzd - yze) * (1.0 / 12.0)
    qxy = (xys - xyt) * 0.25
    qxz = (xzs - xzt) * 0.25
    qyz = (yzs - yzt) * 0.25
    gxz = (sx - sz) * 0.5 + (exy - eyz) * 0.25
    gyz = (sy - sz) * 0.5 + (exy - exz) * 0.25
    return [rho, ux, uy, uz, qxy, qxz, qyz, gxz, gyz]


def add_crossing(mom, e, sign):
    ez, xp, xm, yp, ym = e
    rho, ux, uy, uz, qxy, qxz, qyz, gxz, gyz = mom
    xs, xd, ys, yd = xp + xm, xp - xm, yp + ym, yp - ym
    four = xs + ys
    half = ez * 0.5
    return [
        rho + ez * (1.0 / 18.0) + four * (1.0 / 36.0),
        ux + xd * (1.0 / 12.0),
        uy + yd * (1.0 / 12.0),
        uz + sign * (ez * (1.0 / 6.0) + four * (1.0 / 12.0)),
        qxy,
        qxz + (sign * 0.25) * xd,
        qyz + (sign * 0.25) * yd,
        gxz - ys * 0.25 - half,
        gyz - xs * 0.25 - half,
    ]


def collided_from(mom, tau, wanted=range(19)):
    rho, ux, uy, uz, qxy, qxz, qyz, gxz, gyz = mom
    xx, yy, zz = ux * ux, uy * uy, uz * uz
    base = rho - (xx + yy + zz) * (1.0 / 6.0)
    hx = gxz - (xx - zz)
    hy = gyz - (yy - zz)
    third = tau * (1.0 / 3.0)
    shear = {
        (0,): third * (hx + hx - hy),
        (1,): third * (hy + hy - hx),
        (2,): -third * (hx + hy),
        (0, 1): tau * (qxy - ux * uy),
        (0, 2): tau * (qxz - ux * uz),
        (1, 2): tau * (qyz - uy * uz),
    }
    u = (ux, uy, uz)
    out = {0: base}
    for num in wanted:
        if num in out:
            continue
        vector = C[num]
        axes = tuple(axis for axis in range(3) if vector[axis])
        if len(axes) == 1:
            speed = u[axes[0]]
            lead = vector[axes[0]]
            even = base + speed * speed * 0.5 + shear[axes]
        else:
            first, second = vector[axes[0]], vector[axes[1]]
            speed = u[axes[0]] + u[axes[1]] if first == second else u[axes[0]] - u[axes[1]]
            lead = first
            even = base + speed * speed * 0.5
            even = even + shear[axes] if first == second else even - shear[axes]
        plus = num if lead > 0 else OPP[num]
        out[plus] = even + speed
        out[OPP[plus]] = even - speed
    return out


def turned(value, shift):
    if isinstance(shift, int):
        shift = shift % LANES
        return value if shift == 0 else pltpu.roll(value, shift, 1)
    return pltpu.roll(value, (shift + LANES) % LANES, 1)


def picked(value, source):
    moved = jnp.take_along_axis(value, jnp.maximum(source, 0), axis=0)
    return jnp.where(source >= 0, moved, CLOSED)


class Place:
    def __init__(self, slots):
        self.slots = slots
        self.lane = lax.broadcasted_iota(jnp.int32, (SUB, LANES), 1)
        sub = lax.broadcasted_iota(jnp.int32, (SUB, LANES), 0)
        self.slot = sub % slots
        self.high = sub // slots
        self.depth = self.lane % EDGE

    def carry(self, cy):
        return self.lane >= LANES - EDGE if cy > 0 else self.lane < EDGE

    def named(self, entries, base):
        found = jnp.full((SUB, LANES), -1, jnp.int32)
        for slot, entry in enumerate(entries):
            found = jnp.where(self.slot == slot, jnp.where(entry >= 0, entry - base, -1), found)
        return found

    def naming(self, entries, base):
        found = jnp.full((SUB, LANES), -1, jnp.int32)
        for slot, entry in enumerate(entries):
            found = jnp.where(self.slot == entry - base, slot, found)
        return found

    def straight(self, found):
        return jnp.where(found >= 0, self.high * self.slots + found, -1)

    def across(self, same, corner, cy):
        inner = self.high == (1 if cy > 0 else 0)
        found = jnp.where(inner, same, corner)
        return jnp.where(found >= 0, (1 - self.high) * self.slots + found, -1)


def column_of(nbr, vector, slots):
    return [nbr[slot, column(vector)] for slot in range(slots)]


def plane_maps(place, nbr):
    slots = place.slots
    maps = {}
    for cx in (1, -1):
        side = place.named(column_of(nbr, (-cx, 0, 0), slots), slots)
        maps[cx, 0] = place.straight(side)
        for cy in (1, -1):
            corner = place.named(column_of(nbr, (-cx, -cy, 0), slots), slots)
            maps[cx, cy] = place.across(side, corner, cy)
    for cy in (1, -1):
        beside = place.named(column_of(nbr, (0, -cy, 0), slots), slots)
        maps[0, cy] = place.across(place.slot, beside, cy)
    return maps


def store_collided(place, maps, still, moved, x, h, fluid):
    kept = []
    for num in range(19):
        cx, cy, cz = C[num]
        value = jnp.where(fluid, h[num], CLOSED)
        kept.append(value)
        still[num, x] = value
        if num:
            if cy:
                value = jnp.where(place.carry(cy), picked(value, maps[0, cy]), value)
            moved[num, x + 1] = turned(value, EDGE * cy + cz)
    return kept


def store_rims(place, maps, still, moved):
    for num in range(1, 19):
        cx, cy, cz = C[num]
        if cx:
            source = still[num, EDGE - 1 if cx > 0 else 0]
            value = picked(source, maps[cx, 0])
            if cy:
                value = jnp.where(place.carry(cy), picked(source, maps[cx, cy]), value)
            moved[num, 0 if cx > 0 else EDGE + 1] = turned(value, EDGE * cy + cz)


def face_pull(place, plane, flat, straight, corner):
    cx, cy = flat
    value = picked(plane, place.straight(straight))
    if cx:
        end = picked(plane, place.straight(corner))
        return jnp.where(place.depth == (0 if cx > 0 else EDGE - 1), turned(end, cx - EDGE * cx), turned(value, cx))
    if cy:
        value = jnp.where(place.carry(cy), picked(plane, place.across(straight, corner, cy)), value)
        return turned(value, EDGE * cy)
    return value


def tau_plane(place, rate):
    tau = jnp.zeros((SUB, LANES), jnp.float32)
    for slot in range(place.slots):
        tau = jnp.where(place.slot == slot, 1.0 - rate[slot], tau)
    return tau


def looped(start, stop, step):
    def run(x, carried):
        step(x)
        return carried

    lax.fori_loop(start, stop, run, 0, unroll=UNROLL)


UNROLL = 4


def first_kernel(pop_hbm, flags, nbr, rate, mom_out, msg_even, msg_odd, raw, still, moved, sides, sems):
    slots = nbr.shape[0]
    place = Place(slots)
    parts = [pl.ds(first, GROUP) for first in range(0, EDGE, GROUP)]
    copies = [pltpu.make_async_copy(pop_hbm.at[:, part], raw.at[:, part], sems.at[at]) for at, part in enumerate(parts)]
    for copy in copies:
        copy.start()
    maps = plane_maps(place, nbr)
    tau = tau_plane(place, rate)
    depth = place.depth

    def collide(x):
        h = collided_from(moments([raw[num, x] for num in range(19)]), tau)
        kept = store_collided(place, maps, still, moved, x, h, flags[x] > 0)
        for at in range(5):
            pltpu.store(sides.at[0, N_MOM + at], turned(kept[UPWARD[at]], x - (EDGE - 1)), mask=depth == x)
            pltpu.store(sides.at[1, N_MOM + at], turned(kept[DOWNWARD[at]], x), mask=depth == x)

    for at, copy in enumerate(copies):
        copy.wait()
        looped(at * GROUP, (at + 1) * GROUP, collide)
    store_rims(place, maps, still, moved)
    keep = {1: depth != 0, -1: depth != EDGE - 1}

    def stream(x):
        g = [still[0, x]]
        for num in range(1, 19):
            value = moved[num, x + 1 - C[num][0]]
            value = jnp.where(value < LIMIT, value, still[OPP[num], x])
            if C[num][2]:
                value = jnp.where(keep[C[num][2]], value, 0.0)
            g.append(value)
        mom = moments(g)
        for at in range(N_MOM):
            mom_out[at, x] = mom[at]
            pltpu.store(sides.at[0, at], turned(mom[at], x - (EDGE - 1)), mask=depth == x)
            pltpu.store(sides.at[1, at], turned(mom[at], x), mask=depth == x)

    looped(0, EDGE, stream)
    odd = lax.axis_index("dev") % 2 == 1
    for at in range(N_MSG):
        upper = tau if at == N_MSG - 1 else sides[0, at]
        lower = tau if at == N_MSG - 1 else sides[1, at]
        msg_even[at] = jnp.where(odd, lower, upper)
        msg_odd[at] = jnp.where(odd, upper, lower)


def second_kernel(
    pop_hbm, flags, nbr, rate, mom_in, msg_even, msg_odd, got_even, got_odd, out_hbm,
    raw, still, moved, faces, sems, out_sems,
):
    slots = nbr.shape[0]
    place = Place(slots)
    incoming = pltpu.make_async_copy(pop_hbm, raw, sems.at[0])
    incoming.start()
    maps = plane_maps(place, nbr)
    tau = tau_plane(place, rate)
    depth = place.depth
    odd = lax.axis_index("dev") % 2 == 1

    def upper_own(at):
        return jnp.where(odd, msg_odd[at], msg_even[at])

    def lower_own(at):
        return jnp.where(odd, msg_even[at], msg_odd[at])

    def upper_got(at):
        return jnp.where(odd, got_odd[at], got_even[at])

    def lower_got(at):
        return jnp.where(odd, got_even[at], got_odd[at])

    for side, sign in ((0, 1), (1, -1)):
        own_msg, got_msg = (upper_own, upper_got) if sign > 0 else (lower_own, lower_got)
        base = (sign + 1) * slots
        inward = DOWNWARD if sign > 0 else UPWARD
        upright = column_of(nbr, (0, 0, sign), slots)
        straight, back_straight = place.named(upright, base), place.naming(upright, base)
        own_out = [own_msg(N_MOM + at) for at in range(5)]
        got_in = [got_msg(N_MOM + at) for at in range(5)]
        leaving, corners = [], []
        for at, (cx, cy) in enumerate(FLAT):
            corner = back_corner = None
            if cx or cy:
                corner = place.named(column_of(nbr, (-cx, -cy, sign), slots), base)
                back_corner = place.naming(column_of(nbr, (cx, cy, sign), slots), base)
            corners.append(corner)
            mirror = FLAT.index((-cx, -cy))
            value = face_pull(place, got_in[at], (cx, cy), straight, corner)
            faces[side, at] = jnp.where(value < LIMIT, value, own_out[mirror])
            value = face_pull(place, own_out[at], (cx, cy), back_straight, back_corner)
            leaving.append(jnp.where(value < LIMIT, value, got_in[mirror]))
        mom = add_crossing([got_msg(at) for at in range(N_MOM)], leaving, float(sign))
        h = collided_from(mom, got_msg(N_MSG - 1), inward)
        for at, flat in enumerate(FLAT):
            value = jnp.where(got_in[0] < LIMIT, h[inward[at]], CLOSED)
            faces[side, 5 + at] = face_pull(place, value, flat, straight, corners[at])

    top, bottom = depth == EDGE - 1, depth == 0
    sign = jnp.where(bottom, 1.0, -1.0)

    def collide(x):
        crossing = []
        for at in range(5):
            value = jnp.where(top, turned(faces[0, at], EDGE - 1 - x), 0.0)
            crossing.append(jnp.where(bottom, turned(faces[1, at], -x), value))
        mom = add_crossing([mom_in[at, x] for at in range(N_MOM)], crossing, sign)
        store_collided(place, maps, still, moved, x, collided_from(mom, tau), flags[x] > 0)

    looped(0, EDGE, collide)
    store_rims(place, maps, still, moved)
    incoming.wait()

    def stream(x):
        fluid = flags[x] > 0
        for num in range(19):
            value = back = still[OPP[num], x]
            if num:
                cx, cy, cz = C[num]
                value = moved[num, x + 1 - cx]
                if cz > 0:
                    value = jnp.where(bottom, turned(faces[1, 5 + UPWARD.index(num)], -x), value)
                elif cz < 0:
                    value = jnp.where(top, turned(faces[0, 5 + DOWNWARD.index(num)], EDGE - 1 - x), value)
                value = jnp.where(value < LIMIT, value, back)
            raw[num, x] = jnp.where(fluid, value, raw[num, x])

    outs = []
    for at, first in enumerate(range(0, EDGE, GROUP)):
        looped(first, first + GROUP, stream)
        part = pl.ds(first, GROUP)
        outs.append(pltpu.make_async_copy(raw.at[:, part], out_hbm.at[:, part], out_sems.at[at]))
        outs[-1].start()
    for out in outs:
        out.wait()


def body(populations, fluid_flags, neighbours, relax_rate):
    slots, velocities, cells = populations.shape
    assert cells == EDGE**3 and 2 * slots == SUB and velocities == 19
    peers = lax.axis_size("dev")
    assert peers % 2 == 0
    tiles = cells // LANES
    view = (EDGE, SUB, LANES)
    pops = populations.transpose(1, 0, 2).reshape(19, slots, tiles, LANES).transpose(0, 2, 1, 3).reshape((19,) + view)
    flags = fluid_flags.reshape(slots, tiles, LANES).transpose(1, 0, 2).reshape(view)
    vmem = pl.BlockSpec(memory_space=pltpu.VMEM)
    smem = pl.BlockSpec(memory_space=pltpu.SMEM)
    hbm = pl.BlockSpec(memory_space=pltpu.HBM)
    face = (SUB, LANES)
    scratch = [
        pltpu.VMEM((19,) + view, jnp.float32),
        pltpu.VMEM((19,) + view, jnp.float32),
        pltpu.VMEM((19, EDGE + 2) + face, jnp.float32),
    ]
    params = pltpu.CompilerParams(vmem_limit_bytes=16 * 2**20)
    message = jax.ShapeDtypeStruct((N_MSG,) + face, jnp.float32)
    mom, msg_even, msg_odd = pl.pallas_call(
        first_kernel,
        out_shape=(jax.ShapeDtypeStruct((N_MOM,) + view, jnp.float32), message, message),
        in_specs=[hbm, vmem, smem, smem],
        out_specs=(vmem, vmem, vmem),
        scratch_shapes=scratch + [
            pltpu.VMEM((2, N_MOM + 5) + face, jnp.float32),
            pltpu.SemaphoreType.DMA((EDGE // GROUP,)),
        ],
        compiler_params=params,
        name="collide_and_stream",
    )(pops, flags, neighbours, relax_rate)
    even_pairs = [(i, i ^ 1) for i in range(peers)]
    odd_pairs = [(i, (i + 1) % peers if i % 2 else (i - 1) % peers) for i in range(peers)]
    got_odd = lax.ppermute(msg_odd, "dev", odd_pairs)
    got_even = lax.ppermute(msg_even, "dev", even_pairs)
    out = pl.pallas_call(
        second_kernel,
        out_shape=jax.ShapeDtypeStruct(pops.shape, jnp.float32),
        in_specs=[hbm, vmem, smem, smem, vmem, vmem, vmem, vmem, vmem],
        out_specs=hbm,
        scratch_shapes=scratch + [
            pltpu.VMEM((2, 10) + face, jnp.float32),
            pltpu.SemaphoreType.DMA((1,)),
            pltpu.SemaphoreType.DMA((EDGE // GROUP,)),
        ],
        compiler_params=params,
        name="finish",
    )(pops, flags, neighbours, relax_rate, mom, msg_even, msg_odd, got_even, got_odd)
    out = out.reshape(19, tiles, slots, LANES).transpose(0, 2, 1, 3).reshape(19, slots, cells)
    return out.transpose(1, 0, 2)


def solution(mesh):
    placed = (
        P(("group", "dev"), None, None),
        P(("group", "dev"), None),
        P(("group", "dev"), None),
        P(("group", "dev")),
    )
    return jax.shard_map(
        body, mesh=mesh, in_specs=placed, out_specs=P(("group", "dev"), None, None), check_vma=False
    )
```

```python
import jax
import jax.numpy as jnp
from jax import lax
from jax.experimental import pallas as pl
from jax.experimental.pallas import tpu as pltpu
from jax.sharding import PartitionSpec as P

EDGE = 16
LANES = 128
SUB = 8
CLOSED = 1.0e30
LIMIT = 1.0e29
GROUP = 4


def directions():
    listed = [(0, 0, 0)]
    for axis in range(3):
        for sign in (1, -1):
            vector = [0, 0, 0]
            vector[axis] = sign
            listed.append(tuple(vector))
    for one, two in ((0, 1), (0, 2), (1, 2)):
        for sign_one in (1, -1):
            for sign_two in (1, -1):
                vector = [0, 0, 0]
                vector[one] = sign_one
                vector[two] = sign_two
                listed.append(tuple(vector))
    return listed


C = directions()
INDEX = {vector: num for num, vector in enumerate(C)}
OPP = [INDEX[tuple(-part for part in vector)] for vector in C]
FLAT = ((0, 0), (1, 0), (-1, 0), (0, 1), (0, -1))
UPWARD = [INDEX[(a, b, 1)] for a, b in FLAT]
DOWNWARD = [INDEX[(a, b, -1)] for a, b in FLAT]
N_MOM = 9
N_MSG = N_MOM + 5 + 1


def column(vector):
    return INDEX[vector] - 1


def moments(g):
    sx, dx = g[1] + g[2], g[1] - g[2]
    sy, dy = g[3] + g[4], g[3] - g[4]
    sz, dz = g[5] + g[6], g[5] - g[6]
    pairs = []
    for base in (7, 11, 15):
        pairs.append((g[base] + g[base + 3], g[base] - g[base + 3], g[base + 1] + g[base + 2], g[base + 1] - g[base + 2]))
    (xys, xyd, xyt, xye), (xzs, xzd, xzt, xze), (yzs, yzd, yzt, yze) = pairs
    exy, exz, eyz = xys + xyt, xzs + xzt, yzs + yzt
    rho = g[0] * (1.0 / 3.0) + (sx + sy + sz) * (1.0 / 18.0) + (exy + exz + eyz) * (1.0 / 36.0)
    ux = dx * (1.0 / 6.0) + (xyd + xye + xzd + xze) * (1.0 / 12.0)
    uy = dy * (1.0 / 6.0) + (xyd - xye + yzd + yze) * (1.0 / 12.0)
    uz = dz * (1.0 / 6.0) + (xzd - xze + yzd - yze) * (1.0 / 12.0)
    qxy = (xys - xyt) * 0.25
    qxz = (xzs - xzt) * 0.25
    qyz = (yzs - yzt) * 0.25
    gxz = (sx - sz) * 0.5 + (exy - eyz) * 0.25
    gyz = (sy - sz) * 0.5 + (exy - exz) * 0.25
    return [rho, ux, uy, uz, qxy, qxz, qyz, gxz, gyz]


def add_crossing(mom, e, sign):
    ez, xp, xm, yp, ym = e
    rho, ux, uy, uz, qxy, qxz, qyz, gxz, gyz = mom
    xs, xd, ys, yd = xp + xm, xp - xm, yp + ym, yp - ym
    four = xs + ys
    half = ez * 0.5
    return [
        rho + ez * (1.0 / 18.0) + four * (1.0 / 36.0),
        ux + xd * (1.0 / 12.0),
        uy + yd * (1.0 / 12.0),
        uz + sign * (ez * (1.0 / 6.0) + four * (1.0 / 12.0)),
        qxy,
        qxz + (sign * 0.25) * xd,
        qyz + (sign * 0.25) * yd,
        gxz - ys * 0.25 - half,
        gyz - xs * 0.25 - half,
    ]


def collided_from(mom, tau, wanted=range(19)):
    rho, ux, uy, uz, qxy, qxz, qyz, gxz, gyz = mom
    xx, yy, zz = ux * ux, uy * uy, uz * uz
    base = rho - (xx + yy + zz) * (1.0 / 6.0)
    hx = gxz - (xx - zz)
    hy = gyz - (yy - zz)
    third = tau * (1.0 / 3.0)
    shear = {
        (0,): third * (hx + hx - hy),
        (1,): third * (hy + hy - hx),
        (2,): -third * (hx + hy),
        (0, 1): tau * (qxy - ux * uy),
        (0, 2): tau * (qxz - ux * uz),
        (1, 2): tau * (qyz - uy * uz),
    }
    u = (ux, uy, uz)
    out = {0: base}
    for num in wanted:
        if num in out:
            continue
        vector = C[num]
        axes = tuple(axis for axis in range(3) if vector[axis])
        if len(axes) == 1:
            speed = u[axes[0]]
            lead = vector[axes[0]]
            even = base + speed * speed * 0.5 + shear[axes]
        else:
            first, second = vector[axes[0]], vector[axes[1]]
            speed = u[axes[0]] + u[axes[1]] if first == second else u[axes[0]] - u[axes[1]]
            lead = first
            even = base + speed * speed * 0.5
            even = even + shear[axes] if first == second else even - shear[axes]
        plus = num if lead > 0 else OPP[num]
        out[plus] = even + speed
        out[OPP[plus]] = even - speed
    return out


def turned(value, shift):
    if isinstance(shift, int):
        shift = shift % LANES
        return value if shift == 0 else pltpu.roll(value, shift, 1)
    return pltpu.roll(value, (shift + LANES) % LANES, 1)


def picked(value, source):
    moved = jnp.take_along_axis(value, jnp.maximum(source, 0), axis=0)
    return jnp.where(source >= 0, moved, CLOSED)


class Place:
    def __init__(self, slots):
        self.slots = slots
        self.lane = lax.broadcasted_iota(jnp.int32, (SUB, LANES), 1)
        sub = lax.broadcasted_iota(jnp.int32, (SUB, LANES), 0)
        self.slot = sub % slots
        self.high = sub // slots
        self.depth = self.lane % EDGE

    def carry(self, cy):
        return self.lane >= LANES - EDGE if cy > 0 else self.lane < EDGE

    def named(self, entries, base):
        found = jnp.full((SUB, LANES), -1, jnp.int32)
        for slot, entry in enumerate(entries):
            found = jnp.where(self.slot == slot, jnp.where(entry >= 0, entry - base, -1), found)
        return found

    def naming(self, entries, base):
        found = jnp.full((SUB, LANES), -1, jnp.int32)
        for slot, entry in enumerate(entries):
            found = jnp.where(self.slot == entry - base, slot, found)
        return found

    def straight(self, found):
        return jnp.where(found >= 0, self.high * self.slots + found, -1)

    def across(self, same, corner, cy):
        inner = self.high == (1 if cy > 0 else 0)
        found = jnp.where(inner, same, corner)
        return jnp.where(found >= 0, (1 - self.high) * self.slots + found, -1)


def column_of(nbr, vector, slots):
    return [nbr[slot, column(vector)] for slot in range(slots)]


def plane_maps(place, nbr):
    slots = place.slots
    maps = {}
    for cx in (1, -1):
        side = place.named(column_of(nbr, (-cx, 0, 0), slots), slots)
        maps[cx, 0] = place.straight(side)
        for cy in (1, -1):
            corner = place.named(column_of(nbr, (-cx, -cy, 0), slots), slots)
            maps[cx, cy] = place.across(side, corner, cy)
    for cy in (1, -1):
        beside = place.named(column_of(nbr, (0, -cy, 0), slots), slots)
        maps[0, cy] = place.across(place.slot, beside, cy)
    return maps


def store_collided(place, maps, still, moved, x, h, fluid):
    kept = []
    for num in range(19):
        cx, cy, cz = C[num]
        value = jnp.where(fluid, h[num], CLOSED)
        kept.append(value)
        still[num, x] = value
        if num:
            if cy:
                value = jnp.where(place.carry(cy), picked(value, maps[0, cy]), value)
            moved[num, x + 1] = turned(value, EDGE * cy + cz)
    return kept


def store_rims(place, maps, still, moved):
    for num in range(1, 19):
        cx, cy, cz = C[num]
        if cx:
            source = still[num, EDGE - 1 if cx > 0 else 0]
            value = picked(source, maps[cx, 0])
            if cy:
                value = jnp.where(place.carry(cy), picked(source, maps[cx, cy]), value)
            moved[num, 0 if cx > 0 else EDGE + 1] = turned(value, EDGE * cy + cz)


def face_pull(place, plane, flat, straight, corner):
    cx, cy = flat
    value = picked(plane, place.straight(straight))
    if cx:
        end = picked(plane, place.straight(corner))
        return jnp.where(place.depth == (0 if cx > 0 else EDGE - 1), turned(end, cx - EDGE * cx), turned(value, cx))
    if cy:
        value = jnp.where(place.carry(cy), picked(plane, place.across(straight, corner, cy)), value)
        return turned(value, EDGE * cy)
    return value


def tau_plane(place, rate):
    tau = jnp.zeros((SUB, LANES), jnp.float32)
    for slot in range(place.slots):
        tau = jnp.where(place.slot == slot, 1.0 - rate[slot], tau)
    return tau


def looped(start, stop, step):
    def run(x, carried):
        step(x)
        return carried

    lax.fori_loop(start, stop, run, 0, unroll=UNROLL)


UNROLL = 4


def small_copies(hbm_refs, refs, sems):
    copies = [pltpu.make_async_copy(src, dst, sems.at[at]) for at, (src, dst) in enumerate(zip(hbm_refs, refs))]
    for copy in copies:
        copy.start()
    return copies


def first_kernel(
    pop_hbm, flags_hbm, nbr_hbm, rate_hbm, mom_out, msg_even, msg_odd,
    raw, still, moved, flags, nbr, rate, small_sems, sides, sems,
):
    slots = nbr.shape[0]
    place = Place(slots)
    small = small_copies((nbr_hbm, rate_hbm, flags_hbm), (nbr, rate, flags), small_sems)
    parts = [pl.ds(first, GROUP) for first in range(0, EDGE, GROUP)]
    copies = [pltpu.make_async_copy(pop_hbm.at[:, part], raw.at[:, part], sems.at[at]) for at, part in enumerate(parts)]
    for copy in copies:
        copy.start()
    for copy in small:
        copy.wait()
    maps = plane_maps(place, nbr)
    tau = tau_plane(place, rate)
    depth = place.depth

    def collide(x):
        h = collided_from(moments([raw[num, x] for num in range(19)]), tau)
        kept = store_collided(place, maps, still, moved, x, h, flags[x] > 0)
        for at in range(5):
            pltpu.store(sides.at[0, N_MOM + at], turned(kept[UPWARD[at]], x - (EDGE - 1)), mask=depth == x)
            pltpu.store(sides.at[1, N_MOM + at], turned(kept[DOWNWARD[at]], x), mask=depth == x)

    for at, copy in enumerate(copies):
        copy.wait()
        looped(at * GROUP, (at + 1) * GROUP, collide)
    store_rims(place, maps, still, moved)
    keep = {1: depth != 0, -1: depth != EDGE - 1}

    def stream(x):
        g = [still[0, x]]
        for num in range(1, 19):
            value = moved[num, x + 1 - C[num][0]]
            value = jnp.where(value < LIMIT, value, still[OPP[num], x])
            if C[num][2]:
                value = jnp.where(keep[C[num][2]], value, 0.0)
            g.append(value)
        mom = moments(g)
        for at in range(N_MOM):
            mom_out[at, x] = mom[at]
            pltpu.store(sides.at[0, at], turned(mom[at], x - (EDGE - 1)), mask=depth == x)
            pltpu.store(sides.at[1, at], turned(mom[at], x), mask=depth == x)

    looped(0, EDGE, stream)
    odd = lax.axis_index("dev") % 2 == 1
    for at in range(N_MSG):
        upper = tau if at == N_MSG - 1 else sides[0, at]
        lower = tau if at == N_MSG - 1 else sides[1, at]
        msg_even[at] = jnp.where(odd, lower, upper)
        msg_odd[at] = jnp.where(odd, upper, lower)


def second_kernel(
    pop_hbm, flags_hbm, nbr_hbm, rate_hbm, mom_in, msg_even, msg_odd, got_even, got_odd, out_hbm,
    raw, still, moved, flags, nbr, rate, small_sems, faces, sems, out_sems,
):
    slots = nbr.shape[0]
    place = Place(slots)
    small = small_copies((nbr_hbm, rate_hbm, flags_hbm), (nbr, rate, flags), small_sems)
    incoming = pltpu.make_async_copy(pop_hbm, raw, sems.at[0])
    incoming.start()
    for copy in small:
        copy.wait()
    maps = plane_maps(place, nbr)
    tau = tau_plane(place, rate)
    depth = place.depth
    odd = lax.axis_index("dev") % 2 == 1

    def upper_own(at):
        return jnp.where(odd, msg_odd[at], msg_even[at])

    def lower_own(at):
        return jnp.where(odd, msg_even[at], msg_odd[at])

    def upper_got(at):
        return jnp.where(odd, got_odd[at], got_even[at])

    def lower_got(at):
        return jnp.where(odd, got_even[at], got_odd[at])

    for side, sign in ((0, 1), (1, -1)):
        own_msg, got_msg = (upper_own, upper_got) if sign > 0 else (lower_own, lower_got)
        base = (sign + 1) * slots
        inward = DOWNWARD if sign > 0 else UPWARD
        upright = column_of(nbr, (0, 0, sign), slots)
        straight, back_straight = place.named(upright, base), place.naming(upright, base)
        own_out = [own_msg(N_MOM + at) for at in range(5)]
        got_in = [got_msg(N_MOM + at) for at in range(5)]
        leaving, corners = [], []
        for at, (cx, cy) in enumerate(FLAT):
            corner = back_corner = None
            if cx or cy:
                corner = place.named(column_of(nbr, (-cx, -cy, sign), slots), base)
                back_corner = place.naming(column_of(nbr, (cx, cy, sign), slots), base)
            corners.append(corner)
            mirror = FLAT.index((-cx, -cy))
            value = face_pull(place, got_in[at], (cx, cy), straight, corner)
            faces[side, at] = jnp.where(value < LIMIT, value, own_out[mirror])
            value = face_pull(place, own_out[at], (cx, cy), back_straight, back_corner)
            leaving.append(jnp.where(value < LIMIT, value, got_in[mirror]))
        mom = add_crossing([got_msg(at) for at in range(N_MOM)], leaving, float(sign))
        h = collided_from(mom, got_msg(N_MSG - 1), inward)
        for at, flat in enumerate(FLAT):
            value = jnp.where(got_in[0] < LIMIT, h[inward[at]], CLOSED)
            faces[side, 5 + at] = face_pull(place, value, flat, straight, corners[at])

    top, bottom = depth == EDGE - 1, depth == 0
    sign = jnp.where(bottom, 1.0, -1.0)

    def collide(x):
        crossing = []
        for at in range(5):
            value = jnp.where(top, turned(faces[0, at], EDGE - 1 - x), 0.0)
            crossing.append(jnp.where(bottom, turned(faces[1, at], -x), value))
        mom = add_crossing([mom_in[at, x] for at in range(N_MOM)], crossing, sign)
        store_collided(place, maps, still, moved, x, collided_from(mom, tau), flags[x] > 0)

    looped(0, EDGE, collide)
    store_rims(place, maps, still, moved)
    incoming.wait()

    def stream(x):
        fluid = flags[x] > 0
        for num in range(19):
            value = back = still[OPP[num], x]
            if num:
                cx, cy, cz = C[num]
                value = moved[num, x + 1 - cx]
                if cz > 0:
                    value = jnp.where(bottom, turned(faces[1, 5 + UPWARD.index(num)], -x), value)
                elif cz < 0:
                    value = jnp.where(top, turned(faces[0, 5 + DOWNWARD.index(num)], EDGE - 1 - x), value)
                value = jnp.where(value < LIMIT, value, back)
            raw[num, x] = jnp.where(fluid, value, raw[num, x])

    outs = []
    for at, first in enumerate(range(0, EDGE, GROUP)):
        looped(first, first + GROUP, stream)
        part = pl.ds(first, GROUP)
        outs.append(pltpu.make_async_copy(raw.at[:, part], out_hbm.at[:, part], out_sems.at[at]))
        outs[-1].start()
    for out in outs:
        out.wait()


def body(populations, fluid_flags, neighbours, relax_rate):
    slots, velocities, cells = populations.shape
    assert cells == EDGE**3 and 2 * slots == SUB and velocities == 19
    peers = lax.axis_size("dev")
    assert peers % 2 == 0
    tiles = cells // LANES
    view = (EDGE, SUB, LANES)
    pops = populations.transpose(1, 0, 2).reshape(19, slots, tiles, LANES).transpose(0, 2, 1, 3).reshape((19,) + view)
    flags = fluid_flags.reshape(slots, tiles, LANES).transpose(1, 0, 2).reshape(view)
    args = [pltpu.with_memory_space_constraint(arg, pltpu.HBM) for arg in (pops, flags, neighbours, relax_rate)]
    vmem = pl.BlockSpec(memory_space=pltpu.VMEM)
    hbm = pl.BlockSpec(memory_space=pltpu.HBM)
    face = (SUB, LANES)
    scratch = [
        pltpu.VMEM((19,) + view, jnp.float32),
        pltpu.VMEM((19,) + view, jnp.float32),
        pltpu.VMEM((19, EDGE + 2) + face, jnp.float32),
        pltpu.VMEM(view, jnp.int32),
        pltpu.SMEM(neighbours.shape, jnp.int32),
        pltpu.SMEM(relax_rate.shape, jnp.float32),
        pltpu.SemaphoreType.DMA((3,)),
    ]
    params = pltpu.CompilerParams(vmem_limit_bytes=16 * 2**20)
    message = pltpu.VMEM((N_MSG,) + face, jnp.float32)
    mom, msg_even, msg_odd = pl.pallas_call(
        first_kernel,
        out_shape=(pltpu.VMEM((N_MOM,) + view, jnp.float32), message, message),
        in_specs=[hbm] * 4,
        out_specs=(vmem, vmem, vmem),
        scratch_shapes=scratch + [
            pltpu.VMEM((2, N_MOM + 5) + face, jnp.float32),
            pltpu.SemaphoreType.DMA((EDGE // GROUP,)),
        ],
        compiler_params=params,
        name="collide_and_stream",
    )(*args)
    even_pairs = [(i, i ^ 1) for i in range(peers)]
    odd_pairs = [(i, (i + 1) % peers if i % 2 else (i - 1) % peers) for i in range(peers)]
    got_odd = lax.ppermute(msg_odd, "dev", odd_pairs)
    got_even = lax.ppermute(msg_even, "dev", even_pairs)
    out = pl.pallas_call(
        second_kernel,
        out_shape=jax.ShapeDtypeStruct(pops.shape, jnp.float32),
        in_specs=[hbm] * 4 + [vmem] * 5,
        out_specs=hbm,
        scratch_shapes=scratch + [
            pltpu.VMEM((2, 10) + face, jnp.float32),
            pltpu.SemaphoreType.DMA((1,)),
            pltpu.SemaphoreType.DMA((EDGE // GROUP,)),
        ],
        compiler_params=params,
        name="finish",
    )(*args, mom, msg_even, msg_odd, got_even, got_odd)
    out = out.reshape(19, tiles, slots, LANES).transpose(0, 2, 1, 3).reshape(19, slots, cells)
    return out.transpose(1, 0, 2)


def solution(mesh):
    placed = (
        P(("group", "dev"), None, None),
        P(("group", "dev"), None),
        P(("group", "dev"), None),
        P(("group", "dev")),
    )
    return jax.shard_map(
        body, mesh=mesh, in_specs=placed, out_specs=P(("group", "dev"), None, None), check_vma=False
    )
```

```python
import jax
import jax.numpy as jnp
from jax import lax
from jax.experimental import pallas as pl
from jax.experimental.pallas import tpu as pltpu
from jax.sharding import PartitionSpec as P

EDGE = 16
LANES = 128
SUB = 8
CLOSED = 1.0e30
LIMIT = 1.0e29
ARRIVING = 8
LEAVING = 4
STREAMED = 8
INNER = 8


def directions():
    listed = [(0, 0, 0)]
    for axis in range(3):
        for sign in (1, -1):
            vector = [0, 0, 0]
            vector[axis] = sign
            listed.append(tuple(vector))
    for one, two in ((0, 1), (0, 2), (1, 2)):
        for sign_one in (1, -1):
            for sign_two in (1, -1):
                vector = [0, 0, 0]
                vector[one] = sign_one
                vector[two] = sign_two
                listed.append(tuple(vector))
    return listed


C = directions()
INDEX = {vector: num for num, vector in enumerate(C)}
OPP = [INDEX[tuple(-part for part in vector)] for vector in C]
FLAT = ((0, 0), (1, 0), (-1, 0), (0, 1), (0, -1))
UPWARD = [INDEX[(a, b, 1)] for a, b in FLAT]
DOWNWARD = [INDEX[(a, b, -1)] for a, b in FLAT]
MAP_KEYS = [(cx, cy) for cx in (0, 1, -1) for cy in (0, 1, -1) if cx or cy]
N_MOM = 9
N_MSG = N_MOM + 5 + 1


def column(vector):
    return INDEX[vector] - 1


def moments(g):
    sx, dx = g[1] + g[2], g[1] - g[2]
    sy, dy = g[3] + g[4], g[3] - g[4]
    sz, dz = g[5] + g[6], g[5] - g[6]
    pairs = []
    for base in (7, 11, 15):
        pairs.append((g[base] + g[base + 3], g[base] - g[base + 3], g[base + 1] + g[base + 2], g[base + 1] - g[base + 2]))
    (xys, xyd, xyt, xye), (xzs, xzd, xzt, xze), (yzs, yzd, yzt, yze) = pairs
    exy, exz, eyz = xys + xyt, xzs + xzt, yzs + yzt
    rho = g[0] * (1.0 / 3.0) + (sx + sy + sz) * (1.0 / 18.0) + (exy + exz + eyz) * (1.0 / 36.0)
    ux = dx * (1.0 / 6.0) + (xyd + xye + xzd + xze) * (1.0 / 12.0)
    uy = dy * (1.0 / 6.0) + (xyd - xye + yzd + yze) * (1.0 / 12.0)
    uz = dz * (1.0 / 6.0) + (xzd - xze + yzd - yze) * (1.0 / 12.0)
    qxy = (xys - xyt) * 0.25
    qxz = (xzs - xzt) * 0.25
    qyz = (yzs - yzt) * 0.25
    gxz = (sx - sz) * 0.5 + (exy - eyz) * 0.25
    gyz = (sy - sz) * 0.5 + (exy - exz) * 0.25
    return [rho, ux, uy, uz, qxy, qxz, qyz, gxz, gyz]


def add_crossing(mom, e, sign):
    ez, xp, xm, yp, ym = e
    rho, ux, uy, uz, qxy, qxz, qyz, gxz, gyz = mom
    xs, xd, ys, yd = xp + xm, xp - xm, yp + ym, yp - ym
    four = xs + ys
    half = ez * 0.5
    return [
        rho + ez * (1.0 / 18.0) + four * (1.0 / 36.0),
        ux + xd * (1.0 / 12.0),
        uy + yd * (1.0 / 12.0),
        uz + sign * (ez * (1.0 / 6.0) + four * (1.0 / 12.0)),
        qxy,
        qxz + (sign * 0.25) * xd,
        qyz + (sign * 0.25) * yd,
        gxz - ys * 0.25 - half,
        gyz - xs * 0.25 - half,
    ]


def collided_from(mom, tau, wanted=range(19)):
    rho, ux, uy, uz, qxy, qxz, qyz, gxz, gyz = mom
    xx, yy, zz = ux * ux, uy * uy, uz * uz
    base = rho - (xx + yy + zz) * (1.0 / 6.0)
    hx = gxz - (xx - zz)
    hy = gyz - (yy - zz)
    third = tau * (1.0 / 3.0)
    shear = {
        (0,): third * (hx + hx - hy),
        (1,): third * (hy + hy - hx),
        (2,): -third * (hx + hy),
        (0, 1): tau * (qxy - ux * uy),
        (0, 2): tau * (qxz - ux * uz),
        (1, 2): tau * (qyz - uy * uz),
    }
    u = (ux, uy, uz)
    out = {0: base}
    for num in wanted:
        if num in out:
            continue
        vector = C[num]
        axes = tuple(axis for axis in range(3) if vector[axis])
        if len(axes) == 1:
            speed = u[axes[0]]
            lead = vector[axes[0]]
            even = base + speed * speed * 0.5 + shear[axes]
        else:
            first, second = vector[axes[0]], vector[axes[1]]
            speed = u[axes[0]] + u[axes[1]] if first == second else u[axes[0]] - u[axes[1]]
            lead = first
            even = base + speed * speed * 0.5
            even = even + shear[axes] if first == second else even - shear[axes]
        plus = num if lead > 0 else OPP[num]
        out[plus] = even + speed
        out[OPP[plus]] = even - speed
    return out


def turned(value, shift):
    if isinstance(shift, int):
        shift = shift % LANES
        return value if shift == 0 else pltpu.roll(value, shift, 1)
    return pltpu.roll(value, (shift + LANES) % LANES, 1)


def picked(value, source):
    moved = jnp.take_along_axis(value, jnp.maximum(source, 0), axis=0)
    return jnp.where(source >= 0, moved, CLOSED)


class Place:
    def __init__(self, slots):
        self.slots = slots
        self.lane = lax.broadcasted_iota(jnp.int32, (SUB, LANES), 1)
        sub = lax.broadcasted_iota(jnp.int32, (SUB, LANES), 0)
        self.slot = sub % slots
        self.high = sub // slots
        self.depth = self.lane % EDGE

    def carry(self, cy):
        return self.lane >= LANES - EDGE if cy > 0 else self.lane < EDGE

    def named(self, entries, base):
        found = jnp.full((SUB, LANES), -1, jnp.int32)
        for slot, entry in enumerate(entries):
            found = jnp.where(self.slot == slot, jnp.where(entry >= 0, entry - base, -1), found)
        return found

    def naming(self, entries, base):
        found = jnp.full((SUB, LANES), -1, jnp.int32)
        for slot, entry in enumerate(entries):
            found = jnp.where(self.slot == entry - base, slot, found)
        return found

    def straight(self, found):
        return jnp.where(found >= 0, self.high * self.slots + found, -1)

    def across(self, same, corner, cy):
        inner = self.high == (1 if cy > 0 else 0)
        found = jnp.where(inner, same, corner)
        return jnp.where(found >= 0, (1 - self.high) * self.slots + found, -1)


def column_of(nbr, vector, slots):
    return [nbr[slot, column(vector)] for slot in range(slots)]


def plane_maps(place, nbr):
    slots = place.slots
    maps = {}
    for cx in (1, -1):
        side = place.named(column_of(nbr, (-cx, 0, 0), slots), slots)
        maps[cx, 0] = place.straight(side)
        for cy in (1, -1):
            corner = place.named(column_of(nbr, (-cx, -cy, 0), slots), slots)
            maps[cx, cy] = place.across(side, corner, cy)
    for cy in (1, -1):
        beside = place.named(column_of(nbr, (0, -cy, 0), slots), slots)
        maps[0, cy] = place.across(place.slot, beside, cy)
    return maps


def store_collided(place, maps, still, moved, x, h, fluid):
    kept = []
    for num in range(19):
        cx, cy, cz = C[num]
        value = jnp.where(fluid, h[num], CLOSED)
        kept.append(value)
        still[num, x] = value
        if num:
            if cy:
                value = jnp.where(place.carry(cy), picked(value, maps[0, cy]), value)
            moved[num, x + 1] = turned(value, EDGE * cy + cz)
    return kept


def store_rims(place, maps, still, moved):
    for num in range(1, 19):
        cx, cy, cz = C[num]
        if cx:
            source = still[num, EDGE - 1 if cx > 0 else 0]
            value = picked(source, maps[cx, 0])
            if cy:
                value = jnp.where(place.carry(cy), picked(source, maps[cx, cy]), value)
            moved[num, 0 if cx > 0 else EDGE + 1] = turned(value, EDGE * cy + cz)


def face_pull(place, plane, flat, straight, corner):
    cx, cy = flat
    value = picked(plane, straight)
    if cx:
        end = picked(plane, corner)
        return jnp.where(place.depth == (0 if cx > 0 else EDGE - 1), turned(end, cx - EDGE * cx), turned(value, cx))
    if cy:
        value = jnp.where(place.carry(cy), picked(plane, corner), value)
        return turned(value, EDGE * cy)
    return value


def face_shift(place, maps, plane, vector):
    cx, cy, _ = vector
    value = plane
    if cy:
        value = jnp.where(place.carry(cy), picked(plane, maps[0, cy]), plane)
    value = turned(value, cx + EDGE * cy)
    if cx:
        end = picked(plane, maps[cx, 0])
        if cy:
            end = jnp.where(place.carry(cy), picked(plane, maps[cx, cy]), end)
        end = turned(end, cx - EDGE * cx + EDGE * cy)
        value = jnp.where(place.depth == (0 if cx > 0 else EDGE - 1), end, value)
    return value


def tau_plane(place, rate):
    tau = jnp.zeros((SUB, LANES), jnp.float32)
    for slot in range(place.slots):
        tau = jnp.where(place.slot == slot, 1.0 - rate[slot], tau)
    return tau


def small_copies(hbm_refs, refs, sems):
    copies = [pltpu.make_async_copy(src, dst, sems.at[at]) for at, (src, dst) in enumerate(zip(hbm_refs, refs))]
    for copy in copies:
        copy.start()
    return copies


def looped(start, stop, step, unroll=1):
    def run(x, carried):
        step(x)
        return carried

    lax.fori_loop(start, stop, run, 0, unroll=unroll)


def first_kernel(
    pop_hbm, flags_hbm, nbr_hbm, rate_hbm, mom_out, msg_even, msg_odd, raw, flags, maps_out,
    still, moved, nbr, rate, small_sems, sides, sems,
):
    slots = nbr.shape[0]
    place = Place(slots)
    small = small_copies((nbr_hbm, rate_hbm, flags_hbm), (nbr, rate, flags), small_sems)

    def arrival(at):
        part = pl.ds(at * ARRIVING, ARRIVING)
        return pltpu.make_async_copy(pop_hbm.at[:, part], raw.at[:, part], sems.at[at])

    for at in range(EDGE // ARRIVING):
        arrival(at).start()
    for copy in small:
        copy.wait()
    maps = plane_maps(place, nbr)
    tau = tau_plane(place, rate)
    for at, key in enumerate(MAP_KEYS):
        maps_out[at] = maps[key]
    depth = place.depth

    def collide(x):
        h = collided_from(moments([raw[num, x] for num in range(19)]), tau)
        kept = store_collided(place, maps, still, moved, x, h, flags[x] > 0)
        for at in range(5):
            pltpu.store(sides.at[0, N_MOM + at], turned(kept[UPWARD[at]], x - (EDGE - 1)), mask=depth == x)
            pltpu.store(sides.at[1, N_MOM + at], turned(kept[DOWNWARD[at]], x), mask=depth == x)

    keep = {1: depth != 0, -1: depth != EDGE - 1}

    def stream(x):
        g = [still[0, x]]
        for num in range(1, 19):
            value = moved[num, x + 1 - C[num][0]]
            value = jnp.where(value < LIMIT, value, still[OPP[num], x])
            if C[num][2]:
                value = jnp.where(keep[C[num][2]], value, 0.0)
            g.append(value)
        mom = moments(g)
        for at in range(N_MOM):
            mom_out[at, x] = mom[at]
            pltpu.store(sides.at[0, at], turned(mom[at], x - (EDGE - 1)), mask=depth == x)
            pltpu.store(sides.at[1, at], turned(mom[at], x), mask=depth == x)

    def collide_arrived(at):
        arrival(at).wait()
        looped(0, ARRIVING, lambda part: collide(at * ARRIVING + part), ARRIVING)

    looped(0, EDGE // ARRIVING, collide_arrived)
    store_rims(place, maps, still, moved)
    looped(0, EDGE, stream, STREAMED)
    odd = lax.axis_index("dev") % 2 == 1
    for at in range(N_MSG):
        upper = tau if at == N_MSG - 1 else sides[0, at]
        lower = tau if at == N_MSG - 1 else sides[1, at]
        msg_even[at] = jnp.where(odd, lower, upper)
        msg_odd[at] = jnp.where(odd, upper, lower)


def interior_kernel(nbr_hbm, msg_even, mom_in, raw, flags, maps_in, res, packs, face_maps, still, moved, nbr, small_sems):
    slots = nbr.shape[0]
    place = Place(slots)
    small = small_copies((nbr_hbm,), (nbr,), small_sems)
    maps = {key: maps_in[at] for at, key in enumerate(MAP_KEYS)}
    depth = place.depth
    tau = msg_even[N_MSG - 1]
    def collide(x):
        h = collided_from([mom_in[at, x] for at in range(N_MOM)], tau)
        store_collided(place, maps, still, moved, x, h, flags[x] > 0)

    def stream(x):
        fluid = flags[x] > 0
        for num in range(19):
            value = back = still[OPP[num], x]
            if num:
                cx, cy, cz = C[num]
                value = moved[num, x + 1 - cx]
                if cz > 0:
                    pltpu.store(packs.at[0, UPWARD.index(num)], turned(value, x - (EDGE - 1)), mask=depth == x)
                if cz < 0:
                    pltpu.store(packs.at[1, DOWNWARD.index(num)], turned(value, x), mask=depth == x)
                value = jnp.where(value < LIMIT, value, back)
                if cz > 0:
                    pltpu.store(packs.at[1, 5 + UPWARD.index(num)], turned(value, x - 1), mask=depth == x)
                if cz < 0:
                    pltpu.store(packs.at[0, 5 + DOWNWARD.index(num)], turned(value, x - (EDGE - 2)), mask=depth == x)
            res[num, x] = jnp.where(fluid, value, raw[num, x])

    looped(0, EDGE, collide, INNER)
    store_rims(place, maps, still, moved)
    looped(0, EDGE, stream, INNER)
    small[0].wait()
    for side, sign in ((0, 1), (1, -1)):
        base = (sign + 1) * slots
        upright = column_of(nbr, (0, 0, sign), slots)
        straight, back = place.named(upright, base), place.naming(upright, base)
        face_maps[side, 0] = place.straight(straight)
        face_maps[side, 5] = place.straight(back)
        for at, (cx, cy) in enumerate(FLAT):
            if at:
                corner = place.named(column_of(nbr, (-cx, -cy, sign), slots), base)
                far = place.naming(column_of(nbr, (cx, cy, sign), slots), base)
                face_maps[side, at] = place.straight(corner) if cx else place.across(straight, corner, cy)
                face_maps[side, 5 + at] = place.straight(far) if cx else place.across(back, far, cy)


def last_kernel(
    msg_even, msg_odd, got_even, got_odd, flags, maps_in, res, packs, face_maps, out_hbm,
    raw, layers, out_sems,
):
    place = Place(SUB // 2)
    maps = {key: maps_in[at] for at, key in enumerate(MAP_KEYS)}
    depth = place.depth
    odd = lax.axis_index("dev") % 2 == 1
    tau = msg_even[N_MSG - 1]

    def upper_own(at):
        return jnp.where(odd, msg_odd[at], msg_even[at])

    def lower_own(at):
        return jnp.where(odd, msg_even[at], msg_odd[at])

    def upper_got(at):
        return jnp.where(odd, got_odd[at], got_even[at])

    def lower_got(at):
        return jnp.where(odd, got_even[at], got_odd[at])

    def opened(value, back):
        return jnp.where(value < LIMIT, value, back)

    edges, nexts = {}, {}
    for side, sign in ((0, 1), (1, -1)):
        own_msg, got_msg = (upper_own, upper_got) if sign > 0 else (lower_own, lower_got)
        inward, outward = (DOWNWARD, UPWARD) if sign > 0 else (UPWARD, DOWNWARD)
        own_out = [own_msg(N_MOM + at) for at in range(5)]
        got_in = [got_msg(N_MOM + at) for at in range(5)]
        entering, leaving = [], []
        for at, flat in enumerate(FLAT):
            mirror = FLAT.index((-flat[0], -flat[1]))
            value = face_pull(place, got_in[at], flat, face_maps[side, 0], face_maps[side, at])
            entering.append(opened(value, own_out[mirror]))
            value = face_pull(place, own_out[at], flat, face_maps[side, 5], face_maps[side, 5 + at])
            leaving.append(opened(value, got_in[mirror]))
        far_mom = add_crossing([got_msg(at) for at in range(N_MOM)], leaving, float(sign))
        far = collided_from(far_mom, got_msg(N_MSG - 1), inward)
        mom = add_crossing([own_msg(at) for at in range(N_MOM)], entering, float(-sign))
        fluid = own_out[0] < LIMIT
        h = collided_from(mom, tau)
        h = [jnp.where(fluid, h[num], CLOSED) for num in range(19)]
        edges[side, 0] = h[0]
        for num in range(1, 19):
            if not C[num][2]:
                edges[side, num] = opened(face_shift(place, maps, h[num], C[num]), h[OPP[num]])
        for at, flat in enumerate(FLAT):
            value = jnp.where(got_in[0] < LIMIT, far[inward[at]], CLOSED)
            value = face_pull(place, value, flat, face_maps[side, 0], face_maps[side, at])
            edges[side, inward[at]] = opened(value, h[OPP[inward[at]]])
            edges[side, outward[at]] = opened(packs[side, at], h[OPP[outward[at]]])
            value = face_shift(place, maps, h[inward[at]], C[inward[at]])
            nexts[inward[at]] = opened(value, packs[side, 5 + at])

    phase = depth % 4
    for num in range(19):
        bottom = edges[1, num]
        top = turned(edges[0, num], EDGE - 1)
        extra = None
        if C[num][2] > 0:
            extra, offset = turned(nexts[num], 1), 1
        elif C[num][2] < 0:
            extra, offset = turned(nexts[num], EDGE - 2), 2
        for r in range(4):
            value = jnp.where(phase == r, bottom, top)
            if extra is not None:
                value = jnp.where(phase == (r + offset) % 4, extra, value)
            layers[num, r] = value

    ends = (depth == 0) | (depth == EDGE - 1)
    lanes = {0: ends, 1: ends | (depth == 1), -1: ends | (depth == EDGE - 2)}

    def departure(at):
        part = pl.ds(at * LEAVING, LEAVING)
        return pltpu.make_async_copy(raw.at[:, part], out_hbm.at[:, part], out_sems.at[at])

    def leave(at):
        for part in range(LEAVING):
            x = at * LEAVING + part
            fluid = flags[x] > 0
            for num in range(19):
                value = turned(layers[num, part % 4], -x)
                raw[num, x] = jnp.where(fluid & lanes[C[num][2]], value, res[num, x])
        departure(at).start()

    looped(0, EDGE // LEAVING, leave)
    looped(0, EDGE // LEAVING, lambda at: departure(at).wait())


def body(populations, fluid_flags, neighbours, relax_rate):
    slots, velocities, cells = populations.shape
    assert cells == EDGE**3 and 2 * slots == SUB and velocities == 19
    peers = lax.axis_size("dev")
    assert peers % 2 == 0
    tiles = cells // LANES
    view = (EDGE, SUB, LANES)
    pops = populations.transpose(1, 0, 2).reshape(19, slots, tiles, LANES).transpose(0, 2, 1, 3).reshape((19,) + view)
    flags = fluid_flags.reshape(slots, tiles, LANES).transpose(1, 0, 2).reshape(view)
    pops, flags, neighbours, relax_rate = [
        pltpu.with_memory_space_constraint(arg, pltpu.HBM) for arg in (pops, flags, neighbours, relax_rate)
    ]
    vmem = pl.BlockSpec(memory_space=pltpu.VMEM)
    hbm = pl.BlockSpec(memory_space=pltpu.HBM)
    face = (SUB, LANES)
    still = pltpu.VMEM((19,) + view, jnp.float32)
    moved = pltpu.VMEM((19, EDGE + 2) + face, jnp.float32)
    nbr = pltpu.SMEM(neighbours.shape, jnp.int32)
    rate = pltpu.SMEM(relax_rate.shape, jnp.float32)
    dma = pltpu.SemaphoreType.DMA
    params = pltpu.CompilerParams(vmem_limit_bytes=16 * 2**20)
    message = pltpu.VMEM((N_MSG,) + face, jnp.float32)
    mom, msg_even, msg_odd, raw, flags_here, maps = pl.pallas_call(
        first_kernel,
        out_shape=(
            pltpu.VMEM((N_MOM,) + view, jnp.float32), message, message,
            pltpu.VMEM((19,) + view, jnp.float32), pltpu.VMEM(view, jnp.int32),
            pltpu.VMEM((len(MAP_KEYS),) + face, jnp.int32),
        ),
        in_specs=[hbm] * 4,
        out_specs=(vmem,) * 6,
        scratch_shapes=[
            still, moved, nbr, rate, dma((3,)),
            pltpu.VMEM((2, N_MOM + 5) + face, jnp.float32), dma((EDGE // ARRIVING,)),
        ],
        compiler_params=params,
        name="collide_and_stream",
    )(pops, flags, neighbours, relax_rate)
    even_pairs = [(i, i ^ 1) for i in range(peers)]
    odd_pairs = [(i, (i + 1) % peers if i % 2 else (i - 1) % peers) for i in range(peers)]
    got_odd = lax.ppermute(msg_odd, "dev", odd_pairs)
    got_even = lax.ppermute(msg_even, "dev", even_pairs)
    res, packs, face_maps = pl.pallas_call(
        interior_kernel,
        out_shape=(
            pltpu.VMEM((19,) + view, jnp.float32),
            pltpu.VMEM((2, 10) + face, jnp.float32),
            pltpu.VMEM((2, 10) + face, jnp.int32),
        ),
        in_specs=[hbm] + [vmem] * 5,
        out_specs=(vmem,) * 3,
        scratch_shapes=[still, moved, nbr, dma((1,))],
        compiler_params=params,
        cost_estimate=pl.CostEstimate(flops=12_000_000, bytes_accessed=4_000_000, transcendentals=0),
        name="interior",
    )(neighbours, msg_even, mom, raw, flags_here, maps)
    out = pl.pallas_call(
        last_kernel,
        out_shape=jax.ShapeDtypeStruct(pops.shape, jnp.float32),
        in_specs=[vmem] * 9,
        out_specs=hbm,
        scratch_shapes=[
            pltpu.VMEM((19,) + view, jnp.float32), pltpu.VMEM((19, 4) + face, jnp.float32),
            dma((EDGE // LEAVING,)),
        ],
        compiler_params=params,
        name="finish",
    )(msg_even, msg_odd, got_even, got_odd, flags_here, maps, res, packs, face_maps)
    out = out.reshape(19, tiles, slots, LANES).transpose(0, 2, 1, 3).reshape(19, slots, cells)
    return out.transpose(1, 0, 2)


def solution(mesh):
    placed = (
        P(("group", "dev"), None, None),
        P(("group", "dev"), None),
        P(("group", "dev"), None),
        P(("group", "dev")),
    )
    return jax.shard_map(
        body, mesh=mesh, in_specs=placed, out_specs=P(("group", "dev"), None, None), check_vma=False
    )
```

```python
import jax
import jax.numpy as jnp
from jax import lax
from jax.experimental import pallas as pl
from jax.experimental.pallas import tpu as pltpu
from jax.sharding import PartitionSpec as P

EDGE = 16
LANES = 128
SUB = 8
CLOSED = 1.0e30
LIMIT = 1.0e29
ARRIVING = 8
LEAVING = 8
INNER = 8


def directions():
    listed = [(0, 0, 0)]
    for axis in range(3):
        for sign in (1, -1):
            vector = [0, 0, 0]
            vector[axis] = sign
            listed.append(tuple(vector))
    for one, two in ((0, 1), (0, 2), (1, 2)):
        for sign_one in (1, -1):
            for sign_two in (1, -1):
                vector = [0, 0, 0]
                vector[one] = sign_one
                vector[two] = sign_two
                listed.append(tuple(vector))
    return listed


C = directions()
INDEX = {vector: num for num, vector in enumerate(C)}
OPP = [INDEX[tuple(-part for part in vector)] for vector in C]
FLAT = ((0, 0), (1, 0), (-1, 0), (0, 1), (0, -1))
UPWARD = [INDEX[(a, b, 1)] for a, b in FLAT]
DOWNWARD = [INDEX[(a, b, -1)] for a, b in FLAT]
MAP_KEYS = [(cx, cy) for cx in (0, 1, -1) for cy in (0, 1, -1) if cx or cy]
N_MOM = 9
N_MSG = N_MOM + 5 + 1


def column(vector):
    return INDEX[vector] - 1


def moments(g):
    sx, dx = g[1] + g[2], g[1] - g[2]
    sy, dy = g[3] + g[4], g[3] - g[4]
    sz, dz = g[5] + g[6], g[5] - g[6]
    pairs = []
    for base in (7, 11, 15):
        pairs.append((g[base] + g[base + 3], g[base] - g[base + 3], g[base + 1] + g[base + 2], g[base + 1] - g[base + 2]))
    (xys, xyd, xyt, xye), (xzs, xzd, xzt, xze), (yzs, yzd, yzt, yze) = pairs
    exy, exz, eyz = xys + xyt, xzs + xzt, yzs + yzt
    rho = g[0] * (1.0 / 3.0) + (sx + sy + sz) * (1.0 / 18.0) + (exy + exz + eyz) * (1.0 / 36.0)
    ux = dx * (1.0 / 6.0) + (xyd + xye + xzd + xze) * (1.0 / 12.0)
    uy = dy * (1.0 / 6.0) + (xyd - xye + yzd + yze) * (1.0 / 12.0)
    uz = dz * (1.0 / 6.0) + (xzd - xze + yzd - yze) * (1.0 / 12.0)
    qxy = (xys - xyt) * 0.25
    qxz = (xzs - xzt) * 0.25
    qyz = (yzs - yzt) * 0.25
    gxz = (sx - sz) * 0.5 + (exy - eyz) * 0.25
    gyz = (sy - sz) * 0.5 + (exy - exz) * 0.25
    return [rho, ux, uy, uz, qxy, qxz, qyz, gxz, gyz]


def add_crossing(mom, e, sign):
    ez, xp, xm, yp, ym = e
    rho, ux, uy, uz, qxy, qxz, qyz, gxz, gyz = mom
    xs, xd, ys, yd = xp + xm, xp - xm, yp + ym, yp - ym
    four = xs + ys
    half = ez * 0.5
    return [
        rho + ez * (1.0 / 18.0) + four * (1.0 / 36.0),
        ux + xd * (1.0 / 12.0),
        uy + yd * (1.0 / 12.0),
        uz + sign * (ez * (1.0 / 6.0) + four * (1.0 / 12.0)),
        qxy,
        qxz + (sign * 0.25) * xd,
        qyz + (sign * 0.25) * yd,
        gxz - ys * 0.25 - half,
        gyz - xs * 0.25 - half,
    ]


def collided_from(mom, tau, wanted=range(19)):
    rho, ux, uy, uz, qxy, qxz, qyz, gxz, gyz = mom
    xx, yy, zz = ux * ux, uy * uy, uz * uz
    base = rho - (xx + yy + zz) * (1.0 / 6.0)
    hx = gxz - (xx - zz)
    hy = gyz - (yy - zz)
    third = tau * (1.0 / 3.0)
    shear = {
        (0,): third * (hx + hx - hy),
        (1,): third * (hy + hy - hx),
        (2,): -third * (hx + hy),
        (0, 1): tau * (qxy - ux * uy),
        (0, 2): tau * (qxz - ux * uz),
        (1, 2): tau * (qyz - uy * uz),
    }
    u = (ux, uy, uz)
    out = {0: base}
    for num in wanted:
        if num in out:
            continue
        vector = C[num]
        axes = tuple(axis for axis in range(3) if vector[axis])
        if len(axes) == 1:
            speed = u[axes[0]]
            lead = vector[axes[0]]
            even = base + speed * speed * 0.5 + shear[axes]
        else:
            first, second = vector[axes[0]], vector[axes[1]]
            speed = u[axes[0]] + u[axes[1]] if first == second else u[axes[0]] - u[axes[1]]
            lead = first
            even = base + speed * speed * 0.5
            even = even + shear[axes] if first == second else even - shear[axes]
        plus = num if lead > 0 else OPP[num]
        out[plus] = even + speed
        out[OPP[plus]] = even - speed
    return out


def turned(value, shift):
    if isinstance(shift, int):
        shift = shift % LANES
        return value if shift == 0 else pltpu.roll(value, shift, 1)
    return pltpu.roll(value, (shift + LANES) % LANES, 1)


def picked(value, source):
    moved = jnp.take_along_axis(value, jnp.maximum(source, 0), axis=0)
    return jnp.where(source >= 0, moved, CLOSED)


def opened(value, back):
    return jnp.where(value < LIMIT, value, back)


class Place:
    def __init__(self, slots):
        self.slots = slots
        self.lane = lax.broadcasted_iota(jnp.int32, (SUB, LANES), 1)
        sub = lax.broadcasted_iota(jnp.int32, (SUB, LANES), 0)
        self.slot = sub % slots
        self.high = sub // slots
        self.depth = self.lane % EDGE

    def carry(self, cy):
        return self.lane >= LANES - EDGE if cy > 0 else self.lane < EDGE

    def named(self, entries, base):
        found = jnp.full((SUB, LANES), -1, jnp.int32)
        for slot, entry in enumerate(entries):
            found = jnp.where(self.slot == slot, jnp.where(entry >= 0, entry - base, -1), found)
        return found

    def naming(self, entries, base):
        found = jnp.full((SUB, LANES), -1, jnp.int32)
        for slot, entry in enumerate(entries):
            found = jnp.where(self.slot == entry - base, slot, found)
        return found

    def straight(self, found):
        return jnp.where(found >= 0, self.high * self.slots + found, -1)

    def across(self, same, corner, cy):
        inner = self.high == (1 if cy > 0 else 0)
        found = jnp.where(inner, same, corner)
        return jnp.where(found >= 0, (1 - self.high) * self.slots + found, -1)


def column_of(nbr, vector, slots):
    return [nbr[slot, column(vector)] for slot in range(slots)]


def plane_maps(place, nbr):
    slots = place.slots
    maps = {}
    for cx in (1, -1):
        side = place.named(column_of(nbr, (-cx, 0, 0), slots), slots)
        maps[cx, 0] = place.straight(side)
        for cy in (1, -1):
            corner = place.named(column_of(nbr, (-cx, -cy, 0), slots), slots)
            maps[cx, cy] = place.across(side, corner, cy)
    for cy in (1, -1):
        beside = place.named(column_of(nbr, (0, -cy, 0), slots), slots)
        maps[0, cy] = place.across(place.slot, beside, cy)
    return maps


def store_moved(place, maps, moved, x, kept):
    for num in range(1, 19):
        cx, cy, cz = C[num]
        value = kept[num]
        if cy:
            value = jnp.where(place.carry(cy), picked(value, maps[0, cy]), value)
        moved[num, x + 1] = turned(value, EDGE * cy + cz)


def store_still(still, x, h, fluid):
    kept = [jnp.where(fluid, h[num], CLOSED) for num in range(19)]
    for num in range(19):
        still[num, x] = kept[num]
    return kept


def store_rims(place, maps, still, moved):
    for num in range(1, 19):
        cx, cy, cz = C[num]
        if cx:
            source = still[num, EDGE - 1 if cx > 0 else 0]
            value = picked(source, maps[cx, 0])
            if cy:
                value = jnp.where(place.carry(cy), picked(source, maps[cx, cy]), value)
            moved[num, 0 if cx > 0 else EDGE + 1] = turned(value, EDGE * cy + cz)


def face_pull(place, plane, flat, straight, corner):
    cx, cy = flat
    value = picked(plane, straight)
    if cx:
        end = picked(plane, corner)
        return jnp.where(place.depth == (0 if cx > 0 else EDGE - 1), turned(end, cx - EDGE * cx), turned(value, cx))
    if cy:
        value = jnp.where(place.carry(cy), picked(plane, corner), value)
        return turned(value, EDGE * cy)
    return value


def face_shift(place, maps, plane, vector):
    cx, cy, _ = vector
    value = plane
    if cy:
        value = jnp.where(place.carry(cy), picked(plane, maps[0, cy]), plane)
    value = turned(value, cx + EDGE * cy)
    if cx:
        end = picked(plane, maps[cx, 0])
        if cy:
            end = jnp.where(place.carry(cy), picked(plane, maps[cx, cy]), end)
        end = turned(end, cx - EDGE * cx + EDGE * cy)
        value = jnp.where(place.depth == (0 if cx > 0 else EDGE - 1), end, value)
    return value


def unlayered(place, layers, num, z):
    phase = place.depth % 4
    value = layers[num, (0 - z) % 4]
    for at in range(1, 4):
        value = jnp.where(phase == at, layers[num, (at - z) % 4], value)
    return turned(value, -z)


def tau_plane(place, rate):
    tau = jnp.zeros((SUB, LANES), jnp.float32)
    for slot in range(place.slots):
        tau = jnp.where(place.slot == slot, 1.0 - rate[slot], tau)
    return tau


def small_copies(hbm_refs, refs, sems):
    copies = [pltpu.make_async_copy(src, dst, sems.at[at]) for at, (src, dst) in enumerate(zip(hbm_refs, refs))]
    for copy in copies:
        copy.start()
    return copies


def looped(start, stop, step, unroll=1):
    def run(x, carried):
        step(x)
        return carried

    lax.fori_loop(start, stop, run, 0, unroll=unroll)


def first_kernel(
    pop_hbm, flags_hbm, nbr_hbm, rate_hbm, still, msg_even, msg_odd, raw, flags, maps_out,
    nbr, rate, small_sems, layers, sems,
):
    slots = nbr.shape[0]
    place = Place(slots)
    small = small_copies((nbr_hbm, rate_hbm, flags_hbm), (nbr, rate, flags), small_sems)

    def arrival(at):
        part = pl.ds(at * ARRIVING, ARRIVING)
        return pltpu.make_async_copy(pop_hbm.at[:, part], raw.at[:, part], sems.at[at])

    for at in range(EDGE // ARRIVING):
        arrival(at).start()
    for copy in small:
        copy.wait()
    maps = plane_maps(place, nbr)
    tau = tau_plane(place, rate)
    for at, key in enumerate(MAP_KEYS):
        maps_out[at] = maps[key]
    depth = place.depth

    def collide(x, phase):
        h = collided_from(moments([raw[num, x] for num in range(19)]), tau)
        kept = store_still(still, x, h, flags[x] > 0)
        near = ((depth - x + 2) & (EDGE - 1)) < 4
        for num in range(19):
            pltpu.store(layers.at[num, phase], turned(kept[num], x), mask=near)

    def collide_arrived(at):
        arrival(at).wait()
        for part in range(ARRIVING):
            collide(at * ARRIVING + part, part % 4)

    looped(0, EDGE // ARRIVING, collide_arrived)
    messages = []
    for sign in (1, -1):
        inward, outward = (DOWNWARD, UPWARD) if sign > 0 else (UPWARD, DOWNWARD)
        face, within = (EDGE - 1, EDGE - 2) if sign > 0 else (0, 1)
        h = [unlayered(place, layers, num, face) for num in range(19)]
        g = [None] * 19
        g[0] = h[0]
        for num in range(1, 19):
            if num in inward:
                g[num] = jnp.zeros((SUB, LANES), jnp.float32)
                continue
            source = unlayered(place, layers, num, within) if num in outward else h[num]
            g[num] = opened(face_shift(place, maps, source, C[num]), h[OPP[num]])
        messages.append(moments(g) + [h[num] for num in outward] + [tau])
    odd = lax.axis_index("dev") % 2 == 1
    for at, (upper, lower) in enumerate(zip(*messages)):
        msg_even[at] = jnp.where(odd, lower, upper)
        msg_odd[at] = jnp.where(odd, upper, lower)


def interior_kernel(
    nbr_hbm, msg_even, first_still, raw, flags, maps_in, res, packs, face_maps,
    still, moved, first_moved, nbr, small_sems,
):
    slots = nbr.shape[0]
    place = Place(slots)
    small = small_copies((nbr_hbm,), (nbr,), small_sems)
    maps = {key: maps_in[at] for at, key in enumerate(MAP_KEYS)}
    depth = place.depth
    tau = msg_even[N_MSG - 1]
    keep = {1: depth != 0, -1: depth != EDGE - 1}

    def collide(x):
        g = [first_still[0, x]]
        for num in range(1, 19):
            value = opened(first_moved[num, x + 1 - C[num][0]], first_still[OPP[num], x])
            if C[num][2]:
                value = jnp.where(keep[C[num][2]], value, 0.0)
            g.append(value)
        h = collided_from(moments(g), tau)
        store_moved(place, maps, moved, x, store_still(still, x, h, flags[x] > 0))

    def move(x):
        store_moved(place, maps, first_moved, x, [first_still[num, x] for num in range(19)])

    def stream(x):
        fluid = flags[x] > 0
        for num in range(19):
            value = back = still[OPP[num], x]
            if num:
                cx, cy, cz = C[num]
                value = moved[num, x + 1 - cx]
                if cz > 0:
                    pltpu.store(packs.at[0, UPWARD.index(num)], turned(value, x - (EDGE - 1)), mask=depth == x)
                if cz < 0:
                    pltpu.store(packs.at[1, DOWNWARD.index(num)], turned(value, x), mask=depth == x)
                value = jnp.where(value < LIMIT, value, back)
                if cz > 0:
                    pltpu.store(packs.at[1, 5 + UPWARD.index(num)], turned(value, x - 1), mask=depth == x)
                if cz < 0:
                    pltpu.store(packs.at[0, 5 + DOWNWARD.index(num)], turned(value, x - (EDGE - 2)), mask=depth == x)
            res[num, x] = jnp.where(fluid, value, raw[num, x])

    looped(0, EDGE, move, INNER)
    store_rims(place, maps, first_still, first_moved)
    looped(0, EDGE, collide, INNER)
    store_rims(place, maps, still, moved)
    looped(0, EDGE, stream, INNER)
    small[0].wait()
    for side, sign in ((0, 1), (1, -1)):
        base = (sign + 1) * slots
        upright = column_of(nbr, (0, 0, sign), slots)
        straight, back = place.named(upright, base), place.naming(upright, base)
        face_maps[side, 0] = place.straight(straight)
        face_maps[side, 5] = place.straight(back)
        for at, (cx, cy) in enumerate(FLAT):
            if at:
                corner = place.named(column_of(nbr, (-cx, -cy, sign), slots), base)
                far = place.naming(column_of(nbr, (cx, cy, sign), slots), base)
                face_maps[side, at] = place.straight(corner) if cx else place.across(straight, corner, cy)
                face_maps[side, 5 + at] = place.straight(far) if cx else place.across(back, far, cy)


def last_kernel(
    msg_even, msg_odd, got_even, got_odd, flags, maps_in, res, packs, face_maps, out_hbm,
    raw, layers, out_sems,
):
    place = Place(SUB // 2)
    maps = {key: maps_in[at] for at, key in enumerate(MAP_KEYS)}
    depth = place.depth
    odd = lax.axis_index("dev") % 2 == 1
    tau = msg_even[N_MSG - 1]

    def upper_own(at):
        return jnp.where(odd, msg_odd[at], msg_even[at])

    def lower_own(at):
        return jnp.where(odd, msg_even[at], msg_odd[at])

    def upper_got(at):
        return jnp.where(odd, got_odd[at], got_even[at])

    def lower_got(at):
        return jnp.where(odd, got_even[at], got_odd[at])

    edges, nexts = {}, {}
    for side, sign in ((0, 1), (1, -1)):
        own_msg, got_msg = (upper_own, upper_got) if sign > 0 else (lower_own, lower_got)
        inward, outward = (DOWNWARD, UPWARD) if sign > 0 else (UPWARD, DOWNWARD)
        own_out = [own_msg(N_MOM + at) for at in range(5)]
        got_in = [got_msg(N_MOM + at) for at in range(5)]
        entering, leaving = [], []
        for at, flat in enumerate(FLAT):
            mirror = FLAT.index((-flat[0], -flat[1]))
            value = face_pull(place, got_in[at], flat, face_maps[side, 0], face_maps[side, at])
            entering.append(opened(value, own_out[mirror]))
            value = face_pull(place, own_out[at], flat, face_maps[side, 5], face_maps[side, 5 + at])
            leaving.append(opened(value, got_in[mirror]))
        far_mom = add_crossing([got_msg(at) for at in range(N_MOM)], leaving, float(sign))
        far = collided_from(far_mom, got_msg(N_MSG - 1), inward)
        mom = add_crossing([own_msg(at) for at in range(N_MOM)], entering, float(-sign))
        fluid = own_out[0] < LIMIT
        h = collided_from(mom, tau)
        h = [jnp.where(fluid, h[num], CLOSED) for num in range(19)]
        edges[side, 0] = h[0]
        for num in range(1, 19):
            if not C[num][2]:
                edges[side, num] = opened(face_shift(place, maps, h[num], C[num]), h[OPP[num]])
        for at, flat in enumerate(FLAT):
            value = jnp.where(got_in[0] < LIMIT, far[inward[at]], CLOSED)
            value = face_pull(place, value, flat, face_maps[side, 0], face_maps[side, at])
            edges[side, inward[at]] = opened(value, h[OPP[inward[at]]])
            edges[side, outward[at]] = opened(packs[side, at], h[OPP[outward[at]]])
            value = face_shift(place, maps, h[inward[at]], C[inward[at]])
            nexts[inward[at]] = opened(value, packs[side, 5 + at])

    phase = depth % 4
    for num in range(19):
        bottom = edges[1, num]
        top = turned(edges[0, num], EDGE - 1)
        extra = None
        if C[num][2] > 0:
            extra, offset = turned(nexts[num], 1), 1
        elif C[num][2] < 0:
            extra, offset = turned(nexts[num], EDGE - 2), 2
        for r in range(4):
            value = jnp.where(phase == r, bottom, top)
            if extra is not None:
                value = jnp.where(phase == (r + offset) % 4, extra, value)
            layers[num, r] = value

    ends = (depth == 0) | (depth == EDGE - 1)
    lanes = {0: ends, 1: ends | (depth == 1), -1: ends | (depth == EDGE - 2)}

    def departure(at):
        part = pl.ds(at * LEAVING, LEAVING)
        return pltpu.make_async_copy(raw.at[:, part], out_hbm.at[:, part], out_sems.at[at])

    def leave(at):
        for part in range(LEAVING):
            x = at * LEAVING + part
            fluid = flags[x] > 0
            for num in range(19):
                value = turned(layers[num, part % 4], -x)
                raw[num, x] = jnp.where(fluid & lanes[C[num][2]], value, res[num, x])
        departure(at).start()

    looped(0, EDGE // LEAVING, leave)
    looped(0, EDGE // LEAVING, lambda at: departure(at).wait())


def body(populations, fluid_flags, neighbours, relax_rate):
    slots, velocities, cells = populations.shape
    assert cells == EDGE**3 and 2 * slots == SUB and velocities == 19
    peers = lax.axis_size("dev")
    assert peers % 2 == 0
    tiles = cells // LANES
    view = (EDGE, SUB, LANES)
    pops = populations.transpose(1, 0, 2).reshape(19, slots, tiles, LANES).transpose(0, 2, 1, 3).reshape((19,) + view)
    flags = fluid_flags.reshape(slots, tiles, LANES).transpose(1, 0, 2).reshape(view)
    pops, flags, neighbours, relax_rate = [
        pltpu.with_memory_space_constraint(arg, pltpu.HBM) for arg in (pops, flags, neighbours, relax_rate)
    ]
    vmem = pl.BlockSpec(memory_space=pltpu.VMEM)
    hbm = pl.BlockSpec(memory_space=pltpu.HBM)
    face = (SUB, LANES)
    still = pltpu.VMEM((19,) + view, jnp.float32)
    moved = pltpu.VMEM((19, EDGE + 2) + face, jnp.float32)
    nbr = pltpu.SMEM(neighbours.shape, jnp.int32)
    rate = pltpu.SMEM(relax_rate.shape, jnp.float32)
    dma = pltpu.SemaphoreType.DMA
    params = pltpu.CompilerParams(vmem_limit_bytes=16 * 2**20)
    message = pltpu.VMEM((N_MSG,) + face, jnp.float32)
    first_still, msg_even, msg_odd, raw, flags_here, maps = pl.pallas_call(
        first_kernel,
        out_shape=(
            still, message, message, still, pltpu.VMEM(view, jnp.int32),
            pltpu.VMEM((len(MAP_KEYS),) + face, jnp.int32),
        ),
        in_specs=[hbm] * 4,
        out_specs=(vmem,) * 6,
        scratch_shapes=[
            nbr, rate, dma((3,)), pltpu.VMEM((19, 4) + face, jnp.float32), dma((EDGE // ARRIVING,)),
        ],
        compiler_params=params,
        name="collide_first",
    )(pops, flags, neighbours, relax_rate)
    even_pairs = [(i, i ^ 1) for i in range(peers)]
    odd_pairs = [(i, (i + 1) % peers if i % 2 else (i - 1) % peers) for i in range(peers)]
    got_odd = lax.ppermute(msg_odd, "dev", odd_pairs)
    got_even = lax.ppermute(msg_even, "dev", even_pairs)
    res, packs, face_maps = pl.pallas_call(
        interior_kernel,
        out_shape=(
            pltpu.VMEM((19,) + view, jnp.float32),
            pltpu.VMEM((2, 10) + face, jnp.float32),
            pltpu.VMEM((2, 10) + face, jnp.int32),
        ),
        in_specs=[hbm] + [vmem] * 5,
        out_specs=(vmem,) * 3,
        scratch_shapes=[still, moved, moved, nbr, dma((1,))],
        compiler_params=params,
        cost_estimate=pl.CostEstimate(flops=12_000_000, bytes_accessed=4_000_000, transcendentals=0),
        name="interior",
    )(neighbours, msg_even, first_still, raw, flags_here, maps)
    out = pl.pallas_call(
        last_kernel,
        out_shape=jax.ShapeDtypeStruct(pops.shape, jnp.float32),
        in_specs=[vmem] * 9,
        out_specs=hbm,
        scratch_shapes=[
            pltpu.VMEM((19,) + view, jnp.float32), pltpu.VMEM((19, 4) + face, jnp.float32),
            dma((EDGE // LEAVING,)),
        ],
        compiler_params=params,
        name="finish",
    )(msg_even, msg_odd, got_even, got_odd, flags_here, maps, res, packs, face_maps)
    out = out.reshape(19, tiles, slots, LANES).transpose(0, 2, 1, 3).reshape(19, slots, cells)
    return out.transpose(1, 0, 2)


def solution(mesh):
    placed = (
        P(("group", "dev"), None, None),
        P(("group", "dev"), None),
        P(("group", "dev"), None),
        P(("group", "dev")),
    )
    return jax.shard_map(
        body, mesh=mesh, in_specs=placed, out_specs=P(("group", "dev"), None, None), check_vma=False
    )
```

```python
import jax
import jax.numpy as jnp
from jax import lax
from jax.experimental import pallas as pl
from jax.experimental.pallas import tpu as pltpu
from jax.sharding import PartitionSpec as P

EDGE = 16
LANES = 128
SUB = 8
CLOSED = 1.0e30
LIMIT = 1.0e29
ARRIVING = 8
TRIP = 8
LEAVING = 8
INNER = 8


def directions():
    listed = [(0, 0, 0)]
    for axis in range(3):
        for sign in (1, -1):
            vector = [0, 0, 0]
            vector[axis] = sign
            listed.append(tuple(vector))
    for one, two in ((0, 1), (0, 2), (1, 2)):
        for sign_one in (1, -1):
            for sign_two in (1, -1):
                vector = [0, 0, 0]
                vector[one] = sign_one
                vector[two] = sign_two
                listed.append(tuple(vector))
    return listed


C = directions()
INDEX = {vector: num for num, vector in enumerate(C)}
OPP = [INDEX[tuple(-part for part in vector)] for vector in C]
FLAT = ((0, 0), (1, 0), (-1, 0), (0, 1), (0, -1))
UPWARD = [INDEX[(a, b, 1)] for a, b in FLAT]
DOWNWARD = [INDEX[(a, b, -1)] for a, b in FLAT]
MAP_KEYS = [(cx, cy) for cx in (0, 1, -1) for cy in (0, 1, -1) if cx or cy]
N_MOM = 9
SENT = (0, 1, 2, 3, 5, 6)
N_MSG = len(SENT) + 1 + 5 + 1


def column(vector):
    return INDEX[vector] - 1


def moments(g):
    sx, dx = g[1] + g[2], g[1] - g[2]
    sy, dy = g[3] + g[4], g[3] - g[4]
    sz, dz = g[5] + g[6], g[5] - g[6]
    pairs = []
    for base in (7, 11, 15):
        pairs.append((g[base] + g[base + 3], g[base] - g[base + 3], g[base + 1] + g[base + 2], g[base + 1] - g[base + 2]))
    (xys, xyd, xyt, xye), (xzs, xzd, xzt, xze), (yzs, yzd, yzt, yze) = pairs
    exy, exz, eyz = xys + xyt, xzs + xzt, yzs + yzt
    rho = g[0] * (1.0 / 3.0) + (sx + sy + sz) * (1.0 / 18.0) + (exy + exz + eyz) * (1.0 / 36.0)
    ux = dx * (1.0 / 6.0) + (xyd + xye + xzd + xze) * (1.0 / 12.0)
    uy = dy * (1.0 / 6.0) + (xyd - xye + yzd + yze) * (1.0 / 12.0)
    uz = dz * (1.0 / 6.0) + (xzd - xze + yzd - yze) * (1.0 / 12.0)
    qxy = (xys - xyt) * 0.25
    qxz = (xzs - xzt) * 0.25
    qyz = (yzs - yzt) * 0.25
    gxz = (sx - sz) * 0.5 + (exy - eyz) * 0.25
    gyz = (sy - sz) * 0.5 + (exy - exz) * 0.25
    return [rho, ux, uy, uz, qxy, qxz, qyz, gxz, gyz]


def add_crossing(mom, e, sign):
    ez, xp, xm, yp, ym = e
    rho, ux, uy, uz, qxy, qxz, qyz, gxz, gyz = mom
    xs, xd, ys, yd = xp + xm, xp - xm, yp + ym, yp - ym
    four = xs + ys
    half = ez * 0.5
    return [
        rho + ez * (1.0 / 18.0) + four * (1.0 / 36.0),
        ux + xd * (1.0 / 12.0),
        uy + yd * (1.0 / 12.0),
        uz + sign * (ez * (1.0 / 6.0) + four * (1.0 / 12.0)),
        qxy,
        qxz + (sign * 0.25) * xd,
        qyz + (sign * 0.25) * yd,
        gxz - ys * 0.25 - half,
        gyz - xs * 0.25 - half,
    ]


def collided_from(mom, tau, wanted=range(19)):
    rho, ux, uy, uz, qxy, qxz, qyz, gxz, gyz = mom
    xx, yy, zz = ux * ux, uy * uy, uz * uz
    base = rho - (xx + yy + zz) * (1.0 / 6.0)
    hx = gxz - (xx - zz)
    hy = gyz - (yy - zz)
    third = tau * (1.0 / 3.0)
    shear = {
        (0,): third * (hx + hx - hy),
        (1,): third * (hy + hy - hx),
        (2,): -third * (hx + hy),
        (0, 1): tau * (qxy - ux * uy),
        (0, 2): tau * (qxz - ux * uz),
        (1, 2): tau * (qyz - uy * uz),
    }
    u = (ux, uy, uz)
    out = {0: base}
    for num in wanted:
        if num in out:
            continue
        vector = C[num]
        axes = tuple(axis for axis in range(3) if vector[axis])
        if len(axes) == 1:
            speed = u[axes[0]]
            lead = vector[axes[0]]
            even = base + speed * speed * 0.5 + shear[axes]
        else:
            first, second = vector[axes[0]], vector[axes[1]]
            speed = u[axes[0]] + u[axes[1]] if first == second else u[axes[0]] - u[axes[1]]
            lead = first
            even = base + speed * speed * 0.5
            even = even + shear[axes] if first == second else even - shear[axes]
        plus = num if lead > 0 else OPP[num]
        out[plus] = even + speed
        out[OPP[plus]] = even - speed
    return out


def turned(value, shift):
    if isinstance(shift, int):
        shift = shift % LANES
        return value if shift == 0 else pltpu.roll(value, shift, 1)
    return pltpu.roll(value, (shift + LANES) % LANES, 1)


def picked(value, source):
    moved = jnp.take_along_axis(value, jnp.maximum(source, 0), axis=0)
    return jnp.where(source >= 0, moved, CLOSED)


def opened(value, back):
    return jnp.where(value < LIMIT, value, back)


class Place:
    def __init__(self, slots):
        self.slots = slots
        self.lane = lax.broadcasted_iota(jnp.int32, (SUB, LANES), 1)
        sub = lax.broadcasted_iota(jnp.int32, (SUB, LANES), 0)
        self.slot = sub % slots
        self.high = sub // slots
        self.depth = self.lane % EDGE

    def carry(self, cy):
        return self.lane >= LANES - EDGE if cy > 0 else self.lane < EDGE

    def named(self, entries, base):
        found = jnp.full((SUB, LANES), -1, jnp.int32)
        for slot, entry in enumerate(entries):
            found = jnp.where(self.slot == slot, jnp.where(entry >= 0, entry - base, -1), found)
        return found

    def naming(self, entries, base):
        found = jnp.full((SUB, LANES), -1, jnp.int32)
        for slot, entry in enumerate(entries):
            found = jnp.where(self.slot == entry - base, slot, found)
        return found

    def straight(self, found):
        return jnp.where(found >= 0, self.high * self.slots + found, -1)

    def across(self, same, corner, cy):
        inner = self.high == (1 if cy > 0 else 0)
        found = jnp.where(inner, same, corner)
        return jnp.where(found >= 0, (1 - self.high) * self.slots + found, -1)


def column_of(nbr, vector, slots):
    return [nbr[slot, column(vector)] for slot in range(slots)]


def plane_maps(place, nbr):
    slots = place.slots
    maps = {}
    for cx in (1, -1):
        side = place.named(column_of(nbr, (-cx, 0, 0), slots), slots)
        maps[cx, 0] = place.straight(side)
        for cy in (1, -1):
            corner = place.named(column_of(nbr, (-cx, -cy, 0), slots), slots)
            maps[cx, cy] = place.across(side, corner, cy)
    for cy in (1, -1):
        beside = place.named(column_of(nbr, (0, -cy, 0), slots), slots)
        maps[0, cy] = place.across(place.slot, beside, cy)
    return maps


def store_moved(place, maps, moved, x, kept):
    for num in range(1, 19):
        _, cy, cz = C[num]
        value = kept[num]
        if cy:
            value = jnp.where(place.carry(cy), picked(value, maps[0, cy]), value)
        moved[num, x + 1] = turned(value, EDGE * cy + cz)


def store_still(still, x, h, fluid):
    kept = [jnp.where(fluid, h[num], CLOSED) for num in range(19)]
    for num in range(19):
        still[num, x] = kept[num]
    return kept


def store_rims(place, maps, still, moved):
    for num in range(1, 19):
        cx, cy, cz = C[num]
        if cx:
            source = still[num, EDGE - 1 if cx > 0 else 0]
            value = picked(source, maps[cx, 0])
            if cy:
                value = jnp.where(place.carry(cy), picked(source, maps[cx, cy]), value)
            moved[num, 0 if cx > 0 else EDGE + 1] = turned(value, EDGE * cy + cz)


def face_pull(place, plane, flat, straight, corner):
    cx, cy = flat
    value = picked(plane, straight)
    if cx:
        end = picked(plane, corner)
        return jnp.where(place.depth == (0 if cx > 0 else EDGE - 1), turned(end, cx - EDGE * cx), turned(value, cx))
    if cy:
        value = jnp.where(place.carry(cy), picked(plane, corner), value)
        return turned(value, EDGE * cy)
    return value


def face_shift(place, maps, plane, vector):
    cx, cy, _ = vector
    value = plane
    if cy:
        value = jnp.where(place.carry(cy), picked(plane, maps[0, cy]), plane)
    value = turned(value, cx + EDGE * cy)
    if cx:
        end = picked(plane, maps[cx, 0])
        if cy:
            end = jnp.where(place.carry(cy), picked(plane, maps[cx, cy]), end)
        end = turned(end, cx - EDGE * cx + EDGE * cy)
        value = jnp.where(place.depth == (0 if cx > 0 else EDGE - 1), end, value)
    return value


def layers_of(num):
    cz = C[num][2]
    return (0, EDGE - 1) + ((EDGE - 2,) if cz > 0 else (1,) if cz < 0 else ())


LAYERS = [(num, z) for num in range(19) for z in layers_of(num)]


def tau_plane(place, rate):
    tau = jnp.zeros((SUB, LANES), jnp.float32)
    for slot in range(place.slots):
        tau = jnp.where(place.slot == slot, 1.0 - rate[slot], tau)
    return tau


def small_copies(hbm_refs, refs, sems):
    copies = [pltpu.make_async_copy(src, dst, sems.at[at]) for at, (src, dst) in enumerate(zip(hbm_refs, refs))]
    for copy in copies:
        copy.start()
    return copies


def looped(start, stop, step, unroll=1):
    def run(x, carried):
        step(x)
        return carried

    lax.fori_loop(start, stop, run, 0, unroll=unroll)


def first_kernel(
    pop_hbm, flags_hbm, nbr_hbm, rate_hbm, still, msg_even, msg_odd, raw, flags, maps_out, tau_out, sides,
    nbr, rate, small_sems, layers, sems,
):
    slots = nbr.shape[0]
    place = Place(slots)
    small = small_copies((nbr_hbm, rate_hbm, flags_hbm), (nbr, rate, flags), small_sems)

    def arrival(at):
        part = pl.ds(at * ARRIVING, ARRIVING)
        return pltpu.make_async_copy(pop_hbm.at[:, part], raw.at[:, part], sems.at[at])

    for at in range(EDGE // ARRIVING):
        arrival(at).start()
    for copy in small:
        copy.wait()
    maps = plane_maps(place, nbr)
    tau = tau_plane(place, rate)
    tau_out[...] = tau
    for at, key in enumerate(MAP_KEYS):
        maps_out[at] = maps[key]
    depth = place.depth

    def collide(x):
        h = collided_from(moments([raw[num, x] for num in range(19)]), tau)
        kept = store_still(still, x, h, flags[x] > 0)
        at_z = {z: depth == ((x + z) & (EDGE - 1)) for z in (0, 1, EDGE - 2, EDGE - 1)}
        for num in range(19):
            value = turned(kept[num], x)
            for z in layers_of(num):
                pltpu.store(layers.at[LAYERS.index((num, z))], value, mask=at_z[z])

    def collide_arrived(at):
        for part in range(TRIP):
            if part % ARRIVING == 0:
                arrival(at * (TRIP // ARRIVING) + part // ARRIVING).wait()
            collide(at * TRIP + part)

    looped(0, EDGE // TRIP, collide_arrived)
    messages = []
    for side, sign in ((0, 1), (1, -1)):
        inward, outward = (DOWNWARD, UPWARD) if sign > 0 else (UPWARD, DOWNWARD)
        face, within = (EDGE - 1, EDGE - 2) if sign > 0 else (0, 1)
        h = [turned(layers[LAYERS.index((num, face))], -face) for num in range(19)]
        g = [None] * 19
        g[0] = h[0]
        for num in range(1, 19):
            if num in inward:
                g[num] = jnp.zeros((SUB, LANES), jnp.float32)
                continue
            source = turned(layers[LAYERS.index((num, within))], -within) if num in outward else h[num]
            g[num] = opened(face_shift(place, maps, source, C[num]), h[OPP[num]])
        mom = moments(g)
        out = [h[num] for num in outward]
        for at, value in enumerate(mom + out):
            sides[side, at] = value
        messages.append([mom[at] for at in SENT] + [mom[7] + mom[8]] + out + [tau])
    odd = lax.axis_index("dev") % 2 == 1
    for at, (upper, lower) in enumerate(zip(*messages)):
        msg_even[at] = jnp.where(odd, lower, upper)
        msg_odd[at] = jnp.where(odd, upper, lower)


def interior_kernel(
    nbr_hbm, tau_in, sides, first_still, raw, flags, maps_in, res, packs, face_maps, pulls,
    still, moved, first_moved, layers, nbr, small_sems,
):
    slots = nbr.shape[0]
    place = Place(slots)
    small = small_copies((nbr_hbm,), (nbr,), small_sems)
    maps = {key: maps_in[at] for at, key in enumerate(MAP_KEYS)}
    depth = place.depth
    tau = tau_in[...]
    keep = {1: depth != 0, -1: depth != EDGE - 1}

    def collide(x):
        g = [first_still[0, x]]
        for num in range(1, 19):
            value = opened(first_moved[num, x + 1 - C[num][0]], first_still[OPP[num], x])
            if C[num][2]:
                value = jnp.where(keep[C[num][2]], value, 0.0)
            g.append(value)
        h = collided_from(moments(g), tau)
        store_moved(place, maps, moved, x, store_still(still, x, h, flags[x] > 0))

    def move(x):
        store_moved(place, maps, first_moved, x, [first_still[num, x] for num in range(19)])

    end = {1: depth == EDGE - 1, -1: depth == 0}

    def stream(x):
        fluid = flags[x] > 0
        near = {
            1: (depth == ((x + EDGE - 1) & (EDGE - 1))) | (depth == ((x + 1) & (EDGE - 1))),
            -1: (depth == x) | (depth == ((x + EDGE - 2) & (EDGE - 1))),
        }
        for num in range(19):
            value = back = still[OPP[num], x]
            if num:
                cx, _, cz = C[num]
                value = moved[num, x + 1 - cx]
                if cz:
                    value = jnp.where((value < LIMIT) | end[cz], value, back)
                    at = (UPWARD if cz > 0 else DOWNWARD).index(num)
                    part = lax.rem(x, 4)
                    pltpu.store(layers.at[(1 - cz) // 2, at, part], turned(value, x), mask=near[cz])
                else:
                    value = opened(value, back)
            res[num, x] = jnp.where(fluid, value, raw[num, x])

    looped(0, EDGE, move, INNER)
    store_rims(place, maps, first_still, first_moved)
    looped(0, EDGE, collide, INNER)
    store_rims(place, maps, still, moved)
    looped(0, EDGE, stream, INNER)
    small[0].wait()
    for side, sign in ((0, 1), (1, -1)):
        base = (sign + 1) * slots
        upright = column_of(nbr, (0, 0, sign), slots)
        straight, back = place.named(upright, base), place.naming(upright, base)
        face_maps[side, 0] = place.straight(straight)
        for at, (cx, cy) in enumerate(FLAT):
            if at:
                corner = place.named(column_of(nbr, (-cx, -cy, sign), slots), base)
                far = place.naming(column_of(nbr, (cx, cy, sign), slots), base)
                face_maps[side, at] = place.straight(corner) if cx else place.across(straight, corner, cy)
                own_far = place.straight(far) if cx else place.across(back, far, cy)
            pulls[side, at] = face_pull(place, sides[side, N_MOM + at], (cx, cy), place.straight(back), own_far if at else None)
    phase = depth % 4
    for way, picks in ((0, ((0, 0, EDGE - 1), (1, 5, 1))), (1, ((1, 0, 0), (0, 5, EDGE - 2)))):
        for at in range(5):
            for side, first, z in picks:
                value = layers[way, at, (0 - z) % 4]
                for step in range(1, 4):
                    value = jnp.where(phase == step, layers[way, at, (step - z) % 4], value)
                packs[side, first + at] = turned(value, -z)


def last_kernel(
    tau_in, sides, got_even, got_odd, flags, maps_in, res, packs, face_maps, pulls, out_hbm,
    raw, layers, out_sems,
):
    place = Place(SUB // 2)
    maps = {key: maps_in[at] for at, key in enumerate(MAP_KEYS)}
    depth = place.depth
    odd = lax.axis_index("dev") % 2 == 1
    tau = tau_in[...]

    def upper_got(at):
        return jnp.where(odd, got_odd[at], got_even[at])

    def lower_got(at):
        return jnp.where(odd, got_even[at], got_odd[at])

    edges, nexts = {}, {}
    for side, sign in ((0, 1), (1, -1)):
        got_msg = upper_got if sign > 0 else lower_got
        inward, outward = (DOWNWARD, UPWARD) if sign > 0 else (UPWARD, DOWNWARD)
        own_out = [sides[side, N_MOM + at] for at in range(5)]
        got_in = [got_msg(len(SENT) + 1 + at) for at in range(5)]
        entering, leaving = [], []
        for at, flat in enumerate(FLAT):
            mirror = FLAT.index((-flat[0], -flat[1]))
            value = face_pull(place, got_in[at], flat, face_maps[side, 0], face_maps[side, at])
            entering.append(opened(value, own_out[mirror]))
            leaving.append(opened(pulls[side, at], got_in[mirror]))
        zero = jnp.zeros((SUB, LANES), jnp.float32)
        got_mom = [zero] * N_MOM
        for at, which in enumerate(SENT + (7,)):
            got_mom[which] = got_msg(at)
        far = collided_from(add_crossing(got_mom, leaving, float(sign)), got_msg(N_MSG - 1), inward)
        mom = add_crossing([sides[side, at] for at in range(N_MOM)], entering, float(-sign))
        fluid = own_out[0] < LIMIT
        h = collided_from(mom, tau)
        h = [jnp.where(fluid, h[num], CLOSED) for num in range(19)]
        edges[side, 0] = h[0]
        for num in range(1, 19):
            if not C[num][2]:
                edges[side, num] = opened(face_shift(place, maps, h[num], C[num]), h[OPP[num]])
        for at, flat in enumerate(FLAT):
            value = jnp.where(got_in[0] < LIMIT, far[inward[at]], CLOSED)
            value = face_pull(place, value, flat, face_maps[side, 0], face_maps[side, at])
            edges[side, inward[at]] = opened(value, h[OPP[inward[at]]])
            edges[side, outward[at]] = opened(packs[side, at], h[OPP[outward[at]]])
            value = face_shift(place, maps, h[inward[at]], C[inward[at]])
            nexts[inward[at]] = opened(value, packs[side, 5 + at])

    phase = depth % 4
    for num in range(19):
        bottom = edges[1, num]
        top = turned(edges[0, num], EDGE - 1)
        extra = None
        if C[num][2] > 0:
            extra, offset = turned(nexts[num], 1), 1
        elif C[num][2] < 0:
            extra, offset = turned(nexts[num], EDGE - 2), 2
        for r in range(4):
            value = jnp.where(phase == r, bottom, top)
            if extra is not None:
                value = jnp.where(phase == (r + offset) % 4, extra, value)
            layers[num, r] = value

    ends = (depth == 0) | (depth == EDGE - 1)
    lanes = {0: ends, 1: ends | (depth == 1), -1: ends | (depth == EDGE - 2)}

    def departure(at):
        part = pl.ds(at * LEAVING, LEAVING)
        return pltpu.make_async_copy(raw.at[:, part], out_hbm.at[:, part], out_sems.at[at])

    def leave(at):
        for part in range(LEAVING):
            x = at * LEAVING + part
            fluid = flags[x] > 0
            for num in range(19):
                value = turned(layers[num, part % 4], -x)
                raw[num, x] = jnp.where(fluid & lanes[C[num][2]], value, res[num, x])
        departure(at).start()

    looped(0, EDGE // LEAVING, leave)
    looped(0, EDGE // LEAVING, lambda at: departure(at).wait())


def body(populations, fluid_flags, neighbours, relax_rate):
    slots, velocities, cells = populations.shape
    assert cells == EDGE**3 and 2 * slots == SUB and velocities == 19
    peers = lax.axis_size("dev")
    assert peers % 2 == 0
    tiles = cells // LANES
    view = (EDGE, SUB, LANES)
    pops = populations.transpose(1, 0, 2).reshape(19, slots, tiles, LANES).transpose(0, 2, 1, 3).reshape((19,) + view)
    flags = fluid_flags.reshape(slots, tiles, LANES).transpose(1, 0, 2).reshape(view)
    pops, flags, neighbours, relax_rate = [
        pltpu.with_memory_space_constraint(arg, pltpu.HBM) for arg in (pops, flags, neighbours, relax_rate)
    ]
    vmem = pl.BlockSpec(memory_space=pltpu.VMEM)
    hbm = pl.BlockSpec(memory_space=pltpu.HBM)
    face = (SUB, LANES)
    still = pltpu.VMEM((19,) + view, jnp.float32)
    moved = pltpu.VMEM((19, EDGE + 2) + face, jnp.float32)
    nbr = pltpu.SMEM(neighbours.shape, jnp.int32)
    rate = pltpu.SMEM(relax_rate.shape, jnp.float32)
    dma = pltpu.SemaphoreType.DMA
    params = pltpu.CompilerParams(vmem_limit_bytes=16 * 2**20)
    message = pltpu.VMEM((N_MSG,) + face, jnp.float32)
    plane = pltpu.VMEM(face, jnp.float32)
    first_still, msg_even, msg_odd, raw, flags_here, maps, tau, sides = pl.pallas_call(
        first_kernel,
        out_shape=(
            still, message, message, still, pltpu.VMEM(view, jnp.int32),
            pltpu.VMEM((len(MAP_KEYS),) + face, jnp.int32), plane, pltpu.VMEM((2, N_MOM + 5) + face, jnp.float32),
        ),
        in_specs=[hbm] * 4,
        out_specs=(vmem,) * 8,
        scratch_shapes=[
            nbr, rate, dma((3,)), pltpu.VMEM((len(LAYERS),) + face, jnp.float32), dma((EDGE // ARRIVING,)),
        ],
        compiler_params=params,
        name="collide_first",
    )(pops, flags, neighbours, relax_rate)
    even_pairs = [(i, i ^ 1) for i in range(peers)]
    groups = lax.axis_size("group")
    odd_pairs = []
    for i in range(groups * peers):
        group, dev = divmod(i, peers)
        to = dev + 1 if dev % 2 else dev - 1
        if 0 <= to < peers:
            odd_pairs.append((i, group * peers + to))
        elif groups % 2 == 0:
            odd_pairs.append((i, (group ^ 1) * peers + dev))
        else:
            odd_pairs.append((i, group * peers + to % peers))
    got_odd = lax.ppermute(msg_odd, ("group", "dev"), odd_pairs)
    got_even = lax.ppermute(msg_even, "dev", even_pairs)
    res, packs, face_maps, pulls = pl.pallas_call(
        interior_kernel,
        out_shape=(
            pltpu.VMEM((19,) + view, jnp.float32),
            pltpu.VMEM((2, 10) + face, jnp.float32),
            pltpu.VMEM((2, 5) + face, jnp.int32),
            pltpu.VMEM((2, 5) + face, jnp.float32),
        ),
        in_specs=[hbm] + [vmem] * 6,
        out_specs=(vmem,) * 4,
        scratch_shapes=[still, moved, moved, pltpu.VMEM((2, 5, 4) + face, jnp.float32), nbr, dma((1,))],
        compiler_params=params,
        cost_estimate=pl.CostEstimate(flops=12_000_000, bytes_accessed=4_000_000, transcendentals=0),
        name="interior",
    )(neighbours, tau, sides, first_still, raw, flags_here, maps)
    out = pl.pallas_call(
        last_kernel,
        out_shape=jax.ShapeDtypeStruct(pops.shape, jnp.float32),
        in_specs=[vmem] * 10,
        out_specs=hbm,
        scratch_shapes=[
            pltpu.VMEM((19,) + view, jnp.float32), pltpu.VMEM((19, 4) + face, jnp.float32),
            dma((EDGE // LEAVING,)),
        ],
        compiler_params=params,
        name="finish",
    )(tau, sides, got_even, got_odd, flags_here, maps, res, packs, face_maps, pulls)
    out = out.reshape(19, tiles, slots, LANES).transpose(0, 2, 1, 3).reshape(19, slots, cells)
    return out.transpose(1, 0, 2)


def solution(mesh):
    placed = (
        P(("group", "dev"), None, None),
        P(("group", "dev"), None),
        P(("group", "dev"), None),
        P(("group", "dev")),
    )
    return jax.shard_map(
        body, mesh=mesh, in_specs=placed, out_specs=P(("group", "dev"), None, None), check_vma=False
    )
```

```python
import jax
import jax.numpy as jnp
from jax import lax
from jax.experimental import pallas as pl
from jax.experimental.pallas import tpu as pltpu
from jax.sharding import PartitionSpec as P

EDGE = 16
LANES = 128
SUB = 8
CLOSED = 1.0e30
LIMIT = 1.0e29
ARRIVING = 8
TRIP = 8
LEAVING = 8
INNER = 8


def directions():
    listed = [(0, 0, 0)]
    for axis in range(3):
        for sign in (1, -1):
            vector = [0, 0, 0]
            vector[axis] = sign
            listed.append(tuple(vector))
    for one, two in ((0, 1), (0, 2), (1, 2)):
        for sign_one in (1, -1):
            for sign_two in (1, -1):
                vector = [0, 0, 0]
                vector[one] = sign_one
                vector[two] = sign_two
                listed.append(tuple(vector))
    return listed


C = directions()
INDEX = {vector: num for num, vector in enumerate(C)}
OPP = [INDEX[tuple(-part for part in vector)] for vector in C]
FLAT = ((0, 0), (1, 0), (-1, 0), (0, 1), (0, -1))
UPWARD = [INDEX[(a, b, 1)] for a, b in FLAT]
DOWNWARD = [INDEX[(a, b, -1)] for a, b in FLAT]
MAP_KEYS = [(cx, cy) for cx in (0, 1, -1) for cy in (0, 1, -1) if cx or cy]
N_MOM = 9
SENT = (0, 1, 2, 3, 5, 6)
N_MSG = len(SENT) + 1 + 5 + 1


def column(vector):
    return INDEX[vector] - 1


def moments(g):
    sx, dx = g[1] + g[2], g[1] - g[2]
    sy, dy = g[3] + g[4], g[3] - g[4]
    sz, dz = g[5] + g[6], g[5] - g[6]
    pairs = []
    for base in (7, 11, 15):
        pairs.append((g[base] + g[base + 3], g[base] - g[base + 3], g[base + 1] + g[base + 2], g[base + 1] - g[base + 2]))
    (xys, xyd, xyt, xye), (xzs, xzd, xzt, xze), (yzs, yzd, yzt, yze) = pairs
    exy, exz, eyz = xys + xyt, xzs + xzt, yzs + yzt
    rho = g[0] * (1.0 / 3.0) + (sx + sy + sz) * (1.0 / 18.0) + (exy + exz + eyz) * (1.0 / 36.0)
    ux = dx * (1.0 / 6.0) + (xyd + xye + xzd + xze) * (1.0 / 12.0)
    uy = dy * (1.0 / 6.0) + (xyd - xye + yzd + yze) * (1.0 / 12.0)
    uz = dz * (1.0 / 6.0) + (xzd - xze + yzd - yze) * (1.0 / 12.0)
    qxy = (xys - xyt) * 0.25
    qxz = (xzs - xzt) * 0.25
    qyz = (yzs - yzt) * 0.25
    gxz = (sx - sz) * 0.5 + (exy - eyz) * 0.25
    gyz = (sy - sz) * 0.5 + (exy - exz) * 0.25
    return [rho, ux, uy, uz, qxy, qxz, qyz, gxz, gyz]


def add_crossing(mom, e, sign):
    ez, xp, xm, yp, ym = e
    rho, ux, uy, uz, qxy, qxz, qyz, gxz, gyz = mom
    xs, xd, ys, yd = xp + xm, xp - xm, yp + ym, yp - ym
    four = xs + ys
    half = ez * 0.5
    return [
        rho + ez * (1.0 / 18.0) + four * (1.0 / 36.0),
        ux + xd * (1.0 / 12.0),
        uy + yd * (1.0 / 12.0),
        uz + sign * (ez * (1.0 / 6.0) + four * (1.0 / 12.0)),
        qxy,
        qxz + (sign * 0.25) * xd,
        qyz + (sign * 0.25) * yd,
        gxz - ys * 0.25 - half,
        gyz - xs * 0.25 - half,
    ]


def collided_from(mom, tau, wanted=range(19)):
    rho, ux, uy, uz, qxy, qxz, qyz, gxz, gyz = mom
    xx, yy, zz = ux * ux, uy * uy, uz * uz
    base = rho - (xx + yy + zz) * (1.0 / 6.0)
    hx = gxz - (xx - zz)
    hy = gyz - (yy - zz)
    third = tau * (1.0 / 3.0)
    shear = {
        (0,): third * (hx + hx - hy),
        (1,): third * (hy + hy - hx),
        (2,): -third * (hx + hy),
        (0, 1): tau * (qxy - ux * uy),
        (0, 2): tau * (qxz - ux * uz),
        (1, 2): tau * (qyz - uy * uz),
    }
    u = (ux, uy, uz)
    out = {0: base}
    for num in wanted:
        if num in out:
            continue
        vector = C[num]
        axes = tuple(axis for axis in range(3) if vector[axis])
        if len(axes) == 1:
            speed = u[axes[0]]
            lead = vector[axes[0]]
            even = base + speed * speed * 0.5 + shear[axes]
        else:
            first, second = vector[axes[0]], vector[axes[1]]
            speed = u[axes[0]] + u[axes[1]] if first == second else u[axes[0]] - u[axes[1]]
            lead = first
            even = base + speed * speed * 0.5
            even = even + shear[axes] if first == second else even - shear[axes]
        plus = num if lead > 0 else OPP[num]
        out[plus] = even + speed
        out[OPP[plus]] = even - speed
    return out


def turned(value, shift):
    if isinstance(shift, int):
        shift = shift % LANES
        return value if shift == 0 else pltpu.roll(value, shift, 1)
    return pltpu.roll(value, (shift + LANES) % LANES, 1)


def picked(value, source):
    moved = jnp.take_along_axis(value, jnp.maximum(source, 0), axis=0)
    return jnp.where(source >= 0, moved, CLOSED)


def opened(value, back):
    return jnp.where(value < LIMIT, value, back)


class Place:
    def __init__(self, slots):
        self.slots = slots
        self.lane = lax.broadcasted_iota(jnp.int32, (SUB, LANES), 1)
        sub = lax.broadcasted_iota(jnp.int32, (SUB, LANES), 0)
        self.slot = sub % slots
        self.high = sub // slots
        self.depth = self.lane % EDGE

    def carry(self, cy):
        return self.lane >= LANES - EDGE if cy > 0 else self.lane < EDGE

    def named(self, entries, base):
        found = jnp.full((SUB, LANES), -1, jnp.int32)
        for slot, entry in enumerate(entries):
            found = jnp.where(self.slot == slot, jnp.where(entry >= 0, entry - base, -1), found)
        return found

    def naming(self, entries, base):
        found = jnp.full((SUB, LANES), -1, jnp.int32)
        for slot, entry in enumerate(entries):
            found = jnp.where(self.slot == entry - base, slot, found)
        return found

    def straight(self, found):
        return jnp.where(found >= 0, self.high * self.slots + found, -1)

    def across(self, same, corner, cy):
        inner = self.high == (1 if cy > 0 else 0)
        found = jnp.where(inner, same, corner)
        return jnp.where(found >= 0, (1 - self.high) * self.slots + found, -1)


def column_of(nbr, vector, slots):
    return [nbr[slot, column(vector)] for slot in range(slots)]


def plane_maps(place, nbr):
    slots = place.slots
    maps = {}
    for cx in (1, -1):
        side = place.named(column_of(nbr, (-cx, 0, 0), slots), slots)
        maps[cx, 0] = place.straight(side)
        for cy in (1, -1):
            corner = place.named(column_of(nbr, (-cx, -cy, 0), slots), slots)
            maps[cx, cy] = place.across(side, corner, cy)
    for cy in (1, -1):
        beside = place.named(column_of(nbr, (0, -cy, 0), slots), slots)
        maps[0, cy] = place.across(place.slot, beside, cy)
    return maps


def store_moved(place, maps, moved, x, kept):
    for num in range(1, 19):
        _, cy, cz = C[num]
        value = kept[num]
        if cy:
            value = jnp.where(place.carry(cy), picked(value, maps[0, cy]), value)
        moved[num, x + 1] = turned(value, EDGE * cy + cz)


def store_still(still, x, h, fluid):
    kept = [jnp.where(fluid, h[num], CLOSED) for num in range(19)]
    for num in range(19):
        still[num, x] = kept[num]
    return kept


def store_rims(place, maps, still, moved):
    for num in range(1, 19):
        cx, cy, cz = C[num]
        if cx:
            source = still[num, EDGE - 1 if cx > 0 else 0]
            value = picked(source, maps[cx, 0])
            if cy:
                value = jnp.where(place.carry(cy), picked(source, maps[cx, cy]), value)
            moved[num, 0 if cx > 0 else EDGE + 1] = turned(value, EDGE * cy + cz)


def face_pull(place, plane, flat, straight, corner):
    cx, cy = flat
    value = picked(plane, straight)
    if cx:
        end = picked(plane, corner)
        return jnp.where(place.depth == (0 if cx > 0 else EDGE - 1), turned(end, cx - EDGE * cx), turned(value, cx))
    if cy:
        value = jnp.where(place.carry(cy), picked(plane, corner), value)
        return turned(value, EDGE * cy)
    return value


def face_shift(place, maps, plane, vector):
    cx, cy, _ = vector
    value = plane
    if cy:
        value = jnp.where(place.carry(cy), picked(plane, maps[0, cy]), plane)
    value = turned(value, cx + EDGE * cy)
    if cx:
        end = picked(plane, maps[cx, 0])
        if cy:
            end = jnp.where(place.carry(cy), picked(plane, maps[cx, cy]), end)
        end = turned(end, cx - EDGE * cx + EDGE * cy)
        value = jnp.where(place.depth == (0 if cx > 0 else EDGE - 1), end, value)
    return value


def layers_of(num):
    cz = C[num][2]
    return (0, EDGE - 1) + ((EDGE - 2,) if cz > 0 else (1,) if cz < 0 else ())


LAYERS = [(num, z) for num in range(19) for z in layers_of(num)]


def tau_plane(place, rate):
    tau = jnp.zeros((SUB, LANES), jnp.float32)
    for slot in range(place.slots):
        tau = jnp.where(place.slot == slot, 1.0 - rate[slot], tau)
    return tau


def small_copies(hbm_refs, refs, sems):
    copies = [pltpu.make_async_copy(src, dst, sems.at[at]) for at, (src, dst) in enumerate(zip(hbm_refs, refs))]
    for copy in copies:
        copy.start()
    return copies


def looped(start, stop, step, unroll=1):
    def run(x, carried):
        step(x)
        return carried

    lax.fori_loop(start, stop, run, 0, unroll=unroll)


def first_kernel(
    pop_hbm, flags_hbm, nbr_hbm, rate_hbm, still, msg_even, msg_odd, raw, flags, maps_out, tau_out, sides,
    nbr, rate, small_sems, layers, sems,
):
    slots = nbr.shape[0]
    place = Place(slots)
    small = small_copies((nbr_hbm, rate_hbm, flags_hbm), (nbr, rate, flags), small_sems)

    def arrival(at):
        part = pl.ds(at * ARRIVING, ARRIVING)
        return pltpu.make_async_copy(pop_hbm.at[:, part], raw.at[:, part], sems.at[at])

    for at in range(EDGE // ARRIVING):
        arrival(at).start()
    for copy in small:
        copy.wait()
    maps = plane_maps(place, nbr)
    tau = tau_plane(place, rate)
    tau_out[...] = tau
    for at, key in enumerate(MAP_KEYS):
        maps_out[at] = maps[key]
    depth = place.depth

    def collide(x):
        h = collided_from(moments([raw[num, x] for num in range(19)]), tau)
        kept = store_still(still, x, h, flags[x] > 0)
        at_z = {z: depth == ((x + z) & (EDGE - 1)) for z in (0, 1, EDGE - 2, EDGE - 1)}
        for num in range(19):
            value = turned(kept[num], x)
            for z in layers_of(num):
                pltpu.store(layers.at[LAYERS.index((num, z))], value, mask=at_z[z])

    def collide_arrived(at):
        for part in range(TRIP):
            if part % ARRIVING == 0:
                arrival(at * (TRIP // ARRIVING) + part // ARRIVING).wait()
            collide(at * TRIP + part)

    looped(0, EDGE // TRIP, collide_arrived)
    messages = []
    for side, sign in ((0, 1), (1, -1)):
        inward, outward = (DOWNWARD, UPWARD) if sign > 0 else (UPWARD, DOWNWARD)
        face, within = (EDGE - 1, EDGE - 2) if sign > 0 else (0, 1)
        h = [turned(layers[LAYERS.index((num, face))], -face) for num in range(19)]
        g = [None] * 19
        g[0] = h[0]
        for num in range(1, 19):
            if num in inward:
                g[num] = jnp.zeros((SUB, LANES), jnp.float32)
                continue
            source = turned(layers[LAYERS.index((num, within))], -within) if num in outward else h[num]
            g[num] = opened(face_shift(place, maps, source, C[num]), h[OPP[num]])
        mom = moments(g)
        out = [h[num] for num in outward]
        for at, value in enumerate(mom + out):
            sides[side, at] = value
        messages.append([mom[at] for at in SENT] + [mom[7] + mom[8]] + out + [tau])
    odd = lax.axis_index("dev") % 2 == 1
    for at, (upper, lower) in enumerate(zip(*messages)):
        msg_even[at] = jnp.where(odd, lower, upper)
        msg_odd[at] = jnp.where(odd, upper, lower)


def interior_kernel(
    nbr_hbm, tau_in, sides, first_still, raw, flags, maps_in, res, packs, face_maps, pulls,
    still, moved, first_moved, layers, nbr, small_sems,
):
    slots = nbr.shape[0]
    place = Place(slots)
    small = small_copies((nbr_hbm,), (nbr,), small_sems)
    maps = {key: maps_in[at] for at, key in enumerate(MAP_KEYS)}
    depth = place.depth
    tau = tau_in[...]
    keep = {1: depth != 0, -1: depth != EDGE - 1}

    def collide(x):
        g = [first_still[0, x]]
        for num in range(1, 19):
            value = opened(first_moved[num, x + 1 - C[num][0]], first_still[OPP[num], x])
            if C[num][2]:
                value = jnp.where(keep[C[num][2]], value, 0.0)
            g.append(value)
        h = collided_from(moments(g), tau)
        store_moved(place, maps, moved, x, store_still(still, x, h, flags[x] > 0))

    def move(x):
        store_moved(place, maps, first_moved, x, [first_still[num, x] for num in range(19)])

    end = {1: depth == EDGE - 1, -1: depth == 0}

    def stream(x):
        fluid = flags[x] > 0
        near = {
            1: (depth == ((x + EDGE - 1) & (EDGE - 1))) | (depth == ((x + 1) & (EDGE - 1))),
            -1: (depth == x) | (depth == ((x + EDGE - 2) & (EDGE - 1))),
        }
        for num in range(19):
            value = back = still[OPP[num], x]
            if num:
                cx, _, cz = C[num]
                value = moved[num, x + 1 - cx]
                if cz:
                    value = jnp.where((value < LIMIT) | end[cz], value, back)
                    at = (UPWARD if cz > 0 else DOWNWARD).index(num)
                    part = lax.rem(x, 4)
                    pltpu.store(layers.at[(1 - cz) // 2, at, part], turned(value, x), mask=near[cz])
                else:
                    value = opened(value, back)
            res[num, x] = jnp.where(fluid, value, raw[num, x])

    looped(0, EDGE, move, INNER)
    store_rims(place, maps, first_still, first_moved)
    looped(0, EDGE, collide, INNER)
    store_rims(place, maps, still, moved)
    looped(0, EDGE, stream, INNER)
    small[0].wait()
    for side, sign in ((0, 1), (1, -1)):
        base = (sign + 1) * slots
        upright = column_of(nbr, (0, 0, sign), slots)
        straight, back = place.named(upright, base), place.naming(upright, base)
        face_maps[side, 0] = place.straight(straight)
        for at, (cx, cy) in enumerate(FLAT):
            if at:
                corner = place.named(column_of(nbr, (-cx, -cy, sign), slots), base)
                far = place.naming(column_of(nbr, (cx, cy, sign), slots), base)
                face_maps[side, at] = place.straight(corner) if cx else place.across(straight, corner, cy)
                own_far = place.straight(far) if cx else place.across(back, far, cy)
            pulls[side, at] = face_pull(place, sides[side, N_MOM + at], (cx, cy), place.straight(back), own_far if at else None)
    phase = depth % 4
    for way, picks in ((0, ((0, 0, EDGE - 1), (1, 5, 1))), (1, ((1, 0, 0), (0, 5, EDGE - 2)))):
        for at in range(5):
            for side, first, z in picks:
                value = layers[way, at, (0 - z) % 4]
                for step in range(1, 4):
                    value = jnp.where(phase == step, layers[way, at, (step - z) % 4], value)
                packs[side, first + at] = turned(value, -z)


def last_kernel(
    tau_in, sides, got_even, got_odd, flags, maps_in, res, packs, face_maps, pulls, out_hbm,
    raw, layers, out_sems,
):
    place = Place(SUB // 2)
    maps = {key: maps_in[at] for at, key in enumerate(MAP_KEYS)}
    depth = place.depth
    odd = lax.axis_index("dev") % 2 == 1
    tau = tau_in[...]

    def upper_got(at):
        return jnp.where(odd, got_odd[at], got_even[at])

    def lower_got(at):
        return jnp.where(odd, got_even[at], got_odd[at])

    edges, nexts = {}, {}
    for side, sign in ((0, 1), (1, -1)):
        got_msg = upper_got if sign > 0 else lower_got
        inward, outward = (DOWNWARD, UPWARD) if sign > 0 else (UPWARD, DOWNWARD)
        own_out = [sides[side, N_MOM + at] for at in range(5)]
        got_in = [got_msg(len(SENT) + 1 + at) for at in range(5)]
        entering, leaving = [], []
        for at, flat in enumerate(FLAT):
            mirror = FLAT.index((-flat[0], -flat[1]))
            value = face_pull(place, got_in[at], flat, face_maps[side, 0], face_maps[side, at])
            entering.append(opened(value, own_out[mirror]))
            leaving.append(opened(pulls[side, at], got_in[mirror]))
        zero = jnp.zeros((SUB, LANES), jnp.float32)
        got_mom = [zero] * N_MOM
        for at, which in enumerate(SENT + (7,)):
            got_mom[which] = got_msg(at)
        far = collided_from(add_crossing(got_mom, leaving, float(sign)), got_msg(N_MSG - 1), inward)
        mom = add_crossing([sides[side, at] for at in range(N_MOM)], entering, float(-sign))
        fluid = own_out[0] < LIMIT
        h = collided_from(mom, tau)
        h = [jnp.where(fluid, h[num], CLOSED) for num in range(19)]
        edges[side, 0] = h[0]
        for num in range(1, 19):
            if not C[num][2]:
                edges[side, num] = opened(face_shift(place, maps, h[num], C[num]), h[OPP[num]])
        for at, flat in enumerate(FLAT):
            value = jnp.where(got_in[0] < LIMIT, far[inward[at]], CLOSED)
            value = face_pull(place, value, flat, face_maps[side, 0], face_maps[side, at])
            edges[side, inward[at]] = opened(value, h[OPP[inward[at]]])
            edges[side, outward[at]] = opened(packs[side, at], h[OPP[outward[at]]])
            value = face_shift(place, maps, h[inward[at]], C[inward[at]])
            nexts[inward[at]] = opened(value, packs[side, 5 + at])

    phase = depth % 4
    for num in range(19):
        bottom = edges[1, num]
        top = turned(edges[0, num], EDGE - 1)
        extra = None
        if C[num][2] > 0:
            extra, offset = turned(nexts[num], 1), 1
        elif C[num][2] < 0:
            extra, offset = turned(nexts[num], EDGE - 2), 2
        for r in range(4):
            value = jnp.where(phase == r, bottom, top)
            if extra is not None:
                value = jnp.where(phase == (r + offset) % 4, extra, value)
            layers[num, r] = value

    ends = (depth == 0) | (depth == EDGE - 1)
    lanes = {0: ends, 1: ends | (depth == 1), -1: ends | (depth == EDGE - 2)}

    def departure(at):
        part = pl.ds(at * LEAVING, LEAVING)
        return pltpu.make_async_copy(raw.at[:, part], out_hbm.at[:, part], out_sems.at[at])

    for at in range(EDGE // LEAVING):
        for x in range(at * LEAVING, (at + 1) * LEAVING):
            fluid = flags[x] > 0
            for num in range(19):
                value = turned(layers[num, x % 4], -x)
                raw[num, x] = jnp.where(fluid & lanes[C[num][2]], value, res[num, x])
        departure(at).start()
    looped(0, EDGE // LEAVING, lambda at: departure(at).wait())


def body(populations, fluid_flags, neighbours, relax_rate):
    slots, velocities, cells = populations.shape
    assert cells == EDGE**3 and 2 * slots == SUB and velocities == 19
    peers = lax.axis_size("dev")
    assert peers % 2 == 0
    tiles = cells // LANES
    view = (EDGE, SUB, LANES)
    pops = populations.transpose(1, 0, 2).reshape(19, slots, tiles, LANES).transpose(0, 2, 1, 3).reshape((19,) + view)
    flags = fluid_flags.reshape(slots, tiles, LANES).transpose(1, 0, 2).reshape(view)
    pops, flags, neighbours, relax_rate = [
        pltpu.with_memory_space_constraint(arg, pltpu.HBM) for arg in (pops, flags, neighbours, relax_rate)
    ]
    vmem = pl.BlockSpec(memory_space=pltpu.VMEM)
    hbm = pl.BlockSpec(memory_space=pltpu.HBM)
    face = (SUB, LANES)
    still = pltpu.VMEM((19,) + view, jnp.float32)
    moved = pltpu.VMEM((19, EDGE + 2) + face, jnp.float32)
    nbr = pltpu.SMEM(neighbours.shape, jnp.int32)
    rate = pltpu.SMEM(relax_rate.shape, jnp.float32)
    dma = pltpu.SemaphoreType.DMA
    params = pltpu.CompilerParams(vmem_limit_bytes=16 * 2**20)
    message = pltpu.VMEM((N_MSG,) + face, jnp.float32)
    plane = pltpu.VMEM(face, jnp.float32)
    first_still, msg_even, msg_odd, raw, flags_here, maps, tau, sides = pl.pallas_call(
        first_kernel,
        out_shape=(
            still, message, message, still, pltpu.VMEM(view, jnp.int32),
            pltpu.VMEM((len(MAP_KEYS),) + face, jnp.int32), plane, pltpu.VMEM((2, N_MOM + 5) + face, jnp.float32),
        ),
        in_specs=[hbm] * 4,
        out_specs=(vmem,) * 8,
        scratch_shapes=[
            nbr, rate, dma((3,)), pltpu.VMEM((len(LAYERS),) + face, jnp.float32), dma((EDGE // ARRIVING,)),
        ],
        compiler_params=params,
        name="collide_first",
    )(pops, flags, neighbours, relax_rate)
    even_pairs = [(i, i ^ 1) for i in range(peers)]
    groups = lax.axis_size("group")
    odd_pairs = []
    for i in range(groups * peers):
        group, dev = divmod(i, peers)
        to = dev + 1 if dev % 2 else dev - 1
        if 0 <= to < peers:
            odd_pairs.append((i, group * peers + to))
        elif groups % 2 == 0:
            odd_pairs.append((i, (group ^ 1) * peers + dev))
        else:
            odd_pairs.append((i, group * peers + to % peers))
    got_odd = lax.ppermute(msg_odd, ("group", "dev"), odd_pairs)
    got_even = lax.ppermute(msg_even, "dev", even_pairs)
    res, packs, face_maps, pulls = pl.pallas_call(
        interior_kernel,
        out_shape=(
            pltpu.VMEM((19,) + view, jnp.float32),
            pltpu.VMEM((2, 10) + face, jnp.float32),
            pltpu.VMEM((2, 5) + face, jnp.int32),
            pltpu.VMEM((2, 5) + face, jnp.float32),
        ),
        in_specs=[hbm] + [vmem] * 6,
        out_specs=(vmem,) * 4,
        scratch_shapes=[still, moved, moved, pltpu.VMEM((2, 5, 4) + face, jnp.float32), nbr, dma((1,))],
        compiler_params=params,
        cost_estimate=pl.CostEstimate(flops=12_000_000, bytes_accessed=4_000_000, transcendentals=0),
        name="interior",
    )(neighbours, tau, sides, first_still, raw, flags_here, maps)
    out = pl.pallas_call(
        last_kernel,
        out_shape=jax.ShapeDtypeStruct(pops.shape, jnp.float32),
        in_specs=[vmem] * 10,
        out_specs=hbm,
        scratch_shapes=[
            pltpu.VMEM((19,) + view, jnp.float32), pltpu.VMEM((19, 4) + face, jnp.float32),
            dma((EDGE // LEAVING,)),
        ],
        compiler_params=params,
        name="finish",
    )(tau, sides, got_even, got_odd, flags_here, maps, res, packs, face_maps, pulls)
    out = out.reshape(19, tiles, slots, LANES).transpose(0, 2, 1, 3).reshape(19, slots, cells)
    return out.transpose(1, 0, 2)


def solution(mesh):
    placed = (
        P(("group", "dev"), None, None),
        P(("group", "dev"), None),
        P(("group", "dev"), None),
        P(("group", "dev")),
    )
    return jax.shard_map(
        body, mesh=mesh, in_specs=placed, out_specs=P(("group", "dev"), None, None), check_vma=False
    )
```

```python
import jax
import jax.numpy as jnp
from jax import lax
from jax.experimental import pallas as pl
from jax.experimental.pallas import tpu as pltpu
from jax.sharding import PartitionSpec as P

EDGE = 16
LANES = 128
SUB = 8
CLOSED = 1.0e30
LIMIT = 1.0e29
ARRIVING = 8
TRIP = 8
LEAVING = 8
INNER = 8


def directions():
    listed = [(0, 0, 0)]
    for axis in range(3):
        for sign in (1, -1):
            vector = [0, 0, 0]
            vector[axis] = sign
            listed.append(tuple(vector))
    for one, two in ((0, 1), (0, 2), (1, 2)):
        for sign_one in (1, -1):
            for sign_two in (1, -1):
                vector = [0, 0, 0]
                vector[one] = sign_one
                vector[two] = sign_two
                listed.append(tuple(vector))
    return listed


C = directions()
INDEX = {vector: num for num, vector in enumerate(C)}
OPP = [INDEX[tuple(-part for part in vector)] for vector in C]
FLAT = ((0, 0), (1, 0), (-1, 0), (0, 1), (0, -1))
UPWARD = [INDEX[(a, b, 1)] for a, b in FLAT]
DOWNWARD = [INDEX[(a, b, -1)] for a, b in FLAT]
MAP_KEYS = [(cx, cy) for cx in (0, 1, -1) for cy in (0, 1, -1) if cx or cy]
N_MOM = 9
SENT = (0, 1, 2, 3, 5, 6)
N_MSG = len(SENT) + 1 + 5 + 1


def column(vector):
    return INDEX[vector] - 1


def moments(g):
    sx, dx = g[1] + g[2], g[1] - g[2]
    sy, dy = g[3] + g[4], g[3] - g[4]
    sz, dz = g[5] + g[6], g[5] - g[6]
    pairs = []
    for base in (7, 11, 15):
        pairs.append((g[base] + g[base + 3], g[base] - g[base + 3], g[base + 1] + g[base + 2], g[base + 1] - g[base + 2]))
    (xys, xyd, xyt, xye), (xzs, xzd, xzt, xze), (yzs, yzd, yzt, yze) = pairs
    exy, exz, eyz = xys + xyt, xzs + xzt, yzs + yzt
    rho = g[0] * (1.0 / 3.0) + (sx + sy + sz) * (1.0 / 18.0) + (exy + exz + eyz) * (1.0 / 36.0)
    ux = dx * (1.0 / 6.0) + (xyd + xye + xzd + xze) * (1.0 / 12.0)
    uy = dy * (1.0 / 6.0) + (xyd - xye + yzd + yze) * (1.0 / 12.0)
    uz = dz * (1.0 / 6.0) + (xzd - xze + yzd - yze) * (1.0 / 12.0)
    qxy = (xys - xyt) * 0.25
    qxz = (xzs - xzt) * 0.25
    qyz = (yzs - yzt) * 0.25
    gxz = (sx - sz) * 0.5 + (exy - eyz) * 0.25
    gyz = (sy - sz) * 0.5 + (exy - exz) * 0.25
    return [rho, ux, uy, uz, qxy, qxz, qyz, gxz, gyz]


def add_crossing(mom, e, sign):
    ez, xp, xm, yp, ym = e
    rho, ux, uy, uz, qxy, qxz, qyz, gxz, gyz = mom
    xs, xd, ys, yd = xp + xm, xp - xm, yp + ym, yp - ym
    four = xs + ys
    half = ez * 0.5
    return [
        rho + ez * (1.0 / 18.0) + four * (1.0 / 36.0),
        ux + xd * (1.0 / 12.0),
        uy + yd * (1.0 / 12.0),
        uz + sign * (ez * (1.0 / 6.0) + four * (1.0 / 12.0)),
        qxy,
        qxz + (sign * 0.25) * xd,
        qyz + (sign * 0.25) * yd,
        gxz - ys * 0.25 - half,
        gyz - xs * 0.25 - half,
    ]


def collided_from(mom, tau, wanted=range(19)):
    rho, ux, uy, uz, qxy, qxz, qyz, gxz, gyz = mom
    xx, yy, zz = ux * ux, uy * uy, uz * uz
    base = rho - (xx + yy + zz) * (1.0 / 6.0)
    hx = gxz - (xx - zz)
    hy = gyz - (yy - zz)
    third = tau * (1.0 / 3.0)
    shear = {
        (0,): third * (hx + hx - hy),
        (1,): third * (hy + hy - hx),
        (2,): -third * (hx + hy),
        (0, 1): tau * (qxy - ux * uy),
        (0, 2): tau * (qxz - ux * uz),
        (1, 2): tau * (qyz - uy * uz),
    }
    u = (ux, uy, uz)
    out = {0: base}
    for num in wanted:
        if num in out:
            continue
        vector = C[num]
        axes = tuple(axis for axis in range(3) if vector[axis])
        if len(axes) == 1:
            speed = u[axes[0]]
            lead = vector[axes[0]]
            even = base + speed * speed * 0.5 + shear[axes]
        else:
            first, second = vector[axes[0]], vector[axes[1]]
            speed = u[axes[0]] + u[axes[1]] if first == second else u[axes[0]] - u[axes[1]]
            lead = first
            even = base + speed * speed * 0.5
            even = even + shear[axes] if first == second else even - shear[axes]
        plus = num if lead > 0 else OPP[num]
        out[plus] = even + speed
        out[OPP[plus]] = even - speed
    return out


def turned(value, shift):
    if isinstance(shift, int):
        shift = shift % LANES
        return value if shift == 0 else pltpu.roll(value, shift, 1)
    return pltpu.roll(value, (shift + LANES) % LANES, 1)


def picked(value, source):
    moved = jnp.take_along_axis(value, jnp.maximum(source, 0), axis=0)
    return jnp.where(source >= 0, moved, CLOSED)


def opened(value, back):
    return jnp.where(value < LIMIT, value, back)


class Place:
    def __init__(self, slots):
        self.slots = slots
        self.lane = lax.broadcasted_iota(jnp.int32, (SUB, LANES), 1)
        sub = lax.broadcasted_iota(jnp.int32, (SUB, LANES), 0)
        self.slot = sub % slots
        self.high = sub // slots
        self.depth = self.lane % EDGE

    def carry(self, cy):
        return self.lane >= LANES - EDGE if cy > 0 else self.lane < EDGE

    def named(self, entries, base):
        found = jnp.full((SUB, LANES), -1, jnp.int32)
        for slot, entry in enumerate(entries):
            found = jnp.where(self.slot == slot, jnp.where(entry >= 0, entry - base, -1), found)
        return found

    def naming(self, entries, base):
        found = jnp.full((SUB, LANES), -1, jnp.int32)
        for slot, entry in enumerate(entries):
            found = jnp.where(self.slot == entry - base, slot, found)
        return found

    def straight(self, found):
        return jnp.where(found >= 0, self.high * self.slots + found, -1)

    def across(self, same, corner, cy):
        inner = self.high == (1 if cy > 0 else 0)
        found = jnp.where(inner, same, corner)
        return jnp.where(found >= 0, (1 - self.high) * self.slots + found, -1)


def column_of(nbr, vector, slots):
    return [nbr[slot, column(vector)] for slot in range(slots)]


def plane_maps(place, nbr):
    slots = place.slots
    maps = {}
    for cx in (1, -1):
        side = place.named(column_of(nbr, (-cx, 0, 0), slots), slots)
        maps[cx, 0] = place.straight(side)
        for cy in (1, -1):
            corner = place.named(column_of(nbr, (-cx, -cy, 0), slots), slots)
            maps[cx, cy] = place.across(side, corner, cy)
    for cy in (1, -1):
        beside = place.named(column_of(nbr, (0, -cy, 0), slots), slots)
        maps[0, cy] = place.across(place.slot, beside, cy)
    return maps


def store_moved(place, maps, moved, x, kept):
    for num in range(1, 19):
        _, cy, cz = C[num]
        value = kept[num]
        if cy:
            value = jnp.where(place.carry(cy), picked(value, maps[0, cy]), value)
        moved[num, x + 1] = turned(value, EDGE * cy + cz)


def store_still(still, x, h, fluid):
    kept = [jnp.where(fluid, h[num], CLOSED) for num in range(19)]
    for num in range(19):
        still[num, x] = kept[num]
    return kept


def store_rims(place, maps, still, moved):
    for num in range(1, 19):
        cx, cy, cz = C[num]
        if cx:
            source = still[num, EDGE - 1 if cx > 0 else 0]
            value = picked(source, maps[cx, 0])
            if cy:
                value = jnp.where(place.carry(cy), picked(source, maps[cx, cy]), value)
            moved[num, 0 if cx > 0 else EDGE + 1] = turned(value, EDGE * cy + cz)


def face_pull(place, plane, flat, straight, corner):
    cx, cy = flat
    value = picked(plane, straight)
    if cx:
        end = picked(plane, corner)
        return jnp.where(place.depth == (0 if cx > 0 else EDGE - 1), turned(end, cx - EDGE * cx), turned(value, cx))
    if cy:
        value = jnp.where(place.carry(cy), picked(plane, corner), value)
        return turned(value, EDGE * cy)
    return value


def face_shift(place, maps, plane, vector):
    cx, cy, _ = vector
    value = plane
    if cy:
        value = jnp.where(place.carry(cy), picked(plane, maps[0, cy]), plane)
    value = turned(value, cx + EDGE * cy)
    if cx:
        end = picked(plane, maps[cx, 0])
        if cy:
            end = jnp.where(place.carry(cy), picked(plane, maps[cx, cy]), end)
        end = turned(end, cx - EDGE * cx + EDGE * cy)
        value = jnp.where(place.depth == (0 if cx > 0 else EDGE - 1), end, value)
    return value


def layers_of(num):
    cz = C[num][2]
    return (0, EDGE - 1) + ((EDGE - 2,) if cz > 0 else (1,) if cz < 0 else ())


LAYERS = [(num, z) for num in range(19) for z in layers_of(num)]


def tau_plane(place, rate):
    tau = jnp.zeros((SUB, LANES), jnp.float32)
    for slot in range(place.slots):
        tau = jnp.where(place.slot == slot, 1.0 - rate[slot], tau)
    return tau


def small_copies(hbm_refs, refs, sems):
    copies = [pltpu.make_async_copy(src, dst, sems.at[at]) for at, (src, dst) in enumerate(zip(hbm_refs, refs))]
    for copy in copies:
        copy.start()
    return copies


def looped(start, stop, step, unroll=1):
    def run(x, carried):
        step(x)
        return carried

    lax.fori_loop(start, stop, run, 0, unroll=unroll)


def first_kernel(
    pop_hbm, flags_hbm, nbr_hbm, rate_hbm, still, msg_even, msg_odd, raw, flags, maps_out, tau_out, sides,
    nbr, rate, small_sems, layers, sems,
):
    slots = nbr.shape[0]
    place = Place(slots)
    small = small_copies((nbr_hbm, rate_hbm, flags_hbm), (nbr, rate, flags), small_sems)

    def arrival(at):
        part = pl.ds(at * ARRIVING, ARRIVING)
        return pltpu.make_async_copy(pop_hbm.at[:, part], raw.at[:, part], sems.at[at])

    for at in range(EDGE // ARRIVING):
        arrival(at).start()
    for copy in small:
        copy.wait()
    maps = plane_maps(place, nbr)
    tau = tau_plane(place, rate)
    tau_out[...] = tau
    for at, key in enumerate(MAP_KEYS):
        maps_out[at] = maps[key]
    depth = place.depth

    def collide(x):
        h = collided_from(moments([raw[num, x] for num in range(19)]), tau)
        kept = store_still(still, x, h, flags[x] > 0)
        at_z = {z: depth == ((x + z) & (EDGE - 1)) for z in (0, 1, EDGE - 2, EDGE - 1)}
        for num in range(19):
            value = turned(kept[num], x)
            for z in layers_of(num):
                pltpu.store(layers.at[LAYERS.index((num, z))], value, mask=at_z[z])

    def collide_arrived(at):
        for part in range(TRIP):
            if part % ARRIVING == 0:
                arrival(at * (TRIP // ARRIVING) + part // ARRIVING).wait()
            collide(at * TRIP + part)

    looped(0, EDGE // TRIP, collide_arrived)
    messages = []
    for side, sign in ((0, 1), (1, -1)):
        inward, outward = (DOWNWARD, UPWARD) if sign > 0 else (UPWARD, DOWNWARD)
        face, within = (EDGE - 1, EDGE - 2) if sign > 0 else (0, 1)
        h = [turned(layers[LAYERS.index((num, face))], -face) for num in range(19)]
        g = [None] * 19
        g[0] = h[0]
        for num in range(1, 19):
            if num in inward:
                g[num] = jnp.zeros((SUB, LANES), jnp.float32)
                continue
            source = turned(layers[LAYERS.index((num, within))], -within) if num in outward else h[num]
            g[num] = opened(face_shift(place, maps, source, C[num]), h[OPP[num]])
        mom = moments(g)
        out = [h[num] for num in outward]
        for at, value in enumerate(mom + out):
            sides[side, at] = value
        messages.append([mom[at] for at in SENT] + [mom[7] + mom[8]] + out + [tau])
    odd = lax.axis_index("dev") % 2 == 1
    for at, (upper, lower) in enumerate(zip(*messages)):
        msg_even[at] = jnp.where(odd, lower, upper)
        msg_odd[at] = jnp.where(odd, upper, lower)


def interior_kernel(
    nbr_hbm, tau_in, sides, first_still, raw, flags, maps_in, res, packs, face_maps, pulls,
    still, moved, first_moved, layers, nbr, small_sems,
):
    slots = nbr.shape[0]
    place = Place(slots)
    small = small_copies((nbr_hbm,), (nbr,), small_sems)
    maps = {key: maps_in[at] for at, key in enumerate(MAP_KEYS)}
    depth = place.depth
    tau = tau_in[...]
    keep = {1: depth != 0, -1: depth != EDGE - 1}

    def collide(x):
        g = [first_still[0, x]]
        for num in range(1, 19):
            value = opened(first_moved[num, x + 1 - C[num][0]], first_still[OPP[num], x])
            if C[num][2]:
                value = jnp.where(keep[C[num][2]], value, 0.0)
            g.append(value)
        h = collided_from(moments(g), tau)
        store_moved(place, maps, moved, x, store_still(still, x, h, flags[x] > 0))

    def move(x):
        store_moved(place, maps, first_moved, x, [first_still[num, x] for num in range(19)])

    end = {1: depth == EDGE - 1, -1: depth == 0}

    def stream(x):
        fluid = flags[x] > 0
        near = {
            1: (depth == ((x + EDGE - 1) & (EDGE - 1))) | (depth == ((x + 1) & (EDGE - 1))),
            -1: (depth == x) | (depth == ((x + EDGE - 2) & (EDGE - 1))),
        }
        for num in range(19):
            value = back = still[OPP[num], x]
            if num:
                cx, _, cz = C[num]
                value = moved[num, x + 1 - cx]
                if cz:
                    value = jnp.where((value < LIMIT) | end[cz], value, back)
                    at = (UPWARD if cz > 0 else DOWNWARD).index(num)
                    part = x % 4
                    pltpu.store(layers.at[(1 - cz) // 2, at, part], turned(value, x), mask=near[cz])
                else:
                    value = opened(value, back)
            res[num, x] = jnp.where(fluid, value, raw[num, x])

    looped(0, EDGE, move, INNER)
    store_rims(place, maps, first_still, first_moved)
    looped(0, EDGE, collide, INNER)
    store_rims(place, maps, still, moved)
    for x in range(EDGE):
        stream(x)
    small[0].wait()
    for side, sign in ((0, 1), (1, -1)):
        base = (sign + 1) * slots
        upright = column_of(nbr, (0, 0, sign), slots)
        straight, back = place.named(upright, base), place.naming(upright, base)
        face_maps[side, 0] = place.straight(straight)
        for at, (cx, cy) in enumerate(FLAT):
            if at:
                corner = place.named(column_of(nbr, (-cx, -cy, sign), slots), base)
                far = place.naming(column_of(nbr, (cx, cy, sign), slots), base)
                face_maps[side, at] = place.straight(corner) if cx else place.across(straight, corner, cy)
                own_far = place.straight(far) if cx else place.across(back, far, cy)
            pulls[side, at] = face_pull(place, sides[side, N_MOM + at], (cx, cy), place.straight(back), own_far if at else None)
    phase = depth % 4
    for way, picks in ((0, ((0, 0, EDGE - 1), (1, 5, 1))), (1, ((1, 0, 0), (0, 5, EDGE - 2)))):
        for at in range(5):
            for side, first, z in picks:
                value = layers[way, at, (0 - z) % 4]
                for step in range(1, 4):
                    value = jnp.where(phase == step, layers[way, at, (step - z) % 4], value)
                packs[side, first + at] = turned(value, -z)


def last_kernel(
    tau_in, sides, got_even, got_odd, flags, maps_in, res, packs, face_maps, pulls, out_hbm,
    raw, layers, out_sems,
):
    place = Place(SUB // 2)
    maps = {key: maps_in[at] for at, key in enumerate(MAP_KEYS)}
    depth = place.depth
    odd = lax.axis_index("dev") % 2 == 1
    tau = tau_in[...]

    def upper_got(at):
        return jnp.where(odd, got_odd[at], got_even[at])

    def lower_got(at):
        return jnp.where(odd, got_even[at], got_odd[at])

    edges, nexts = {}, {}
    for side, sign in ((0, 1), (1, -1)):
        got_msg = upper_got if sign > 0 else lower_got
        inward, outward = (DOWNWARD, UPWARD) if sign > 0 else (UPWARD, DOWNWARD)
        own_out = [sides[side, N_MOM + at] for at in range(5)]
        got_in = [got_msg(len(SENT) + 1 + at) for at in range(5)]
        entering, leaving = [], []
        for at, flat in enumerate(FLAT):
            mirror = FLAT.index((-flat[0], -flat[1]))
            value = face_pull(place, got_in[at], flat, face_maps[side, 0], face_maps[side, at])
            entering.append(opened(value, own_out[mirror]))
            leaving.append(opened(pulls[side, at], got_in[mirror]))
        zero = jnp.zeros((SUB, LANES), jnp.float32)
        got_mom = [zero] * N_MOM
        for at, which in enumerate(SENT + (7,)):
            got_mom[which] = got_msg(at)
        far = collided_from(add_crossing(got_mom, leaving, float(sign)), got_msg(N_MSG - 1), inward)
        mom = add_crossing([sides[side, at] for at in range(N_MOM)], entering, float(-sign))
        fluid = own_out[0] < LIMIT
        h = collided_from(mom, tau)
        h = [jnp.where(fluid, h[num], CLOSED) for num in range(19)]
        edges[side, 0] = h[0]
        for num in range(1, 19):
            if not C[num][2]:
                edges[side, num] = opened(face_shift(place, maps, h[num], C[num]), h[OPP[num]])
        for at, flat in enumerate(FLAT):
            value = jnp.where(got_in[0] < LIMIT, far[inward[at]], CLOSED)
            value = face_pull(place, value, flat, face_maps[side, 0], face_maps[side, at])
            edges[side, inward[at]] = opened(value, h[OPP[inward[at]]])
            edges[side, outward[at]] = opened(packs[side, at], h[OPP[outward[at]]])
            value = face_shift(place, maps, h[inward[at]], C[inward[at]])
            nexts[inward[at]] = opened(value, packs[side, 5 + at])

    phase = depth % 4
    for num in range(19):
        bottom = edges[1, num]
        top = turned(edges[0, num], EDGE - 1)
        extra = None
        if C[num][2] > 0:
            extra, offset = turned(nexts[num], 1), 1
        elif C[num][2] < 0:
            extra, offset = turned(nexts[num], EDGE - 2), 2
        for r in range(4):
            value = jnp.where(phase == r, bottom, top)
            if extra is not None:
                value = jnp.where(phase == (r + offset) % 4, extra, value)
            layers[num, r] = value

    ends = (depth == 0) | (depth == EDGE - 1)
    lanes = {0: ends, 1: ends | (depth == 1), -1: ends | (depth == EDGE - 2)}

    def departure(at):
        part = pl.ds(at * LEAVING, LEAVING)
        return pltpu.make_async_copy(raw.at[:, part], out_hbm.at[:, part], out_sems.at[at])

    for at in range(EDGE // LEAVING):
        for x in range(at * LEAVING, (at + 1) * LEAVING):
            fluid = flags[x] > 0
            for num in range(19):
                value = turned(layers[num, x % 4], -x)
                raw[num, x] = jnp.where(fluid & lanes[C[num][2]], value, res[num, x])
        departure(at).start()
    looped(0, EDGE // LEAVING, lambda at: departure(at).wait())


def body(populations, fluid_flags, neighbours, relax_rate):
    slots, velocities, cells = populations.shape
    assert cells == EDGE**3 and 2 * slots == SUB and velocities == 19
    peers = lax.axis_size("dev")
    assert peers % 2 == 0
    tiles = cells // LANES
    view = (EDGE, SUB, LANES)
    pops = populations.transpose(1, 0, 2).reshape(19, slots, tiles, LANES).transpose(0, 2, 1, 3).reshape((19,) + view)
    flags = fluid_flags.reshape(slots, tiles, LANES).transpose(1, 0, 2).reshape(view)
    pops, flags, neighbours, relax_rate = [
        pltpu.with_memory_space_constraint(arg, pltpu.HBM) for arg in (pops, flags, neighbours, relax_rate)
    ]
    vmem = pl.BlockSpec(memory_space=pltpu.VMEM)
    hbm = pl.BlockSpec(memory_space=pltpu.HBM)
    face = (SUB, LANES)
    still = pltpu.VMEM((19,) + view, jnp.float32)
    moved = pltpu.VMEM((19, EDGE + 2) + face, jnp.float32)
    nbr = pltpu.SMEM(neighbours.shape, jnp.int32)
    rate = pltpu.SMEM(relax_rate.shape, jnp.float32)
    dma = pltpu.SemaphoreType.DMA
    params = pltpu.CompilerParams(vmem_limit_bytes=16 * 2**20)
    message = pltpu.VMEM((N_MSG,) + face, jnp.float32)
    plane = pltpu.VMEM(face, jnp.float32)
    first_still, msg_even, msg_odd, raw, flags_here, maps, tau, sides = pl.pallas_call(
        first_kernel,
        out_shape=(
            still, message, message, still, pltpu.VMEM(view, jnp.int32),
            pltpu.VMEM((len(MAP_KEYS),) + face, jnp.int32), plane, pltpu.VMEM((2, N_MOM + 5) + face, jnp.float32),
        ),
        in_specs=[hbm] * 4,
        out_specs=(vmem,) * 8,
        scratch_shapes=[
            nbr, rate, dma((3,)), pltpu.VMEM((len(LAYERS),) + face, jnp.float32), dma((EDGE // ARRIVING,)),
        ],
        compiler_params=params,
        name="collide_first",
    )(pops, flags, neighbours, relax_rate)
    even_pairs = [(i, i ^ 1) for i in range(peers)]
    groups = lax.axis_size("group")
    odd_pairs = []
    for i in range(groups * peers):
        group, dev = divmod(i, peers)
        to = dev + 1 if dev % 2 else dev - 1
        if 0 <= to < peers:
            odd_pairs.append((i, group * peers + to))
        elif groups % 2 == 0:
            odd_pairs.append((i, (group ^ 1) * peers + dev))
        else:
            odd_pairs.append((i, group * peers + to % peers))
    got_odd = lax.ppermute(msg_odd, ("group", "dev"), odd_pairs)
    got_even = lax.ppermute(msg_even, "dev", even_pairs)
    res, packs, face_maps, pulls = pl.pallas_call(
        interior_kernel,
        out_shape=(
            pltpu.VMEM((19,) + view, jnp.float32),
            pltpu.VMEM((2, 10) + face, jnp.float32),
            pltpu.VMEM((2, 5) + face, jnp.int32),
            pltpu.VMEM((2, 5) + face, jnp.float32),
        ),
        in_specs=[hbm] + [vmem] * 6,
        out_specs=(vmem,) * 4,
        scratch_shapes=[still, moved, moved, pltpu.VMEM((2, 5, 4) + face, jnp.float32), nbr, dma((1,))],
        compiler_params=params,
        cost_estimate=pl.CostEstimate(flops=12_000_000, bytes_accessed=4_000_000, transcendentals=0),
        name="interior",
    )(neighbours, tau, sides, first_still, raw, flags_here, maps)
    out = pl.pallas_call(
        last_kernel,
        out_shape=jax.ShapeDtypeStruct(pops.shape, jnp.float32),
        in_specs=[vmem] * 10,
        out_specs=hbm,
        scratch_shapes=[
            pltpu.VMEM((19,) + view, jnp.float32), pltpu.VMEM((19, 4) + face, jnp.float32),
            dma((EDGE // LEAVING,)),
        ],
        compiler_params=params,
        name="finish",
    )(tau, sides, got_even, got_odd, flags_here, maps, res, packs, face_maps, pulls)
    out = out.reshape(19, tiles, slots, LANES).transpose(0, 2, 1, 3).reshape(19, slots, cells)
    return out.transpose(1, 0, 2)


def solution(mesh):
    placed = (
        P(("group", "dev"), None, None),
        P(("group", "dev"), None),
        P(("group", "dev"), None),
        P(("group", "dev")),
    )
    return jax.shard_map(
        body, mesh=mesh, in_specs=placed, out_specs=P(("group", "dev"), None, None), check_vma=False
    )
```

```python
import jax
import jax.numpy as jnp
from jax import lax
from jax.experimental import pallas as pl
from jax.experimental.pallas import tpu as pltpu
from jax.sharding import PartitionSpec as P

EDGE = 16
LANES = 128
SUB = 8
CLOSED = 1.0e30
LIMIT = 1.0e29
ARRIVING = 8
TRIP = 8
LEAVING = ((0, 8), (8, 13), (13, 16))
INNER = 8


def directions():
    listed = [(0, 0, 0)]
    for axis in range(3):
        for sign in (1, -1):
            vector = [0, 0, 0]
            vector[axis] = sign
            listed.append(tuple(vector))
    for one, two in ((0, 1), (0, 2), (1, 2)):
        for sign_one in (1, -1):
            for sign_two in (1, -1):
                vector = [0, 0, 0]
                vector[one] = sign_one
                vector[two] = sign_two
                listed.append(tuple(vector))
    return listed


C = directions()
INDEX = {vector: num for num, vector in enumerate(C)}
OPP = [INDEX[tuple(-part for part in vector)] for vector in C]
FLAT = ((0, 0), (1, 0), (-1, 0), (0, 1), (0, -1))
UPWARD = [INDEX[(a, b, 1)] for a, b in FLAT]
DOWNWARD = [INDEX[(a, b, -1)] for a, b in FLAT]
MAP_KEYS = [(cx, cy) for cx in (0, 1, -1) for cy in (0, 1, -1) if cx or cy]
N_MOM = 9
SENT = (0, 1, 2, 3, 5, 6)
N_MSG = len(SENT) + 1 + 5 + 1


def column(vector):
    return INDEX[vector] - 1


def moments(g):
    sx, dx = g[1] + g[2], g[1] - g[2]
    sy, dy = g[3] + g[4], g[3] - g[4]
    sz, dz = g[5] + g[6], g[5] - g[6]
    pairs = []
    for base in (7, 11, 15):
        pairs.append((g[base] + g[base + 3], g[base] - g[base + 3], g[base + 1] + g[base + 2], g[base + 1] - g[base + 2]))
    (xys, xyd, xyt, xye), (xzs, xzd, xzt, xze), (yzs, yzd, yzt, yze) = pairs
    exy, exz, eyz = xys + xyt, xzs + xzt, yzs + yzt
    rho = g[0] * (1.0 / 3.0) + (sx + sy + sz) * (1.0 / 18.0) + (exy + exz + eyz) * (1.0 / 36.0)
    ux = dx * (1.0 / 6.0) + (xyd + xye + xzd + xze) * (1.0 / 12.0)
    uy = dy * (1.0 / 6.0) + (xyd - xye + yzd + yze) * (1.0 / 12.0)
    uz = dz * (1.0 / 6.0) + (xzd - xze + yzd - yze) * (1.0 / 12.0)
    qxy = (xys - xyt) * 0.25
    qxz = (xzs - xzt) * 0.25
    qyz = (yzs - yzt) * 0.25
    gxz = (sx - sz) * 0.5 + (exy - eyz) * 0.25
    gyz = (sy - sz) * 0.5 + (exy - exz) * 0.25
    return [rho, ux, uy, uz, qxy, qxz, qyz, gxz, gyz]


def add_crossing(mom, e, sign):
    ez, xp, xm, yp, ym = e
    rho, ux, uy, uz, qxy, qxz, qyz, gxz, gyz = mom
    xs, xd, ys, yd = xp + xm, xp - xm, yp + ym, yp - ym
    four = xs + ys
    half = ez * 0.5
    return [
        rho + ez * (1.0 / 18.0) + four * (1.0 / 36.0),
        ux + xd * (1.0 / 12.0),
        uy + yd * (1.0 / 12.0),
        uz + sign * (ez * (1.0 / 6.0) + four * (1.0 / 12.0)),
        qxy,
        qxz + (sign * 0.25) * xd,
        qyz + (sign * 0.25) * yd,
        gxz - ys * 0.25 - half,
        gyz - xs * 0.25 - half,
    ]


def collided_from(mom, tau, wanted=range(19)):
    rho, ux, uy, uz, qxy, qxz, qyz, gxz, gyz = mom
    xx, yy, zz = ux * ux, uy * uy, uz * uz
    base = rho - (xx + yy + zz) * (1.0 / 6.0)
    hx = gxz - (xx - zz)
    hy = gyz - (yy - zz)
    third = tau * (1.0 / 3.0)
    shear = {
        (0,): third * (hx + hx - hy),
        (1,): third * (hy + hy - hx),
        (2,): -third * (hx + hy),
        (0, 1): tau * (qxy - ux * uy),
        (0, 2): tau * (qxz - ux * uz),
        (1, 2): tau * (qyz - uy * uz),
    }
    u = (ux, uy, uz)
    out = {0: base}
    for num in wanted:
        if num in out:
            continue
        vector = C[num]
        axes = tuple(axis for axis in range(3) if vector[axis])
        if len(axes) == 1:
            speed = u[axes[0]]
            lead = vector[axes[0]]
            even = base + speed * speed * 0.5 + shear[axes]
        else:
            first, second = vector[axes[0]], vector[axes[1]]
            speed = u[axes[0]] + u[axes[1]] if first == second else u[axes[0]] - u[axes[1]]
            lead = first
            even = base + speed * speed * 0.5
            even = even + shear[axes] if first == second else even - shear[axes]
        plus = num if lead > 0 else OPP[num]
        out[plus] = even + speed
        out[OPP[plus]] = even - speed
    return out


def turned(value, shift):
    if isinstance(shift, int):
        shift = shift % LANES
        return value if shift == 0 else pltpu.roll(value, shift, 1)
    return pltpu.roll(value, (shift + LANES) % LANES, 1)


def picked(value, source):
    moved = jnp.take_along_axis(value, jnp.maximum(source, 0), axis=0)
    return jnp.where(source >= 0, moved, CLOSED)


def opened(value, back):
    return jnp.where(value < LIMIT, value, back)


class Place:
    def __init__(self, slots):
        self.slots = slots
        self.lane = lax.broadcasted_iota(jnp.int32, (SUB, LANES), 1)
        sub = lax.broadcasted_iota(jnp.int32, (SUB, LANES), 0)
        self.slot = sub % slots
        self.high = sub // slots
        self.depth = self.lane % EDGE

    def carry(self, cy):
        return self.lane >= LANES - EDGE if cy > 0 else self.lane < EDGE

    def named(self, entries, base):
        found = jnp.full((SUB, LANES), -1, jnp.int32)
        for slot, entry in enumerate(entries):
            found = jnp.where(self.slot == slot, jnp.where(entry >= 0, entry - base, -1), found)
        return found

    def naming(self, entries, base):
        found = jnp.full((SUB, LANES), -1, jnp.int32)
        for slot, entry in enumerate(entries):
            found = jnp.where(self.slot == entry - base, slot, found)
        return found

    def straight(self, found):
        return jnp.where(found >= 0, self.high * self.slots + found, -1)

    def across(self, same, corner, cy):
        inner = self.high == (1 if cy > 0 else 0)
        found = jnp.where(inner, same, corner)
        return jnp.where(found >= 0, (1 - self.high) * self.slots + found, -1)


def column_of(nbr, vector, slots):
    return [nbr[slot, column(vector)] for slot in range(slots)]


def plane_maps(place, nbr):
    slots = place.slots
    maps = {}
    for cx in (1, -1):
        side = place.named(column_of(nbr, (-cx, 0, 0), slots), slots)
        maps[cx, 0] = place.straight(side)
        for cy in (1, -1):
            corner = place.named(column_of(nbr, (-cx, -cy, 0), slots), slots)
            maps[cx, cy] = place.across(side, corner, cy)
    for cy in (1, -1):
        beside = place.named(column_of(nbr, (0, -cy, 0), slots), slots)
        maps[0, cy] = place.across(place.slot, beside, cy)
    return maps


def store_moved(place, maps, moved, x, kept):
    for num in range(1, 19):
        _, cy, cz = C[num]
        value = kept[num]
        if cy:
            value = jnp.where(place.carry(cy), picked(value, maps[0, cy]), value)
        moved[num, x + 1] = turned(value, EDGE * cy + cz)


def store_still(still, x, h, fluid):
    kept = [jnp.where(fluid, h[num], CLOSED) for num in range(19)]
    for num in range(19):
        still[num, x] = kept[num]
    return kept


def store_rims(place, maps, still, moved):
    for num in range(1, 19):
        cx, cy, cz = C[num]
        if cx:
            source = still[num, EDGE - 1 if cx > 0 else 0]
            value = picked(source, maps[cx, 0])
            if cy:
                value = jnp.where(place.carry(cy), picked(source, maps[cx, cy]), value)
            moved[num, 0 if cx > 0 else EDGE + 1] = turned(value, EDGE * cy + cz)


def face_pull(place, plane, flat, straight, corner):
    cx, cy = flat
    value = picked(plane, straight)
    if cx:
        end = picked(plane, corner)
        return jnp.where(place.depth == (0 if cx > 0 else EDGE - 1), turned(end, cx - EDGE * cx), turned(value, cx))
    if cy:
        value = jnp.where(place.carry(cy), picked(plane, corner), value)
        return turned(value, EDGE * cy)
    return value


def face_shift(place, maps, plane, vector):
    cx, cy, _ = vector
    value = plane
    if cy:
        value = jnp.where(place.carry(cy), picked(plane, maps[0, cy]), plane)
    value = turned(value, cx + EDGE * cy)
    if cx:
        end = picked(plane, maps[cx, 0])
        if cy:
            end = jnp.where(place.carry(cy), picked(plane, maps[cx, cy]), end)
        end = turned(end, cx - EDGE * cx + EDGE * cy)
        value = jnp.where(place.depth == (0 if cx > 0 else EDGE - 1), end, value)
    return value


def layers_of(num):
    cz = C[num][2]
    return (0, EDGE - 1) + ((EDGE - 2,) if cz > 0 else (1,) if cz < 0 else ())


LAYERS = [(num, z) for num in range(19) for z in layers_of(num)]


def tau_plane(place, rate):
    tau = jnp.zeros((SUB, LANES), jnp.float32)
    for slot in range(place.slots):
        tau = jnp.where(place.slot == slot, 1.0 - rate[slot], tau)
    return tau


def small_copies(hbm_refs, refs, sems):
    copies = [pltpu.make_async_copy(src, dst, sems.at[at]) for at, (src, dst) in enumerate(zip(hbm_refs, refs))]
    for copy in copies:
        copy.start()
    return copies


def looped(start, stop, step, unroll=1):
    def run(x, carried):
        step(x)
        return carried

    lax.fori_loop(start, stop, run, 0, unroll=unroll)


def first_kernel(
    pop_hbm, flags_hbm, nbr_hbm, rate_hbm, still, msg_even, msg_odd, raw, flags, maps_out, tau_out, sides,
    nbr, rate, small_sems, layers, sems,
):
    slots = nbr.shape[0]
    place = Place(slots)
    small = small_copies((nbr_hbm, rate_hbm, flags_hbm), (nbr, rate, flags), small_sems)

    def arrival(at):
        part = pl.ds(at * ARRIVING, ARRIVING)
        return pltpu.make_async_copy(pop_hbm.at[:, part], raw.at[:, part], sems.at[at])

    for at in range(EDGE // ARRIVING):
        arrival(at).start()
    for copy in small:
        copy.wait()
    maps = plane_maps(place, nbr)
    tau = tau_plane(place, rate)
    tau_out[...] = tau
    for at, key in enumerate(MAP_KEYS):
        maps_out[at] = maps[key]
    depth = place.depth

    def collide(x):
        h = collided_from(moments([raw[num, x] for num in range(19)]), tau)
        kept = store_still(still, x, h, flags[x] > 0)
        at_z = {z: depth == ((x + z) & (EDGE - 1)) for z in (0, 1, EDGE - 2, EDGE - 1)}
        for num in range(19):
            value = turned(kept[num], x)
            for z in layers_of(num):
                pltpu.store(layers.at[LAYERS.index((num, z))], value, mask=at_z[z])

    def collide_arrived(at):
        for part in range(TRIP):
            if part % ARRIVING == 0:
                arrival(at * (TRIP // ARRIVING) + part // ARRIVING).wait()
            collide(at * TRIP + part)

    looped(0, EDGE // TRIP, collide_arrived)
    messages = []
    for side, sign in ((0, 1), (1, -1)):
        inward, outward = (DOWNWARD, UPWARD) if sign > 0 else (UPWARD, DOWNWARD)
        face, within = (EDGE - 1, EDGE - 2) if sign > 0 else (0, 1)
        h = [turned(layers[LAYERS.index((num, face))], -face) for num in range(19)]
        g = [None] * 19
        g[0] = h[0]
        for num in range(1, 19):
            if num in inward:
                g[num] = jnp.zeros((SUB, LANES), jnp.float32)
                continue
            source = turned(layers[LAYERS.index((num, within))], -within) if num in outward else h[num]
            g[num] = opened(face_shift(place, maps, source, C[num]), h[OPP[num]])
        mom = moments(g)
        out = [h[num] for num in outward]
        for at, value in enumerate(mom + out):
            sides[side, at] = value
        messages.append([mom[at] for at in SENT] + [mom[7] + mom[8]] + out + [tau])
    odd = lax.axis_index("dev") % 2 == 1
    for at, (upper, lower) in enumerate(zip(*messages)):
        msg_even[at] = jnp.where(odd, lower, upper)
        msg_odd[at] = jnp.where(odd, upper, lower)


def interior_kernel(
    nbr_hbm, tau_in, sides, first_still, raw, flags, maps_in, res, packs, face_maps, pulls,
    still, moved, first_moved, layers, nbr, small_sems,
):
    slots = nbr.shape[0]
    place = Place(slots)
    small = small_copies((nbr_hbm,), (nbr,), small_sems)
    maps = {key: maps_in[at] for at, key in enumerate(MAP_KEYS)}
    depth = place.depth
    tau = tau_in[...]
    keep = {1: depth != 0, -1: depth != EDGE - 1}

    def collide(x):
        g = [first_still[0, x]]
        for num in range(1, 19):
            value = opened(first_moved[num, x + 1 - C[num][0]], first_still[OPP[num], x])
            if C[num][2]:
                value = jnp.where(keep[C[num][2]], value, 0.0)
            g.append(value)
        h = collided_from(moments(g), tau)
        store_moved(place, maps, moved, x, store_still(still, x, h, flags[x] > 0))

    def move(x):
        store_moved(place, maps, first_moved, x, [first_still[num, x] for num in range(19)])

    end = {1: depth == EDGE - 1, -1: depth == 0}

    def stream(x):
        fluid = flags[x] > 0
        near = {
            1: (depth == ((x + EDGE - 1) & (EDGE - 1))) | (depth == ((x + 1) & (EDGE - 1))),
            -1: (depth == x) | (depth == ((x + EDGE - 2) & (EDGE - 1))),
        }
        for num in range(19):
            value = back = still[OPP[num], x]
            if num:
                cx, _, cz = C[num]
                value = moved[num, x + 1 - cx]
                if cz:
                    value = jnp.where((value < LIMIT) | end[cz], value, back)
                    at = (UPWARD if cz > 0 else DOWNWARD).index(num)
                    part = x % 4
                    pltpu.store(layers.at[(1 - cz) // 2, at, part], turned(value, x), mask=near[cz])
                else:
                    value = opened(value, back)
            res[num, x] = jnp.where(fluid, value, raw[num, x])

    looped(0, EDGE, move, INNER)
    store_rims(place, maps, first_still, first_moved)
    looped(0, EDGE, collide, INNER)
    store_rims(place, maps, still, moved)
    for x in range(EDGE):
        stream(x)
    small[0].wait()
    for side, sign in ((0, 1), (1, -1)):
        base = (sign + 1) * slots
        upright = column_of(nbr, (0, 0, sign), slots)
        straight, back = place.named(upright, base), place.naming(upright, base)
        face_maps[side, 0] = place.straight(straight)
        for at, (cx, cy) in enumerate(FLAT):
            if at:
                corner = place.named(column_of(nbr, (-cx, -cy, sign), slots), base)
                far = place.naming(column_of(nbr, (cx, cy, sign), slots), base)
                face_maps[side, at] = place.straight(corner) if cx else place.across(straight, corner, cy)
                own_far = place.straight(far) if cx else place.across(back, far, cy)
            pulls[side, at] = face_pull(place, sides[side, N_MOM + at], (cx, cy), place.straight(back), own_far if at else None)
    phase = depth % 4
    for way, picks in ((0, ((0, 0, EDGE - 1), (1, 5, 1))), (1, ((1, 0, 0), (0, 5, EDGE - 2)))):
        for at in range(5):
            for side, first, z in picks:
                value = layers[way, at, (0 - z) % 4]
                for step in range(1, 4):
                    value = jnp.where(phase == step, layers[way, at, (step - z) % 4], value)
                packs[side, first + at] = turned(value, -z)


def last_kernel(
    tau_in, sides, got_even, got_odd, flags, maps_in, res, packs, face_maps, pulls, out_hbm,
    raw, layers, out_sems,
):
    place = Place(SUB // 2)
    maps = {key: maps_in[at] for at, key in enumerate(MAP_KEYS)}
    depth = place.depth
    odd = lax.axis_index("dev") % 2 == 1
    tau = tau_in[...]

    def upper_got(at):
        return jnp.where(odd, got_odd[at], got_even[at])

    def lower_got(at):
        return jnp.where(odd, got_even[at], got_odd[at])

    edges, nexts = {}, {}
    for side, sign in ((0, 1), (1, -1)):
        got_msg = upper_got if sign > 0 else lower_got
        inward, outward = (DOWNWARD, UPWARD) if sign > 0 else (UPWARD, DOWNWARD)
        own_out = [sides[side, N_MOM + at] for at in range(5)]
        got_in = [got_msg(len(SENT) + 1 + at) for at in range(5)]
        entering, leaving = [], []
        for at, flat in enumerate(FLAT):
            mirror = FLAT.index((-flat[0], -flat[1]))
            value = face_pull(place, got_in[at], flat, face_maps[side, 0], face_maps[side, at])
            entering.append(opened(value, own_out[mirror]))
            leaving.append(opened(pulls[side, at], got_in[mirror]))
        zero = jnp.zeros((SUB, LANES), jnp.float32)
        got_mom = [zero] * N_MOM
        for at, which in enumerate(SENT + (7,)):
            got_mom[which] = got_msg(at)
        far = collided_from(add_crossing(got_mom, leaving, float(sign)), got_msg(N_MSG - 1), inward)
        mom = add_crossing([sides[side, at] for at in range(N_MOM)], entering, float(-sign))
        fluid = own_out[0] < LIMIT
        h = collided_from(mom, tau)
        h = [jnp.where(fluid, h[num], CLOSED) for num in range(19)]
        edges[side, 0] = h[0]
        for num in range(1, 19):
            if not C[num][2]:
                edges[side, num] = opened(face_shift(place, maps, h[num], C[num]), h[OPP[num]])
        for at, flat in enumerate(FLAT):
            value = jnp.where(got_in[0] < LIMIT, far[inward[at]], CLOSED)
            value = face_pull(place, value, flat, face_maps[side, 0], face_maps[side, at])
            edges[side, inward[at]] = opened(value, h[OPP[inward[at]]])
            edges[side, outward[at]] = opened(packs[side, at], h[OPP[outward[at]]])
            value = face_shift(place, maps, h[inward[at]], C[inward[at]])
            nexts[inward[at]] = opened(value, packs[side, 5 + at])

    phase = depth % 4
    for num in range(19):
        bottom = edges[1, num]
        top = turned(edges[0, num], EDGE - 1)
        extra = None
        if C[num][2] > 0:
            extra, offset = turned(nexts[num], 1), 1
        elif C[num][2] < 0:
            extra, offset = turned(nexts[num], EDGE - 2), 2
        for r in range(4):
            value = jnp.where(phase == r, bottom, top)
            if extra is not None:
                value = jnp.where(phase == (r + offset) % 4, extra, value)
            layers[num, r] = value

    ends = (depth == 0) | (depth == EDGE - 1)
    lanes = {0: ends, 1: ends | (depth == 1), -1: ends | (depth == EDGE - 2)}

    def departure(at):
        part = pl.ds(LEAVING[at][0], LEAVING[at][1] - LEAVING[at][0])
        return pltpu.make_async_copy(raw.at[:, part], out_hbm.at[:, part], out_sems.at[at])

    for at in range(len(LEAVING)):
        for x in range(*LEAVING[at]):
            fluid = flags[x] > 0
            for num in range(19):
                value = turned(layers[num, x % 4], -x)
                raw[num, x] = jnp.where(fluid & lanes[C[num][2]], value, res[num, x])
        departure(at).start()
    for at in range(len(LEAVING)):
        departure(at).wait()


def body(populations, fluid_flags, neighbours, relax_rate):
    slots, velocities, cells = populations.shape
    assert cells == EDGE**3 and 2 * slots == SUB and velocities == 19
    peers = lax.axis_size("dev")
    assert peers % 2 == 0
    tiles = cells // LANES
    view = (EDGE, SUB, LANES)
    pops = populations.transpose(1, 0, 2).reshape(19, slots, tiles, LANES).transpose(0, 2, 1, 3).reshape((19,) + view)
    flags = fluid_flags.reshape(slots, tiles, LANES).transpose(1, 0, 2).reshape(view)
    pops, flags, neighbours, relax_rate = [
        pltpu.with_memory_space_constraint(arg, pltpu.HBM) for arg in (pops, flags, neighbours, relax_rate)
    ]
    vmem = pl.BlockSpec(memory_space=pltpu.VMEM)
    hbm = pl.BlockSpec(memory_space=pltpu.HBM)
    face = (SUB, LANES)
    still = pltpu.VMEM((19,) + view, jnp.float32)
    moved = pltpu.VMEM((19, EDGE + 2) + face, jnp.float32)
    nbr = pltpu.SMEM(neighbours.shape, jnp.int32)
    rate = pltpu.SMEM(relax_rate.shape, jnp.float32)
    dma = pltpu.SemaphoreType.DMA
    params = pltpu.CompilerParams(vmem_limit_bytes=16 * 2**20)
    message = pltpu.VMEM((N_MSG,) + face, jnp.float32)
    plane = pltpu.VMEM(face, jnp.float32)
    first_still, msg_even, msg_odd, raw, flags_here, maps, tau, sides = pl.pallas_call(
        first_kernel,
        out_shape=(
            still, message, message, still, pltpu.VMEM(view, jnp.int32),
            pltpu.VMEM((len(MAP_KEYS),) + face, jnp.int32), plane, pltpu.VMEM((2, N_MOM + 5) + face, jnp.float32),
        ),
        in_specs=[hbm] * 4,
        out_specs=(vmem,) * 8,
        scratch_shapes=[
            nbr, rate, dma((3,)), pltpu.VMEM((len(LAYERS),) + face, jnp.float32), dma((EDGE // ARRIVING,)),
        ],
        compiler_params=params,
        name="collide_first",
    )(pops, flags, neighbours, relax_rate)
    even_pairs = [(i, i ^ 1) for i in range(peers)]
    groups = lax.axis_size("group")
    odd_pairs = []
    for i in range(groups * peers):
        group, dev = divmod(i, peers)
        to = dev + 1 if dev % 2 else dev - 1
        if 0 <= to < peers:
            odd_pairs.append((i, group * peers + to))
        elif groups % 2 == 0:
            odd_pairs.append((i, (group ^ 1) * peers + dev))
        else:
            odd_pairs.append((i, group * peers + to % peers))
    got_odd = lax.ppermute(msg_odd, ("group", "dev"), odd_pairs)
    got_even = lax.ppermute(msg_even, "dev", even_pairs)
    res, packs, face_maps, pulls = pl.pallas_call(
        interior_kernel,
        out_shape=(
            pltpu.VMEM((19,) + view, jnp.float32),
            pltpu.VMEM((2, 10) + face, jnp.float32),
            pltpu.VMEM((2, 5) + face, jnp.int32),
            pltpu.VMEM((2, 5) + face, jnp.float32),
        ),
        in_specs=[hbm] + [vmem] * 6,
        out_specs=(vmem,) * 4,
        scratch_shapes=[still, moved, moved, pltpu.VMEM((2, 5, 4) + face, jnp.float32), nbr, dma((1,))],
        compiler_params=params,
        cost_estimate=pl.CostEstimate(flops=12_000_000, bytes_accessed=4_000_000, transcendentals=0),
        name="interior",
    )(neighbours, tau, sides, first_still, raw, flags_here, maps)
    out = pl.pallas_call(
        last_kernel,
        out_shape=jax.ShapeDtypeStruct(pops.shape, jnp.float32),
        in_specs=[vmem] * 10,
        out_specs=hbm,
        scratch_shapes=[
            pltpu.VMEM((19,) + view, jnp.float32), pltpu.VMEM((19, 4) + face, jnp.float32),
            dma((len(LEAVING),)),
        ],
        compiler_params=params,
        name="finish",
    )(tau, sides, got_even, got_odd, flags_here, maps, res, packs, face_maps, pulls)
    out = out.reshape(19, tiles, slots, LANES).transpose(0, 2, 1, 3).reshape(19, slots, cells)
    return out.transpose(1, 0, 2)


def solution(mesh):
    placed = (
        P(("group", "dev"), None, None),
        P(("group", "dev"), None),
        P(("group", "dev"), None),
        P(("group", "dev")),
    )
    return jax.shard_map(
        body, mesh=mesh, in_specs=placed, out_specs=P(("group", "dev"), None, None), check_vma=False
    )
```
